32 devices in a mesh: xy: 8 (over y, x, core), gz: 4 (over z).
Axes of the slice: x: 2, y: 2, z: 4, core: 2. Of those that a mesh axis runs over, the one named last changes fastest.
Arguments:
- velocity: float32 [3, 16, 256, 1024], P(None, 'gz', 'xy'), may hold values from -6 to 6
- magnetic: float32 [3, 8, 128, 512], P(None, 'gz', 'xy'), may hold values from -6 to 6
- slot_block_table: int32 [256], P('xy'), may hold values from 0 to 255, as said below
Outputs:
- updated_fine_velocity: float32 [3, 16, 256, 1024], P(None, 'gz', 'xy')
- magnetic_next: float32 [3, 8, 128, 512], P(None, 'gz', 'xy')
The draws below stay inside these ranges and needn't reach their ends.
Inputs may be any that keep to these rules, and one draw needn't show every extreme that they name: `slot_block_table`: each block number appears in one slot; the 32 slots of one device along xy hold exactly 4 blocks of every block row.
All inputs are finite; a program needn't handle non-finite values.
Results may differ from the reference program's by a relative error of at most 0.00005.
Values sent between devices are 32-bit elements; how exact they have to be, the bound alone decides.
No kernel may reach another device: no remote copies, remote signals or barrier semaphores. Data moves between devices by JAX's collectives and lax.ppermute only.
A program may use at most 64 MiB of HBM per device.

```python
import jax
import jax.numpy as jnp

BLOCK_EDGE = 32
BCOLS = 32
BROWS = 8
FBLOCKS = 256
NZF = 16
NZC = 8
NYC = 128
NXC = 512


def draw_slot_block_table(key, part):
    share = BCOLS // BROWS
    row_keys = jax.random.split(jax.random.fold_in(key, 11), BROWS)
    perms = jax.vmap(lambda k: jax.random.permutation(k, BCOLS))(row_keys)
    holders = perms.reshape(BROWS, BROWS, share).transpose(1, 0, 2)
    rowbase = (jnp.arange(BROWS, dtype=jnp.int32) * BCOLS).reshape(1, BROWS, 1)
    listed = (holders.astype(jnp.int32) + rowbase).reshape(BROWS, BCOLS)
    slot_keys = jax.random.split(jax.random.fold_in(key, 23), BROWS)
    slots = jax.vmap(lambda k: jax.random.permutation(k, BCOLS))(slot_keys).astype(jnp.int32)
    return jnp.take_along_axis(listed, slots, axis=1).reshape(BROWS * BCOLS).astype(jnp.int32)


def block_scale(rng, dims, cuts, low, top_value):
    gain, own = 1.0, jax.random.fold_in(rng, 6)
    for dim, shards_of in cuts:
        heights = jnp.exp(jax.random.uniform(jax.random.fold_in(own, dim), (shards_of,), jnp.float32, low / len(cuts), top_value / len(cuts)))
        gain = gain * jnp.repeat(heights, dims[dim] // shards_of).reshape([-1 if axis == dim else 1 for axis in range(len(dims))])
    return gain


def scatter_about(rng, shape, scale, reach, cuts=(), held_as=jnp.bfloat16):
    loudness = block_scale(rng, shape, cuts, -0.22, 0.18) if cuts else 1.0
    array = jax.random.normal(rng, shape, jnp.float32) * scale * loudness
    return jnp.minimum(jnp.maximum(array, -reach), reach).astype(held_as)


def setup_inputs(seed: int = 0) -> dict:
    seeds = jax.random.split(jax.random.key(seed), 4)
    return {
        "velocity": scatter_about(seeds[0], (3, NZF, FBLOCKS, BLOCK_EDGE * BLOCK_EDGE), 1.0, 6.0, ((1, 4), (2, 8)), jnp.float32),
        "magnetic": scatter_about(seeds[1], (3, NZC, NYC, NXC), 1.0, 6.0, ((1, 4), (2, 8)), jnp.float32),
        "slot_block_table": draw_slot_block_table(jax.random.fold_in(seeds[3], 71), 0),
    }


def restrict(fine, blk):
    half_width = blk // 2
    s = fine.shape
    v = fine.reshape(s[0], s[1] // 2, 2, s[2], half_width, 2, half_width, 2)
    return (jnp.sum(v, axis=(2, 5, 7)) * 0.125).reshape(s[0], s[1] // 2, s[2], half_width * half_width)


def central(magnetic_state, axis):
    return (jnp.roll(magnetic_state, -1, axis) - jnp.roll(magnetic_state, 1, axis)) * 0.5


def curl(v):
    return jnp.stack([central(v[2], 1) - central(v[1], 0), central(v[0], 0) - central(v[2], 2), central(v[1], 2) - central(v[0], 1)])


def cross(a, b):
    return jnp.stack([a[1] * b[2] - a[2] * b[1], a[2] * b[0] - a[0] * b[2], a[0] * b[1] - a[1] * b[0]])


def laplace(v):
    total = -6.0 * v
    for axis in (1, 2, 3):
        total = total + jnp.roll(v, 1, axis) + jnp.roll(v, -1, axis)
    return total


def reference(velocity, magnetic, slot_block_table):
    half_width = BLOCK_EDGE // 2
    tile_stack = restrict(velocity, BLOCK_EDGE)
    sorted_positions = jnp.argsort(slot_block_table).astype(jnp.int32)
    ordered = tile_stack[:, :, sorted_positions]
    nzc = ordered.shape[1]
    grid = ordered.reshape(3, nzc, BROWS, BCOLS, half_width, half_width).transpose(0, 1, 2, 4, 3, 5).reshape(3, nzc, BROWS * half_width, BCOLS * half_width)
    emf = cross(grid, magnetic)
    current = curl(magnetic)
    magnetic_next = magnetic + 0.1 * (curl(emf) + 0.5 * laplace(magnetic))
    lorentz_force = cross(current, magnetic)
    blocks = lorentz_force.reshape(3, nzc, BROWS, half_width, BCOLS, half_width).transpose(0, 1, 2, 4, 3, 5).reshape(3, nzc, BROWS * BCOLS, half_width, half_width)
    blocks_per_slot = blocks[:, :, slot_block_table]
    n = blocks_per_slot.shape[2]
    widened_tiles = jnp.broadcast_to(blocks_per_slot.reshape(3, nzc, 1, n, half_width, 1, half_width, 1), (3, nzc, 2, n, half_width, 2, half_width, 2))
    updated_fine_velocity = velocity + 0.1 * widened_tiles.reshape(3, nzc * 2, n, BLOCK_EDGE * BLOCK_EDGE)
    return updated_fine_velocity, magnetic_next
```

```python
import functools
import math

import jax
import jax.numpy as jnp
from jax import lax
from jax.experimental import pallas as pl
from jax.experimental.pallas import tpu as pltpu
from jax.sharding import PartitionSpec as P

F32, BF16 = jnp.float32, jnp.bfloat16
VMEM = pl.BlockSpec(memory_space=pltpu.VMEM)


def split(x):
    hi = x.astype(BF16)
    return hi, (x - hi.astype(F32)).astype(BF16)


def dot(a, b):
    return jnp.dot(a, b, preferred_element_type=F32)


def iota(shape, dim):
    return lax.broadcasted_iota(jnp.int32, shape, dim)


def one_hot(mask):
    return jnp.where(mask, 1.0, 0.0).astype(BF16)


def log2(x):
    assert x == 1 << (x.bit_length() - 1)
    return x.bit_length() - 1


class Plan:
    def __init__(self, vshape, bshape, n):
        self.n = n
        self.slots = vshape[2]
        self.k = self.slots // n
        self.zc = bshape[1]
        self.ny, self.nx = bshape[2:]
        self.edge = math.isqrt(vshape[3])
        self.half = self.edge // 2
        self.area = self.half * self.half
        self.bcols = self.nx // self.half
        self.cz = 3 * self.zc
        self.ru = -(-self.cz * self.k // 8) * 8
        self.rows = n * self.ru
        self.rb = self.cz * self.nx // self.area
        self.r1 = -(-(self.ru + self.rb + 1) // 8) * 8
        self.re = 2 * self.zc * self.nx // self.area
        self.r2 = -(-(self.ru + self.re) // 8) * 8
        self.wrap = self.nx // self.area


def send_positions(p, table):
    s = p.slots
    row = jnp.broadcast_to((table >> log2(p.bcols)).astype(F32), (s, s))
    i, j = iota((s, s), 0), iota((s, s), 1)
    row_s = jnp.sum(jnp.where(i == j, row, 0.0), axis=1, keepdims=True)
    rank = jnp.sum(jnp.where((row_s == row) & (i < j), 1.0, 0.0), axis=0, keepdims=True)
    q = row[0:1] * p.k + rank
    q_s = jnp.sum(jnp.where(i == j, jnp.broadcast_to(q, (s, s)), 0.0), axis=1, keepdims=True)
    return q, q_s


def lane_route(p):
    lane = iota((1, p.rows), 1)
    r = jnp.floor((lane.astype(F32) + 0.5) * (1.0 / p.ru)).astype(jnp.int32)
    i = lane - r * p.ru
    return r, i >> log2(p.k), i & (p.k - 1)


def restrict_kernel(p, v_ref, t_ref, b_ref, out_ref, g3_ref, up_ref, down_ref, last, first):
    n, k, s = p.n, p.k, p.slots
    me = lax.axis_index("xy")
    table = t_ref[...]
    q, q_s = send_positions(p, table)
    lanes = p.cz * s
    rep = one_hot((iota((s, lanes), 1) & (s - 1)) == iota((s, lanes), 0))
    qt = dot(jnp.broadcast_to(q, (8, s)).astype(BF16), rep)[0:1]
    shape = (n, p.ru, lanes)
    i = iota(shape, 1)
    target = (iota(shape, 0) * k + (i & (k - 1))).astype(F32)
    g = one_hot(((i >> log2(k)) == (iota(shape, 2) >> log2(s))) & (target == qt.reshape(1, 1, lanes)))
    g = g.reshape(p.rows, lanes)
    r_l, c_l, j_l = lane_route(p)
    shape = (p.cz, s, p.rows)
    g3 = (iota(shape, 0) == c_l.reshape(1, 1, p.rows)) & (
        q_s.reshape(1, s, 1) == (r_l * k + j_l).astype(F32).reshape(1, 1, p.rows)
    )
    g3_ref[...] = one_hot(g3).reshape(p.cz * s, p.rows)
    half_fine = p.edge * p.edge // 2
    half_area = p.area // 2
    f, c = iota((half_fine, half_area), 0), iota((half_fine, half_area), 1)
    e = log2(p.edge)
    coarse = ((f >> (e + 1)) << (e - 1)) + ((f & (p.edge - 1)) >> 1)
    sel = one_hot(coarse == c)
    z_sum = jnp.concatenate(
        [v_ref[c, 2 * z] + v_ref[c, 2 * z + 1] for c in range(3) for z in range(p.zc)], axis=0
    )
    hi, lo = split(z_sum)
    parts = []
    for h in range(2):
        w = slice(h * half_fine, (h + 1) * half_fine)
        parts.append(dot(hi[:, w], sel) + dot(lo[:, w], sel))
    u = jnp.concatenate(parts, axis=1) * 0.125
    hi, lo = split(u)
    out_ref[:, : p.ru, :] = (dot(g, hi) + dot(g, lo)).reshape(n, p.ru, p.area)
    for c in range(3):
        for z in range(p.zc):
            for h in range(p.wrap):
                at = (c * p.zc + z) * p.wrap + h
                w = slice(h * p.area, (h + 1) * p.area)
                last[at : at + 1, :] = b_ref[c, z, p.ny - 1 : p.ny, w]
                first[at : at + 1, :] = b_ref[c, z, 0:1, w]
    nxt = lax.rem(me + 1, n)
    for r in range(n):
        out_ref[r, p.ru : p.ru + p.rb, :] = jnp.where(r == nxt, last[: p.rb], first[: p.rb])
    col = jnp.broadcast_to((table & (p.bcols - 1)).astype(F32), (s, s))
    qi = iota((s, s), 0).astype(F32)
    col_q = jnp.sum(jnp.where(qi == jnp.broadcast_to(q, (s, s)), col, 0.0), axis=1, keepdims=True)
    qa, la = iota((s, p.area), 0), iota((s, p.area), 1)
    spread = jnp.where((qa & (k - 1)) == (la & (k - 1)), col_q, 0.0).astype(BF16)
    gather = one_hot((iota((n, s), 1) >> log2(k)) == iota((n, s), 0))
    cols = dot(gather, spread)
    at = p.ru + p.rb
    for r in range(n):
        out_ref[r, at : at + 1, :] = cols[r : r + 1]
    up_ref[...] = b_ref[:, p.zc - 1]
    down_ref[...] = b_ref[:, 0]


def tile_transpose(p, t):
    ax = t.ndim - 2
    s, g = iota(t.shape, ax), iota(t.shape, ax + 1) >> log2(p.half)
    for b in (1, 2, 4):
        w = b * p.half
        up = pltpu.roll(pltpu.roll(t, 8 - b, ax), w, ax + 1)
        dn = up if b == 4 else pltpu.roll(pltpu.roll(t, b, ax), 128 - w, ax + 1)
        sb, gb = (s & b) != 0, (g & b) != 0
        t = jnp.where(sb == gb, t, jnp.where(gb, up, dn))
    return t


def blocks_to_grid(p, blk):
    rows = []
    for yh in range(p.half // 8):
        rows.append(
            jnp.concatenate(
                [
                    tile_transpose(p, blk[8 * c : 8 * c + 8, 128 * yh : 128 * yh + 128])
                    for c in range(p.bcols // 8)
                ],
                axis=1,
            )
        )
    return jnp.concatenate(rows, axis=0)


def grid_to_blocks(p, grid):
    rows = []
    for c in range(p.bcols // 8):
        rows.append(
            jnp.concatenate(
                [
                    tile_transpose(p, grid[8 * yh : 8 * yh + 8, 128 * c : 128 * c + 128])
                    for yh in range(p.half // 8)
                ],
                axis=1,
            )
        )
    return jnp.concatenate(rows, axis=0)


def x_next(f):
    return pltpu.roll(f, f.shape[1] - 1, 1)


def x_prev(f):
    return pltpu.roll(f, 1, 1)


def y_next(f, halo):
    return jnp.where(iota(f.shape, 0) == f.shape[0] - 1, halo, pltpu.roll(f, f.shape[0] - 1, 0))


def y_prev(f, halo):
    return jnp.where(iota(f.shape, 0) == 0, halo, pltpu.roll(f, 1, 0))


def row_of(p, ref, src, at):
    return jnp.concatenate([ref[src, pl.ds(at + h, 1), :] for h in range(p.wrap)], axis=1)


def field_kernel(p, r_ref, b_ref, lo_ref, hi_ref, out_ref, next_ref, up_ref, down_ref, e_rows):
    n, k, zc = p.n, p.k, p.zc
    me = lax.axis_index("xy")
    nxt, prv = lax.rem(me + 1, n), lax.rem(me + n - 1, n)
    cols = r_ref[:, p.ru + p.rb, :]
    r_l, c_l, _ = lane_route(p)
    shape = (n, p.rows)
    col_l = jnp.sum(jnp.where(iota(shape, 0) == r_l, cols[:, : p.rows], 0.0), axis=0, keepdims=True)
    shape = (p.cz, p.bcols, p.rows)
    g2 = one_hot(
        (iota(shape, 0) == c_l.reshape(1, 1, p.rows))
        & (iota(shape, 1).astype(F32) == col_l.reshape(1, 1, p.rows))
    ).reshape(p.cz * p.bcols, p.rows)
    shape = (n, p.ru, 128)
    col_s = jnp.sum(
        jnp.where((iota(shape, 1) & (k - 1)) == iota(shape, 2), cols[:, None, :128], 0.0), axis=2, keepdims=True
    )
    lanes = p.cz * p.bcols
    shape = (n, p.ru, lanes)
    lane = iota(shape, 2)
    g2t = one_hot(
        ((iota(shape, 1) >> log2(k)) == (lane >> log2(p.bcols)))
        & (col_s == (lane & (p.bcols - 1)).astype(F32))
    ).reshape(p.rows, lanes)
    hi, lo = split(r_ref[:, : p.ru, :].reshape(p.rows, p.area))
    u_blk = dot(g2, hi) + dot(g2, lo)
    u = [
        [blocks_to_grid(p, u_blk[(c * zc + z) * p.bcols : (c * zc + z + 1) * p.bcols]) for z in range(zc)]
        for c in range(3)
    ]
    b = [[b_ref[c, z] for z in range(zc)] for c in range(3)]
    force = []
    for z in range(zc):
        bz = [b[c][z] for c in range(3)]
        below = [lo_ref[c] if z == 0 else b[c][z - 1] for c in range(3)]
        above = [hi_ref[c] if z == zc - 1 else b[c][z + 1] for c in range(3)]
        north, south, east, west = [], [], [], []
        for c in range(3):
            at = p.ru + (c * zc + z) * p.wrap
            south.append(y_prev(bz[c], row_of(p, r_ref, prv, at)))
            north.append(y_next(bz[c], row_of(p, r_ref, nxt, at)))
            east.append(x_next(bz[c]))
            west.append(x_prev(bz[c]))
        dz = [(above[c] - below[c]) * 0.5 for c in range(2)]
        j0 = (north[2] - south[2]) * 0.5 - dz[1]
        j1 = dz[0] - (east[2] - west[2]) * 0.5
        j2 = (east[1] - west[1]) * 0.5 - (north[0] - south[0]) * 0.5
        force.append([j1 * bz[2] - j2 * bz[1], j2 * bz[0] - j0 * bz[2], j0 * bz[1] - j1 * bz[0]])
        for c in range(3):
            lap = above[c] + below[c] + north[c] + south[c] + east[c] + west[c] - 6.0 * bz[c]
            next_ref[c, z] = bz[c] + 0.05 * lap
    f_blk = jnp.concatenate([grid_to_blocks(p, force[z][c]) for c in range(3) for z in range(zc)], axis=0)
    hi, lo = split(f_blk)
    out_ref[:, : p.ru, :] = (dot(g2t, hi) + dot(g2t, lo)).reshape(n, p.ru, p.area)
    e = []
    for z in range(zc):
        uz, bz = [u[c][z] for c in range(3)], [b[c][z] for c in range(3)]
        e.append([uz[1] * bz[2] - uz[2] * bz[1], uz[2] * bz[0] - uz[0] * bz[2], uz[0] * bz[1] - uz[1] * bz[0]])
    for z in range(zc):
        ez = e[z]
        zero = jnp.zeros_like(ez[0])
        above = e[z + 1] if z < zc - 1 else (zero, zero)
        below = e[z - 1] if z > 0 else (zero, zero)
        dy2 = y_next(ez[2], 0.0) - y_prev(ez[2], 0.0)
        dy0 = y_next(ez[0], 0.0) - y_prev(ez[0], 0.0)
        next_ref[0, z] += 0.05 * (dy2 - (above[1] - below[1]))
        next_ref[1, z] += 0.05 * ((above[0] - below[0]) - (x_next(ez[2]) - x_prev(ez[2])))
        next_ref[2, z] += 0.05 * ((x_next(ez[1]) - x_prev(ez[1])) - dy0)
        for i, c in enumerate((0, 2)):
            for h in range(p.wrap):
                at = (i * zc + z) * p.wrap + h
                w = slice(h * p.area, (h + 1) * p.area)
                e_rows[0, at : at + 1, :] = ez[c][0:1, w]
                e_rows[1, at : at + 1, :] = ez[c][p.ny - 1 : p.ny, w]
    for r in range(n):
        out_ref[r, p.ru : p.ru + p.re, :] = jnp.where(r == nxt, e_rows[1], e_rows[0])
    up_ref[0], up_ref[1] = e[zc - 1][0], e[zc - 1][1]
    down_ref[0], down_ref[1] = e[0][0], e[0][1]


def widen_kernel(p, r_ref, g_ref, v_ref, out_ref):
    half_fine = p.edge * p.edge // 2
    half_area = p.area // 2
    e = log2(p.edge)
    c, f = iota((half_area, half_fine), 0), iota((half_area, half_fine), 1)
    coarse = ((f >> (e + 1)) << (e - 1)) + ((f & (p.edge - 1)) >> 1)
    sel = one_hot(coarse == c)
    hi, lo = split(r_ref[:, : p.ru, :].reshape(p.rows, p.area) * 0.1)
    g = g_ref[...]
    hi, lo = dot(g, hi).astype(BF16), dot(g, lo).astype(BF16)
    s = p.slots
    for h in range(2):
        w = slice(h * half_area, (h + 1) * half_area)
        wide = dot(hi[:, w], sel) + dot(lo[:, w], sel)
        fw = slice(h * half_fine, (h + 1) * half_fine)
        for c in range(3):
            for z in range(p.zc):
                add = wide[(c * p.zc + z) * s : (c * p.zc + z + 1) * s]
                for d in range(2):
                    out_ref[c, 2 * z + d, :, fw] = v_ref[c, 2 * z + d, :, fw] + add


def finish_kernel(p, n_ref, r_ref, lo_ref, hi_ref, out_ref):
    n, zc = p.n, p.zc
    me = lax.axis_index("xy")
    nxt, prv = lax.rem(me + 1, n), lax.rem(me + n - 1, n)
    y = iota((p.ny, p.nx), 0)

    def dy(i, z):
        at = p.ru + (i * zc + z) * p.wrap
        north, south = row_of(p, r_ref, nxt, at), row_of(p, r_ref, prv, at)
        return jnp.where(y == p.ny - 1, north, 0.0) - jnp.where(y == 0, south, 0.0)

    for z in range(zc):
        zero = jnp.zeros((p.ny, p.nx), F32)
        dz = [zero, zero]
        for c in range(2):
            if z == zc - 1:
                dz[c] = dz[c] + hi_ref[c]
            if z == 0:
                dz[c] = dz[c] - lo_ref[c]
        out_ref[0, z] = n_ref[0, z] + 0.05 * (dy(1, z) - dz[1])
        out_ref[1, z] = n_ref[1, z] + 0.05 * dz[0]
        out_ref[2, z] = n_ref[2, z] - 0.05 * dy(0, z)


def struct(*shape, dtype=F32):
    return jax.ShapeDtypeStruct(shape, dtype)


def call(kernel, outs, n_in, name, scratch=()):
    return pl.pallas_call(
        kernel,
        out_shape=outs,
        in_specs=[VMEM] * n_in,
        out_specs=jax.tree.map(lambda _: VMEM, outs),
        scratch_shapes=list(scratch),
        name=name,
    )


def ring(axis, step):
    n = lax.axis_size(axis)
    return [(i, (i + step) % n) for i in range(n)]


def body(velocity, magnetic, slot_block_table):
    p = Plan(velocity.shape, magnetic.shape, lax.axis_size("xy"))
    plane = (p.ny, p.nx)
    sent, g3, up, down = call(
        functools.partial(restrict_kernel, p),
        (
            struct(p.n, p.r1, p.area),
            struct(p.cz * p.slots, p.rows, dtype=BF16),
            struct(3, *plane),
            struct(3, *plane),
        ),
        3,
        "restrict",
        [pltpu.VMEM((-(-p.rb // 8) * 8, p.area), F32)] * 2,
    )(velocity, slot_block_table.reshape(1, p.slots), magnetic)
    got = lax.all_to_all(sent, "xy", 0, 0, tiled=True)
    below = lax.ppermute(up, "gz", ring("gz", 1))
    above = lax.ppermute(down, "gz", ring("gz", -1))
    sent, partial, up, down = call(
        functools.partial(field_kernel, p),
        (struct(p.n, p.r2, p.area), struct(*magnetic.shape), struct(2, *plane), struct(2, *plane)),
        4,
        "field",
        [pltpu.VMEM((2, p.re, p.area), F32)],
    )(got, magnetic, below, above)
    got = lax.all_to_all(sent, "xy", 0, 0, tiled=True)
    below = lax.ppermute(up, "gz", ring("gz", 1))
    above = lax.ppermute(down, "gz", ring("gz", -1))
    updated = call(functools.partial(widen_kernel, p), struct(*velocity.shape), 3, "widen")(got, g3, velocity)
    finished = call(functools.partial(finish_kernel, p), struct(*magnetic.shape), 4, "finish")(
        partial, got, below, above
    )
    return updated, finished


def solution(mesh):
    return jax.shard_map(
        body,
        mesh=mesh,
        in_specs=(P(None, "gz", "xy", None), P(None, "gz", "xy", None), P("xy")),
        out_specs=(P(None, "gz", "xy", None), P(None, "gz", "xy", None)),
        check_vma=False,
    )
```

```python
import functools
import math

import jax
import jax.numpy as jnp
from jax import lax
from jax.experimental import pallas as pl
from jax.experimental.pallas import tpu as pltpu
from jax.sharding import PartitionSpec as P

F32, BF16 = jnp.float32, jnp.bfloat16
VMEM = pl.BlockSpec(memory_space=pltpu.VMEM)


def split(x):
    hi = x.astype(BF16)
    return hi, (x - hi.astype(F32)).astype(BF16)


def dot(a, b):
    return jnp.dot(a, b, preferred_element_type=F32)


def iota(shape, dim):
    return lax.broadcasted_iota(jnp.int32, shape, dim)


def one_hot(mask):
    return jnp.where(mask, 1.0, 0.0).astype(BF16)


def log2(x):
    assert x == 1 << (x.bit_length() - 1)
    return x.bit_length() - 1


class Plan:
    def __init__(self, vshape, bshape, n):
        self.n = n
        self.slots = vshape[2]
        self.k = self.slots // n
        self.zc = bshape[1]
        self.ny, self.nx = bshape[2:]
        self.edge = math.isqrt(vshape[3])
        self.half = self.edge // 2
        self.area = self.half * self.half
        self.bcols = self.nx // self.half
        self.cz = 3 * self.zc
        self.ru = -(-self.cz * self.k // 8) * 8
        self.rows = n * self.ru
        self.rb = self.cz * self.nx // self.area
        self.r1 = -(-(self.ru + self.rb + 1) // 8) * 8
        self.re = 2 * self.zc * self.nx // self.area
        self.r2 = -(-(self.ru + self.re) // 8) * 8
        self.wrap = self.nx // self.area


def send_positions(p, table):
    s = p.slots
    row = jnp.broadcast_to((table >> log2(p.bcols)).astype(F32), (s, s))
    i, j = iota((s, s), 0), iota((s, s), 1)
    row_s = jnp.sum(jnp.where(i == j, row, 0.0), axis=1, keepdims=True)
    rank = jnp.sum(jnp.where((row_s == row) & (i < j), 1.0, 0.0), axis=0, keepdims=True)
    q = row[0:1] * p.k + rank
    q_s = jnp.sum(jnp.where(i == j, jnp.broadcast_to(q, (s, s)), 0.0), axis=1, keepdims=True)
    return q, q_s


def lane_route(p):
    lane = iota((1, p.rows), 1)
    r = jnp.floor((lane.astype(F32) + 0.5) * (1.0 / p.ru)).astype(jnp.int32)
    i = lane - r * p.ru
    return r, i >> log2(p.k), i & (p.k - 1)


def restrict_kernel(p, v_ref, t_ref, b_ref, out_ref, g3_ref, up_ref, down_ref, last, first):
    n, k, s = p.n, p.k, p.slots
    me = lax.axis_index("xy")
    table = t_ref[...]
    q, q_s = send_positions(p, table)
    lanes = p.cz * s
    rep = one_hot((iota((s, lanes), 1) & (s - 1)) == iota((s, lanes), 0))
    qt = dot(jnp.broadcast_to(q, (8, s)).astype(BF16), rep)[0:1]
    shape = (n, p.ru, lanes)
    i = iota(shape, 1)
    target = (iota(shape, 0) * k + (i & (k - 1))).astype(F32)
    g = one_hot(((i >> log2(k)) == (iota(shape, 2) >> log2(s))) & (target == qt.reshape(1, 1, lanes)))
    g = g.reshape(p.rows, lanes)
    r_l, c_l, j_l = lane_route(p)
    shape = (p.cz, s, p.rows)
    g3 = (iota(shape, 0) == c_l.reshape(1, 1, p.rows)) & (
        q_s.reshape(1, s, 1) == (r_l * k + j_l).astype(F32).reshape(1, 1, p.rows)
    )
    g3_ref[...] = one_hot(g3).reshape(p.cz * s, p.rows)
    half_fine = p.edge * p.edge // 2
    half_area = p.area // 2
    f, c = iota((half_fine, half_area), 0), iota((half_fine, half_area), 1)
    e = log2(p.edge)
    coarse = ((f >> (e + 1)) << (e - 1)) + ((f & (p.edge - 1)) >> 1)
    sel = one_hot(coarse == c)
    z_sum = jnp.concatenate(
        [v_ref[c, 2 * z] + v_ref[c, 2 * z + 1] for c in range(3) for z in range(p.zc)], axis=0
    )
    hi, lo = split(z_sum)
    parts = []
    for h in range(2):
        w = slice(h * half_fine, (h + 1) * half_fine)
        parts.append(dot(hi[:, w], sel) + dot(lo[:, w], sel))
    u = jnp.concatenate(parts, axis=1) * 0.125
    hi, lo = split(u)
    out_ref[:, : p.ru, :] = (dot(g, hi) + dot(g, lo)).reshape(n, p.ru, p.area)
    for c in range(3):
        for z in range(p.zc):
            for h in range(p.wrap):
                at = (c * p.zc + z) * p.wrap + h
                w = slice(h * p.area, (h + 1) * p.area)
                last[at : at + 1, :] = b_ref[c, z, p.ny - 1 : p.ny, w]
                first[at : at + 1, :] = b_ref[c, z, 0:1, w]
    nxt = lax.rem(me + 1, n)
    for r in range(n):
        out_ref[r, p.ru : p.ru + p.rb, :] = jnp.where(r == nxt, last[: p.rb], first[: p.rb])
    col = jnp.broadcast_to((table & (p.bcols - 1)).astype(F32), (s, s))
    qi = iota((s, s), 0).astype(F32)
    col_q = jnp.sum(jnp.where(qi == jnp.broadcast_to(q, (s, s)), col, 0.0), axis=1, keepdims=True)
    qa, la = iota((s, p.area), 0), iota((s, p.area), 1)
    spread = jnp.where((qa & (k - 1)) == (la & (k - 1)), col_q, 0.0).astype(BF16)
    gather = one_hot((iota((n, s), 1) >> log2(k)) == iota((n, s), 0))
    cols = dot(gather, spread)
    at = p.ru + p.rb
    for r in range(n):
        out_ref[r, at : at + 1, :] = cols[r : r + 1]
    up_ref[...] = b_ref[:, p.zc - 1]
    down_ref[...] = b_ref[:, 0]


def tile_transpose(p, t):
    ax = t.ndim - 2
    s, g = iota(t.shape, ax), iota(t.shape, ax + 1) >> log2(p.half)
    for b in (1, 2, 4):
        w = b * p.half
        up = pltpu.roll(pltpu.roll(t, 8 - b, ax), w, ax + 1)
        dn = up if b == 4 else pltpu.roll(pltpu.roll(t, b, ax), 128 - w, ax + 1)
        sb, gb = (s & b) != 0, (g & b) != 0
        t = jnp.where(sb == gb, t, jnp.where(gb, up, dn))
    return t


def blocks_to_grid(p, blk):
    rows = []
    for yh in range(p.half // 8):
        rows.append(
            jnp.concatenate(
                [
                    tile_transpose(p, blk[8 * c : 8 * c + 8, 128 * yh : 128 * yh + 128])
                    for c in range(p.bcols // 8)
                ],
                axis=1,
            )
        )
    return jnp.concatenate(rows, axis=0)


def grid_to_blocks(p, grid):
    rows = []
    for c in range(p.bcols // 8):
        rows.append(
            jnp.concatenate(
                [
                    tile_transpose(p, grid[8 * yh : 8 * yh + 8, 128 * c : 128 * c + 128])
                    for yh in range(p.half // 8)
                ],
                axis=1,
            )
        )
    return jnp.concatenate(rows, axis=0)


def x_next(f):
    return pltpu.roll(f, f.shape[1] - 1, 1)


def x_prev(f):
    return pltpu.roll(f, 1, 1)


def y_next(f, halo):
    return jnp.where(iota(f.shape, 0) == f.shape[0] - 1, halo, pltpu.roll(f, f.shape[0] - 1, 0))


def y_prev(f, halo):
    return jnp.where(iota(f.shape, 0) == 0, halo, pltpu.roll(f, 1, 0))


def row_of(p, ref, src, at):
    return jnp.concatenate([ref[src, pl.ds(at + h, 1), :] for h in range(p.wrap)], axis=1)


def field_kernel(p, r_ref, b_ref, lo_ref, hi_ref, out_ref, next_ref, up_ref, down_ref, e_rows):
    n, k, zc = p.n, p.k, p.zc
    me = lax.axis_index("xy")
    nxt, prv = lax.rem(me + 1, n), lax.rem(me + n - 1, n)
    cols = r_ref[:, p.ru + p.rb, :]
    r_l, c_l, _ = lane_route(p)
    shape = (n, p.rows)
    col_l = jnp.sum(jnp.where(iota(shape, 0) == r_l, cols[:, : p.rows], 0.0), axis=0, keepdims=True)
    shape = (p.cz, p.bcols, p.rows)
    g2 = one_hot(
        (iota(shape, 0) == c_l.reshape(1, 1, p.rows))
        & (iota(shape, 1).astype(F32) == col_l.reshape(1, 1, p.rows))
    ).reshape(p.cz * p.bcols, p.rows)
    shape = (n, p.ru, 128)
    col_s = jnp.sum(
        jnp.where((iota(shape, 1) & (k - 1)) == iota(shape, 2), cols[:, None, :128], 0.0), axis=2, keepdims=True
    )
    lanes = p.cz * p.bcols
    shape = (n, p.ru, lanes)
    lane = iota(shape, 2)
    g2t = one_hot(
        ((iota(shape, 1) >> log2(k)) == (lane >> log2(p.bcols)))
        & (col_s == (lane & (p.bcols - 1)).astype(F32))
    ).reshape(p.rows, lanes)
    hi, lo = split(r_ref[:, : p.ru, :].reshape(p.rows, p.area))
    u_blk = dot(g2, hi) + dot(g2, lo)
    u = [
        [blocks_to_grid(p, u_blk[(c * zc + z) * p.bcols : (c * zc + z + 1) * p.bcols]) for z in range(zc)]
        for c in range(3)
    ]
    b = [[b_ref[c, z] for z in range(zc)] for c in range(3)]
    force = []
    for z in range(zc):
        bz = [b[c][z] for c in range(3)]
        below = [lo_ref[c] if z == 0 else b[c][z - 1] for c in range(3)]
        above = [hi_ref[c] if z == zc - 1 else b[c][z + 1] for c in range(3)]
        north, south, east, west = [], [], [], []
        for c in range(3):
            at = p.ru + (c * zc + z) * p.wrap
            south.append(y_prev(bz[c], row_of(p, r_ref, prv, at)))
            north.append(y_next(bz[c], row_of(p, r_ref, nxt, at)))
            east.append(x_next(bz[c]))
            west.append(x_prev(bz[c]))
        dz = [(above[c] - below[c]) * 0.5 for c in range(2)]
        j0 = (north[2] - south[2]) * 0.5 - dz[1]
        j1 = dz[0] - (east[2] - west[2]) * 0.5
        j2 = (east[1] - west[1]) * 0.5 - (north[0] - south[0]) * 0.5
        force.append([j1 * bz[2] - j2 * bz[1], j2 * bz[0] - j0 * bz[2], j0 * bz[1] - j1 * bz[0]])
        for c in range(3):
            lap = above[c] + below[c] + north[c] + south[c] + east[c] + west[c] - 6.0 * bz[c]
            next_ref[c, z] = bz[c] + 0.05 * lap
    f_blk = jnp.concatenate([grid_to_blocks(p, force[z][c]) for c in range(3) for z in range(zc)], axis=0)
    hi, lo = split(f_blk)
    out_ref[:, : p.ru, :] = (dot(g2t, hi) + dot(g2t, lo)).reshape(n, p.ru, p.area)
    e = []
    for z in range(zc):
        uz, bz = [u[c][z] for c in range(3)], [b[c][z] for c in range(3)]
        e.append([uz[1] * bz[2] - uz[2] * bz[1], uz[2] * bz[0] - uz[0] * bz[2], uz[0] * bz[1] - uz[1] * bz[0]])
    for z in range(zc):
        ez = e[z]
        zero = jnp.zeros_like(ez[0])
        above = e[z + 1] if z < zc - 1 else (zero, zero)
        below = e[z - 1] if z > 0 else (zero, zero)
        dy2 = y_next(ez[2], 0.0) - y_prev(ez[2], 0.0)
        dy0 = y_next(ez[0], 0.0) - y_prev(ez[0], 0.0)
        next_ref[0, z] += 0.05 * (dy2 - (above[1] - below[1]))
        next_ref[1, z] += 0.05 * ((above[0] - below[0]) - (x_next(ez[2]) - x_prev(ez[2])))
        next_ref[2, z] += 0.05 * ((x_next(ez[1]) - x_prev(ez[1])) - dy0)
        for i, c in enumerate((0, 2)):
            for h in range(p.wrap):
                at = (i * zc + z) * p.wrap + h
                w = slice(h * p.area, (h + 1) * p.area)
                e_rows[0, at : at + 1, :] = ez[c][0:1, w]
                e_rows[1, at : at + 1, :] = ez[c][p.ny - 1 : p.ny, w]
    for r in range(n):
        out_ref[r, p.ru : p.ru + p.re, :] = jnp.where(r == nxt, e_rows[1], e_rows[0])
    up_ref[0], up_ref[1] = e[zc - 1][0], e[zc - 1][1]
    down_ref[0], down_ref[1] = e[0][0], e[0][1]


def widen_kernel(p, r_ref, g_ref, v_ref, out_ref):
    half_fine = p.edge * p.edge // 2
    half_area = p.area // 2
    e = log2(p.edge)
    c, f = iota((half_area, half_fine), 0), iota((half_area, half_fine), 1)
    coarse = ((f >> (e + 1)) << (e - 1)) + ((f & (p.edge - 1)) >> 1)
    sel = one_hot(coarse == c)
    hi, lo = split(r_ref[:, : p.ru, :].reshape(p.rows, p.area) * 0.1)
    g = g_ref[...]
    hi, lo = dot(g, hi).astype(BF16), dot(g, lo).astype(BF16)
    s = p.slots
    for h in range(2):
        w = slice(h * half_area, (h + 1) * half_area)
        wide = dot(hi[:, w], sel) + dot(lo[:, w], sel)
        fw = slice(h * half_fine, (h + 1) * half_fine)
        for c in range(3):
            for z in range(p.zc):
                add = wide[(c * p.zc + z) * s : (c * p.zc + z + 1) * s]
                for d in range(2):
                    out_ref[c, 2 * z + d, :, fw] = v_ref[c, 2 * z + d, :, fw] + add


def finish_kernel(p, n_ref, r_ref, lo_ref, hi_ref, out_ref):
    n, zc = p.n, p.zc
    me = lax.axis_index("xy")
    nxt, prv = lax.rem(me + 1, n), lax.rem(me + n - 1, n)
    y = iota((p.ny, p.nx), 0)

    def dy(i, z):
        at = p.ru + (i * zc + z) * p.wrap
        north, south = row_of(p, r_ref, nxt, at), row_of(p, r_ref, prv, at)
        return jnp.where(y == p.ny - 1, north, 0.0) - jnp.where(y == 0, south, 0.0)

    for z in range(zc):
        zero = jnp.zeros((p.ny, p.nx), F32)
        dz = [zero, zero]
        for c in range(2):
            if z == zc - 1:
                dz[c] = dz[c] + hi_ref[c]
            if z == 0:
                dz[c] = dz[c] - lo_ref[c]
        out_ref[0, z] = n_ref[0, z] + 0.05 * (dy(1, z) - dz[1])
        out_ref[1, z] = n_ref[1, z] + 0.05 * dz[0]
        out_ref[2, z] = n_ref[2, z] - 0.05 * dy(0, z)


def struct(*shape, dtype=F32):
    return jax.ShapeDtypeStruct(shape, dtype)


def call(kernel, outs, n_in, name, scratch=()):
    return pl.pallas_call(
        kernel,
        out_shape=outs,
        in_specs=[VMEM] * n_in,
        out_specs=jax.tree.map(lambda _: VMEM, outs),
        scratch_shapes=list(scratch),
        name=name,
        compiler_params=pltpu.CompilerParams(vmem_limit_bytes=20 << 20),
    )


def ring(axis, step):
    n = lax.axis_size(axis)
    return [(i, (i + step) % n) for i in range(n)]


def body(velocity, magnetic, slot_block_table):
    p = Plan(velocity.shape, magnetic.shape, lax.axis_size("xy"))
    plane = (p.ny, p.nx)
    sent, g3, up, down = call(
        functools.partial(restrict_kernel, p),
        (
            struct(p.n, p.r1, p.area),
            struct(p.cz * p.slots, p.rows, dtype=BF16),
            struct(3, *plane),
            struct(3, *plane),
        ),
        3,
        "restrict",
        [pltpu.VMEM((-(-p.rb // 8) * 8, p.area), F32)] * 2,
    )(velocity, slot_block_table.reshape(1, p.slots), magnetic)
    got = lax.all_to_all(sent, "xy", 0, 0, tiled=True)
    below = lax.ppermute(up, "gz", ring("gz", 1))
    above = lax.ppermute(down, "gz", ring("gz", -1))
    sent, partial, up, down = call(
        functools.partial(field_kernel, p),
        (struct(p.n, p.r2, p.area), struct(*magnetic.shape), struct(2, *plane), struct(2, *plane)),
        4,
        "field",
        [pltpu.VMEM((2, p.re, p.area), F32)],
    )(got, magnetic, below, above)
    got = lax.all_to_all(sent, "xy", 0, 0, tiled=True)
    below = lax.ppermute(up, "gz", ring("gz", 1))
    above = lax.ppermute(down, "gz", ring("gz", -1))
    updated = call(functools.partial(widen_kernel, p), struct(*velocity.shape), 3, "widen")(got, g3, velocity)
    finished = call(functools.partial(finish_kernel, p), struct(*magnetic.shape), 4, "finish")(
        partial, got, below, above
    )
    return updated, finished


def solution(mesh):
    return jax.shard_map(
        body,
        mesh=mesh,
        in_specs=(P(None, "gz", "xy", None), P(None, "gz", "xy", None), P("xy")),
        out_specs=(P(None, "gz", "xy", None), P(None, "gz", "xy", None)),
        check_vma=False,
    )
```

```python
import functools
import math

import jax
import jax.numpy as jnp
from jax import lax
from jax.experimental import pallas as pl
from jax.experimental.pallas import tpu as pltpu
from jax.sharding import PartitionSpec as P

F32, BF16 = jnp.float32, jnp.bfloat16
VMEM = pl.BlockSpec(memory_space=pltpu.VMEM)
ALL_VMEM = 67043328
HBM = pl.BlockSpec(memory_space=pltpu.HBM)


def split(x):
    hi = x.astype(BF16)
    return hi, (x - hi.astype(F32)).astype(BF16)


def dot(a, b):
    return jnp.dot(a, b, preferred_element_type=F32)


def iota(shape, dim):
    return lax.broadcasted_iota(jnp.int32, shape, dim)


def one_hot(mask):
    return jnp.where(mask, 1.0, 0.0).astype(BF16)


def log2(x):
    assert x == 1 << (x.bit_length() - 1)
    return x.bit_length() - 1


class Plan:
    def __init__(self, vshape, bshape, n):
        self.n = n
        self.slots = vshape[2]
        self.k = self.slots // n
        self.zc = bshape[1]
        self.ny, self.nx = bshape[2:]
        self.edge = math.isqrt(vshape[3])
        self.half = self.edge // 2
        self.area = self.half * self.half
        self.bcols = self.nx // self.half
        self.cz = 3 * self.zc
        self.ru = -(-self.cz * self.k // 8) * 8
        self.rows = n * self.ru
        self.rb = self.cz * self.nx // self.area
        self.r1 = -(-(self.ru + self.rb + 1) // 8) * 8
        self.re = 2 * self.zc * self.nx // self.area
        self.r2 = -(-(self.ru + self.re) // 8) * 8
        self.wrap = self.nx // self.area


def send_positions(p, table):
    s = p.slots
    row = jnp.broadcast_to((table >> log2(p.bcols)).astype(F32), (s, s))
    i, j = iota((s, s), 0), iota((s, s), 1)
    row_s = jnp.sum(jnp.where(i == j, row, 0.0), axis=1, keepdims=True)
    rank = jnp.sum(jnp.where((row_s == row) & (i < j), 1.0, 0.0), axis=0, keepdims=True)
    q = row[0:1] * p.k + rank
    q_s = jnp.sum(jnp.where(i == j, jnp.broadcast_to(q, (s, s)), 0.0), axis=1, keepdims=True)
    return q, q_s


def lane_route(p):
    lane = iota((1, p.rows), 1)
    r = jnp.floor((lane.astype(F32) + 0.5) * (1.0 / p.ru)).astype(jnp.int32)
    i = lane - r * p.ru
    return r, i >> log2(p.k), i & (p.k - 1)


def restrict_kernel(p, v_hbm, t_hbm, b_hbm, out_ref, g3_ref, up_ref, down_ref, v_ref, t_ref, b_ref, last, first, sems):
    n, k, s = p.n, p.k, p.slots
    me = lax.axis_index("xy")
    t_copy = pltpu.make_async_copy(t_hbm, t_ref, sems.at[0])
    b_copy = pltpu.make_async_copy(b_hbm, b_ref, sems.at[1])
    v_copies = [pltpu.make_async_copy(v_hbm.at[c], v_ref.at[c], sems.at[2 + c]) for c in range(3)]
    t_copy.start()
    for copy in v_copies:
        copy.start()
    b_copy.start()
    t_copy.wait()
    table = t_ref[...]
    q, q_s = send_positions(p, table)
    lanes = p.cz * s
    rep = one_hot((iota((s, lanes), 1) & (s - 1)) == iota((s, lanes), 0))
    qt = dot(jnp.broadcast_to(q, (8, s)).astype(BF16), rep)[0:1]
    shape = (n, p.ru, lanes)
    i = iota(shape, 1)
    target = (iota(shape, 0) * k + (i & (k - 1))).astype(F32)
    g = one_hot(((i >> log2(k)) == (iota(shape, 2) >> log2(s))) & (target == qt.reshape(1, 1, lanes)))
    g = g.reshape(p.rows, lanes)
    r_l, c_l, j_l = lane_route(p)
    shape = (p.cz, s, p.rows)
    g3 = (iota(shape, 0) == c_l.reshape(1, 1, p.rows)) & (
        q_s.reshape(1, s, 1) == (r_l * k + j_l).astype(F32).reshape(1, 1, p.rows)
    )
    g3_ref[...] = one_hot(g3).reshape(p.cz * s, p.rows)
    col = jnp.broadcast_to((table & (p.bcols - 1)).astype(F32), (s, s))
    qi = iota((s, s), 0).astype(F32)
    col_q = jnp.sum(jnp.where(qi == jnp.broadcast_to(q, (s, s)), col, 0.0), axis=1, keepdims=True)
    qa, la = iota((s, p.area), 0), iota((s, p.area), 1)
    spread = jnp.where((qa & (k - 1)) == (la & (k - 1)), col_q, 0.0).astype(BF16)
    gather = one_hot((iota((n, s), 1) >> log2(k)) == iota((n, s), 0))
    cols = dot(gather, spread)
    at = p.ru + p.rb
    for r in range(n):
        out_ref[r, at : at + 1, :] = cols[r : r + 1]
    half_fine = p.edge * p.edge // 2
    half_area = p.area // 2
    f, c = iota((half_fine, half_area), 0), iota((half_fine, half_area), 1)
    e = log2(p.edge)
    coarse = ((f >> (e + 1)) << (e - 1)) + ((f & (p.edge - 1)) >> 1)
    sel = one_hot(coarse == c)
    parts = []
    for c in range(3):
        v_copies[c].wait()
        z_sum = jnp.concatenate([v_ref[c, 2 * z] + v_ref[c, 2 * z + 1] for z in range(p.zc)], axis=0)
        hi, lo = split(z_sum)
        ws = [slice(h * half_fine, (h + 1) * half_fine) for h in range(2)]
        parts.append(jnp.concatenate([dot(hi[:, w], sel) + dot(lo[:, w], sel) for w in ws], axis=1))
    hi, lo = split(jnp.concatenate(parts, axis=0) * 0.125)
    out_ref[:, : p.ru, :] = (dot(g, hi) + dot(g, lo)).reshape(n, p.ru, p.area)
    b_copy.wait()
    for c in range(3):
        for z in range(p.zc):
            for h in range(p.wrap):
                at = (c * p.zc + z) * p.wrap + h
                w = slice(h * p.area, (h + 1) * p.area)
                last[at : at + 1, :] = b_ref[c, z, p.ny - 1 : p.ny, w]
                first[at : at + 1, :] = b_ref[c, z, 0:1, w]
    nxt = lax.rem(me + 1, n)
    for r in range(n):
        out_ref[r, p.ru : p.ru + p.rb, :] = jnp.where(r == nxt, last[: p.rb], first[: p.rb])
    up_ref[...] = b_ref[0:2, p.zc - 1]
    down_ref[...] = b_ref[0:2, 0]


def tile_transpose(p, t):
    ax = t.ndim - 2
    s, g = iota(t.shape, ax), iota(t.shape, ax + 1) >> log2(p.half)
    for b in (1, 2, 4):
        w = b * p.half
        up = pltpu.roll(pltpu.roll(t, 8 - b, ax), w, ax + 1)
        dn = up if b == 4 else pltpu.roll(pltpu.roll(t, b, ax), 128 - w, ax + 1)
        sb, gb = (s & b) != 0, (g & b) != 0
        t = jnp.where(sb == gb, t, jnp.where(gb, up, dn))
    return t


def blocks_to_grid(p, blk):
    rows = []
    for yh in range(p.half // 8):
        rows.append(
            jnp.concatenate(
                [
                    tile_transpose(p, blk[8 * c : 8 * c + 8, 128 * yh : 128 * yh + 128])
                    for c in range(p.bcols // 8)
                ],
                axis=1,
            )
        )
    return jnp.concatenate(rows, axis=0)


def grid_to_blocks(p, grid):
    rows = []
    for c in range(p.bcols // 8):
        rows.append(
            jnp.concatenate(
                [
                    tile_transpose(p, grid[8 * yh : 8 * yh + 8, 128 * c : 128 * c + 128])
                    for yh in range(p.half // 8)
                ],
                axis=1,
            )
        )
    return jnp.concatenate(rows, axis=0)


def x_next(f):
    return pltpu.roll(f, f.shape[1] - 1, 1)


def x_prev(f):
    return pltpu.roll(f, 1, 1)


def y_next(f, halo):
    return jnp.where(iota(f.shape, 0) == f.shape[0] - 1, halo, pltpu.roll(f, f.shape[0] - 1, 0))


def y_prev(f, halo):
    return jnp.where(iota(f.shape, 0) == 0, halo, pltpu.roll(f, 1, 0))


def row_of(p, ref, src, at):
    return jnp.concatenate([ref[src, pl.ds(at + h, 1), :] for h in range(p.wrap)], axis=1)


def interior_kernel(p, b_ref, copy_ref, j_ref, next_ref):
    zero = jnp.zeros((p.ny, p.nx), F32)
    for z in range(p.zc):
        b = [b_ref[c, z] for c in range(3)]
        below = [b_ref[c, z - 1] if z > 0 else zero for c in range(3)]
        above = [b_ref[c, z + 1] if z < p.zc - 1 else zero for c in range(3)]
        south, north = [y_prev(f, 0.0) for f in b], [y_next(f, 0.0) for f in b]
        west, east = [x_prev(f) for f in b], [x_next(f) for f in b]
        j_ref[0, z] = ((north[2] - south[2]) - (above[1] - below[1])) * 0.5
        j_ref[1, z] = ((above[0] - below[0]) - (east[2] - west[2])) * 0.5
        j_ref[2, z] = ((east[1] - west[1]) - (north[0] - south[0])) * 0.5
        for c in range(3):
            lap = below[c] + above[c] + south[c] + north[c] + west[c] + east[c] - 6.0 * b[c]
            next_ref[c, z] = b[c] + 0.05 * lap
            copy_ref[c, z] = b[c]


def edge_rows(p, ref, nxt, prv, at):
    y = iota((p.ny, p.nx), 0)
    north = jnp.where(y == p.ny - 1, row_of(p, ref, nxt, at), 0.0)
    return north, jnp.where(y == 0, row_of(p, ref, prv, at), 0.0)


def field_kernel(p, r_ref, b_ref, j_ref, lo_ref, hi_ref, out_ref, e_ref, up_ref, down_ref, e_rows):
    n, k, zc = p.n, p.k, p.zc
    me = lax.axis_index("xy")
    nxt, prv = lax.rem(me + 1, n), lax.rem(me + n - 1, n)
    cols = r_ref[:, p.ru + p.rb, :]
    r_l, c_l, _ = lane_route(p)
    shape = (n, p.rows)
    col_l = jnp.sum(jnp.where(iota(shape, 0) == r_l, cols[:, : p.rows], 0.0), axis=0, keepdims=True)
    shape = (p.cz, p.bcols, p.rows)
    g2 = one_hot(
        (iota(shape, 0) == c_l.reshape(1, 1, p.rows))
        & (iota(shape, 1).astype(F32) == col_l.reshape(1, 1, p.rows))
    ).reshape(p.cz * p.bcols, p.rows)
    shape = (n, p.ru, 128)
    col_s = jnp.sum(
        jnp.where((iota(shape, 1) & (k - 1)) == iota(shape, 2), cols[:, None, :128], 0.0), axis=2, keepdims=True
    )
    lanes = p.cz * p.bcols
    shape = (n, p.ru, lanes)
    lane = iota(shape, 2)
    g2t = one_hot(
        ((iota(shape, 1) >> log2(k)) == (lane >> log2(p.bcols)))
        & (col_s == (lane & (p.bcols - 1)).astype(F32))
    ).reshape(p.rows, lanes)
    hi, lo = split(r_ref[:, : p.ru, :].reshape(p.rows, p.area))
    u_blk = dot(g2, hi) + dot(g2, lo)
    u = [
        [blocks_to_grid(p, u_blk[(c * zc + z) * p.bcols : (c * zc + z + 1) * p.bcols]) for z in range(zc)]
        for c in range(3)
    ]
    b = [[b_ref[c, z] for z in range(zc)] for c in range(3)]
    force = []
    zero = jnp.zeros((p.ny, p.nx), F32)
    for z in range(zc):
        bz = [b[c][z] for c in range(3)]
        dy = {}
        for c in (0, 2):
            north, south = edge_rows(p, r_ref, nxt, prv, p.ru + (c * zc + z) * p.wrap)
            dy[c] = north - south
        dz = [zero, zero]
        for c in range(2):
            if z == zc - 1:
                dz[c] = dz[c] + hi_ref[c]
            if z == 0:
                dz[c] = dz[c] - lo_ref[c]
        j0 = j_ref[0, z] + (dy[2] - dz[1]) * 0.5
        j1 = j_ref[1, z] + dz[0] * 0.5
        j2 = j_ref[2, z] - dy[0] * 0.5
        force.append([j1 * bz[2] - j2 * bz[1], j2 * bz[0] - j0 * bz[2], j0 * bz[1] - j1 * bz[0]])
    f_blk = jnp.concatenate([grid_to_blocks(p, force[z][c]) for c in range(3) for z in range(zc)], axis=0)
    hi, lo = split(f_blk)
    out_ref[:, : p.ru, :] = (dot(g2t, hi) + dot(g2t, lo)).reshape(n, p.ru, p.area)
    for z in range(zc):
        uz, bz = [u[c][z] for c in range(3)], [b[c][z] for c in range(3)]
        ez = [uz[1] * bz[2] - uz[2] * bz[1], uz[2] * bz[0] - uz[0] * bz[2], uz[0] * bz[1] - uz[1] * bz[0]]
        for c in range(3):
            e_ref[c, z] = ez[c]
        if z == zc - 1:
            up_ref[0], up_ref[1], up_ref[2] = ez[0], ez[1], bz[2]
        if z == 0:
            down_ref[0], down_ref[1], down_ref[2] = ez[0], ez[1], bz[2]
        for i, c in enumerate((0, 2)):
            for h in range(p.wrap):
                at = (i * zc + z) * p.wrap + h
                w = slice(h * p.area, (h + 1) * p.area)
                e_rows[0, at : at + 1, :] = ez[c][0:1, w]
                e_rows[1, at : at + 1, :] = ez[c][p.ny - 1 : p.ny, w]
    for r in range(n):
        out_ref[r, p.ru : p.ru + p.re, :] = jnp.where(r == nxt, e_rows[1], e_rows[0])


def local_kernel(p, r_ref, b_ref, lo_ref, hi_ref, e_ref, next_ref):
    n, zc = p.n, p.zc
    me = lax.axis_index("xy")
    nxt, prv = lax.rem(me + 1, n), lax.rem(me + n - 1, n)
    zero = jnp.zeros((p.ny, p.nx), F32)
    for z in range(zc):
        e = [e_ref[c, z] for c in range(3)]
        above = [e_ref[c, z + 1] if z < zc - 1 else zero for c in range(2)]
        below = [e_ref[c, z - 1] if z > 0 else zero for c in range(2)]
        curl = [
            (y_next(e[2], 0.0) - y_prev(e[2], 0.0)) - (above[1] - below[1]),
            (above[0] - below[0]) - (x_next(e[2]) - x_prev(e[2])),
            (x_next(e[1]) - x_prev(e[1])) - (y_next(e[0], 0.0) - y_prev(e[0], 0.0)),
        ]
        for c in range(3):
            north, south = edge_rows(p, r_ref, nxt, prv, p.ru + (c * zc + z) * p.wrap)
            total = curl[c] + north + south
            if c < 2 and z == 0:
                total = total + lo_ref[c]
            if c < 2 and z == zc - 1:
                total = total + hi_ref[c]
            next_ref[c, z] = b_ref[c, z] + 0.05 * total


def finish_kernel(p, r_ref, g_ref, v_ref, n_ref, lo_ref, hi_ref, vel_hbm, mag_hbm, vel, mag, sems):
    n, zc = p.n, p.zc
    half_fine = p.edge * p.edge // 2
    half_area = p.area // 2
    ex = log2(p.edge)
    c, f = iota((half_area, half_fine), 0), iota((half_area, half_fine), 1)
    coarse = ((f >> (ex + 1)) << (ex - 1)) + ((f & (p.edge - 1)) >> 1)
    sel = one_hot(coarse == c)
    hi, lo = split(r_ref[:, : p.ru, :].reshape(p.rows, p.area) * 0.1)
    g = g_ref[...]
    hi, lo = dot(g, hi).astype(BF16), dot(g, lo).astype(BF16)
    s = p.slots
    copies = []
    for c in range(3):
        for z in range(zc):
            at = slice((c * zc + z) * s, (c * zc + z + 1) * s)
            for h in range(2):
                w = slice(h * half_area, (h + 1) * half_area)
                fw = slice(h * half_fine, (h + 1) * half_fine)
                add = dot(hi[at, w], sel) + dot(lo[at, w], sel)
                for d in range(2):
                    vel[c, 2 * z + d, :, fw] = v_ref[c, 2 * z + d, :, fw] + add
        copies.append(pltpu.make_async_copy(vel.at[c], vel_hbm.at[c], sems.at[c]))
        copies[-1].start()
    me = lax.axis_index("xy")
    nxt, prv = lax.rem(me + 1, n), lax.rem(me + n - 1, n)

    def dy(i, z):
        north, south = edge_rows(p, r_ref, nxt, prv, p.ru + (i * zc + z) * p.wrap)
        return north - south

    for z in range(zc):
        dz = [jnp.zeros((p.ny, p.nx), F32)] * 2
        outer = dz[0]
        if z == zc - 1:
            dz = [dz[c] + hi_ref[c] for c in range(2)]
            outer = outer + hi_ref[2]
        if z == 0:
            dz = [dz[c] - lo_ref[c] for c in range(2)]
            outer = outer + lo_ref[2]
        mag[0, z] = n_ref[0, z] + 0.05 * (dy(1, z) - dz[1])
        mag[1, z] = n_ref[1, z] + 0.05 * dz[0]
        mag[2, z] = n_ref[2, z] + 0.05 * (outer - dy(0, z))
    copies.append(pltpu.make_async_copy(mag, mag_hbm, sems.at[3]))
    copies[-1].start()
    for copy in copies:
        copy.wait()


def struct(*shape, dtype=F32):
    return jax.ShapeDtypeStruct(shape, dtype)


def call(kernel, ins, outs, name, scratch=(), grant=20 << 20):
    return pl.pallas_call(
        kernel,
        out_shape=[o for o, _ in outs],
        in_specs=ins,
        out_specs=[spec for _, spec in outs],
        scratch_shapes=list(scratch),
        name=name,
        cost_estimate=pl.CostEstimate(flops=1 << 24, bytes_accessed=1 << 20, transcendentals=0),
        compiler_params=pltpu.CompilerParams(vmem_limit_bytes=grant),
    )


def ring(axis, step):
    n = lax.axis_size(axis)
    return [(i, (i + step) % n) for i in range(n)]


def body(velocity, magnetic, slot_block_table):
    p = Plan(velocity.shape, magnetic.shape, lax.axis_size("xy"))
    plane = (p.ny, p.nx)
    dma = pltpu.SemaphoreType.DMA
    sent, g3, up, down = call(
        functools.partial(restrict_kernel, p),
        [HBM] * 3,
        [
            (struct(p.n, p.r1, p.area), VMEM),
            (struct(p.cz * p.slots, p.rows, dtype=BF16), VMEM),
            (struct(2, *plane), VMEM),
            (struct(2, *plane), VMEM),
        ],
        "restrict",
        [
            pltpu.VMEM(velocity.shape, F32),
            pltpu.VMEM((1, p.slots), jnp.int32),
            pltpu.VMEM(magnetic.shape, F32),
            pltpu.VMEM((-(-p.rb // 8) * 8, p.area), F32),
            pltpu.VMEM((-(-p.rb // 8) * 8, p.area), F32),
            dma((5,)),
        ],
        ALL_VMEM,
    )(velocity, slot_block_table.reshape(1, p.slots), magnetic)
    got = lax.all_to_all(sent, "xy", 0, 0, tiled=True)
    below = lax.ppermute(up, "gz", ring("gz", 1))
    above = lax.ppermute(down, "gz", ring("gz", -1))
    held, _ = lax.optimization_barrier((magnetic, up))
    field, current, diffused = call(
        functools.partial(interior_kernel, p), [VMEM], [(struct(*magnetic.shape), VMEM)] * 3, "interior"
    )(held)
    sent, emf, up, down = call(
        functools.partial(field_kernel, p),
        [VMEM] * 5,
        [
            (struct(p.n, p.r2, p.area), VMEM),
            (struct(*magnetic.shape), VMEM),
            (struct(3, *plane), VMEM),
            (struct(3, *plane), VMEM),
        ],
        "field",
        [pltpu.VMEM((2, p.re, p.area), F32)],
    )(got, field, current, below, above)
    got_force = lax.all_to_all(sent, "xy", 0, 0, tiled=True)
    emf_below = lax.ppermute(up, "gz", ring("gz", 1))
    emf_above = lax.ppermute(down, "gz", ring("gz", -1))
    (partial,) = call(
        functools.partial(local_kernel, p), [VMEM] * 5, [(struct(*magnetic.shape), VMEM)], "local"
    )(got, diffused, below, above, emf)
    return tuple(
        call(
            functools.partial(finish_kernel, p),
            [VMEM] * 6,
            [(struct(*velocity.shape), HBM), (struct(*magnetic.shape), HBM)],
            "finish",
            [pltpu.VMEM(velocity.shape, F32), pltpu.VMEM(magnetic.shape, F32), dma((4,))],
        )(got_force, g3, velocity, partial, emf_below, emf_above)
    )


def solution(mesh):
    return jax.shard_map(
        body,
        mesh=mesh,
        in_specs=(P(None, "gz", "xy", None), P(None, "gz", "xy", None), P("xy")),
        out_specs=(P(None, "gz", "xy", None), P(None, "gz", "xy", None)),
        check_vma=False,
    )
```

```python
import functools
import math

import jax
import jax.numpy as jnp
from jax import lax
from jax.experimental import pallas as pl
from jax.experimental.pallas import tpu as pltpu
from jax.sharding import PartitionSpec as P

F32, BF16 = jnp.float32, jnp.bfloat16
VMEM = pl.BlockSpec(memory_space=pltpu.VMEM)
ALL_VMEM = 67043328
HBM = pl.BlockSpec(memory_space=pltpu.HBM)


def split(x):
    hi = x.astype(BF16)
    return hi, (x - hi.astype(F32)).astype(BF16)


def dot(a, b):
    return jnp.dot(a, b, preferred_element_type=F32)


def iota(shape, dim):
    return lax.broadcasted_iota(jnp.int32, shape, dim)


def one_hot(mask):
    return jnp.where(mask, 1.0, 0.0).astype(BF16)


def log2(x):
    assert x == 1 << (x.bit_length() - 1)
    return x.bit_length() - 1


class Plan:
    def __init__(self, vshape, bshape, n):
        self.n = n
        self.slots = vshape[2]
        self.k = self.slots // n
        self.zc = bshape[1]
        self.ny, self.nx = bshape[2:]
        self.edge = math.isqrt(vshape[3])
        self.half = self.edge // 2
        self.area = self.half * self.half
        self.bcols = self.nx // self.half
        self.cz = 3 * self.zc
        self.ru = -(-self.cz * self.k // 8) * 8
        self.rows = n * self.ru
        self.rb = self.cz * self.nx // self.area
        self.r1 = -(-(self.ru + self.rb + 1) // 8) * 8
        self.re = 2 * self.zc * self.nx // self.area
        self.r2 = -(-(self.ru + self.re) // 8) * 8
        self.wrap = self.nx // self.area


def send_positions(p, table):
    s = p.slots
    row = jnp.broadcast_to((table >> log2(p.bcols)).astype(F32), (s, s))
    i, j = iota((s, s), 0), iota((s, s), 1)
    row_s = jnp.sum(jnp.where(i == j, row, 0.0), axis=1, keepdims=True)
    rank = jnp.sum(jnp.where((row_s == row) & (i < j), 1.0, 0.0), axis=0, keepdims=True)
    q = row[0:1] * p.k + rank
    q_s = jnp.sum(jnp.where(i == j, jnp.broadcast_to(q, (s, s)), 0.0), axis=1, keepdims=True)
    return q, q_s


def lane_route(p):
    lane = iota((1, p.rows), 1)
    r = jnp.floor((lane.astype(F32) + 0.5) * (1.0 / p.ru)).astype(jnp.int32)
    i = lane - r * p.ru
    return r, i >> log2(p.k), i & (p.k - 1)


def restrict_kernel(p, v_hbm, t_hbm, b_hbm, out_ref, up_ref, down_ref, v_ref, t_ref, b_ref, last, first, sems):
    n, k, s = p.n, p.k, p.slots
    me = lax.axis_index("xy")
    t_copy = pltpu.make_async_copy(t_hbm, t_ref, sems.at[0])
    b_copy = pltpu.make_async_copy(b_hbm, b_ref, sems.at[1])
    v_copies = [pltpu.make_async_copy(v_hbm.at[c], v_ref.at[c], sems.at[2 + c]) for c in range(3)]
    t_copy.start()
    for copy in v_copies:
        copy.start()
    b_copy.start()
    t_copy.wait()
    table = t_ref[...]
    q, _ = send_positions(p, table)
    lanes = p.cz * s
    rep = one_hot((iota((s, lanes), 1) & (s - 1)) == iota((s, lanes), 0))
    qt = dot(jnp.broadcast_to(q, (8, s)).astype(BF16), rep)[0:1]
    shape = (n, p.ru, lanes)
    i = iota(shape, 1)
    target = (iota(shape, 0) * k + (i & (k - 1))).astype(F32)
    g = one_hot(((i >> log2(k)) == (iota(shape, 2) >> log2(s))) & (target == qt.reshape(1, 1, lanes)))
    g = g.reshape(p.rows, lanes)
    col = jnp.broadcast_to((table & (p.bcols - 1)).astype(F32), (s, s))
    qi = iota((s, s), 0).astype(F32)
    col_q = jnp.sum(jnp.where(qi == jnp.broadcast_to(q, (s, s)), col, 0.0), axis=1, keepdims=True)
    qa, la = iota((s, p.area), 0), iota((s, p.area), 1)
    spread = jnp.where((qa & (k - 1)) == (la & (k - 1)), col_q, 0.0).astype(BF16)
    gather = one_hot((iota((n, s), 1) >> log2(k)) == iota((n, s), 0))
    cols = dot(gather, spread)
    at = p.ru + p.rb
    for r in range(n):
        out_ref[r, at : at + 1, :] = cols[r : r + 1]
    half_fine = p.edge * p.edge // 2
    half_area = p.area // 2
    f, c = iota((half_fine, half_area), 0), iota((half_fine, half_area), 1)
    e = log2(p.edge)
    coarse = ((f >> (e + 1)) << (e - 1)) + ((f & (p.edge - 1)) >> 1)
    sel = one_hot(coarse == c)
    parts = []
    for c in range(3):
        v_copies[c].wait()
        z_sum = jnp.concatenate([v_ref[c, 2 * z] + v_ref[c, 2 * z + 1] for z in range(p.zc)], axis=0)
        hi, lo = split(z_sum)
        m = p.zc * s
        ws = [slice(h * half_fine, (h + 1) * half_fine) for h in range(2)]
        out = dot(jnp.concatenate([x[:, w] for w in ws for x in (hi, lo)], axis=0), sel)
        halves = [out[2 * h * m : (2 * h + 1) * m] + out[(2 * h + 1) * m : (2 * h + 2) * m] for h in range(2)]
        parts.append(jnp.concatenate(halves, axis=1))
    hi, lo = split(jnp.concatenate(parts, axis=0) * 0.125)
    out_ref[:, : p.ru, :] = (dot(g, hi) + dot(g, lo)).reshape(n, p.ru, p.area)
    b_copy.wait()
    for c in range(3):
        for z in range(p.zc):
            for h in range(p.wrap):
                at = (c * p.zc + z) * p.wrap + h
                w = slice(h * p.area, (h + 1) * p.area)
                last[at : at + 1, :] = b_ref[c, z, p.ny - 1 : p.ny, w]
                first[at : at + 1, :] = b_ref[c, z, 0:1, w]
    nxt = lax.rem(me + 1, n)
    for r in range(n):
        out_ref[r, p.ru : p.ru + p.rb, :] = jnp.where(r == nxt, last[: p.rb], first[: p.rb])
    up_ref[...] = b_ref[0:2, p.zc - 1]
    down_ref[...] = b_ref[0:2, 0]


def tile_transpose(p, t):
    ax = t.ndim - 2
    s, g = iota(t.shape, ax), iota(t.shape, ax + 1) >> log2(p.half)
    for b in (1, 2, 4):
        w = b * p.half
        up = pltpu.roll(pltpu.roll(t, 8 - b, ax), w, ax + 1)
        dn = up if b == 4 else pltpu.roll(pltpu.roll(t, b, ax), 128 - w, ax + 1)
        sb, gb = (s & b) != 0, (g & b) != 0
        t = jnp.where(sb == gb, t, jnp.where(gb, up, dn))
    return t


def blocks_to_grid(p, blk):
    rows = []
    for yh in range(p.half // 8):
        rows.append(
            jnp.concatenate(
                [
                    tile_transpose(p, blk[8 * c : 8 * c + 8, 128 * yh : 128 * yh + 128])
                    for c in range(p.bcols // 8)
                ],
                axis=1,
            )
        )
    return jnp.concatenate(rows, axis=0)


def grid_to_blocks(p, grid):
    rows = []
    for c in range(p.bcols // 8):
        rows.append(
            jnp.concatenate(
                [
                    tile_transpose(p, grid[8 * yh : 8 * yh + 8, 128 * c : 128 * c + 128])
                    for yh in range(p.half // 8)
                ],
                axis=1,
            )
        )
    return jnp.concatenate(rows, axis=0)


def x_next(f):
    return pltpu.roll(f, f.shape[1] - 1, 1)


def x_prev(f):
    return pltpu.roll(f, 1, 1)


def y_next(f, halo):
    return jnp.where(iota(f.shape, 0) == f.shape[0] - 1, halo, pltpu.roll(f, f.shape[0] - 1, 0))


def y_prev(f, halo):
    return jnp.where(iota(f.shape, 0) == 0, halo, pltpu.roll(f, 1, 0))


def row_of(p, ref, src, at):
    return jnp.concatenate([ref[src, pl.ds(at + h, 1), :] for h in range(p.wrap)], axis=1)


def interior_kernel(p, b_ref, t_ref, copy_ref, j_ref, next_ref, g3_ref):
    s, k = p.slots, p.k
    _, q_s = send_positions(p, t_ref[...])
    r_l, c_l, j_l = lane_route(p)
    shape = (p.cz, s, p.rows)
    g3 = (iota(shape, 0) == c_l.reshape(1, 1, p.rows)) & (
        q_s.reshape(1, s, 1) == (r_l * k + j_l).astype(F32).reshape(1, 1, p.rows)
    )
    g3_ref[...] = one_hot(g3).reshape(p.cz * s, p.rows)
    zero = jnp.zeros((p.ny, p.nx), F32)
    for z in range(p.zc):
        b = [b_ref[c, z] for c in range(3)]
        below = [b_ref[c, z - 1] if z > 0 else zero for c in range(3)]
        above = [b_ref[c, z + 1] if z < p.zc - 1 else zero for c in range(3)]
        south, north = [y_prev(f, 0.0) for f in b], [y_next(f, 0.0) for f in b]
        west, east = [x_prev(f) for f in b], [x_next(f) for f in b]
        j_ref[0, z] = ((north[2] - south[2]) - (above[1] - below[1])) * 0.5
        j_ref[1, z] = ((above[0] - below[0]) - (east[2] - west[2])) * 0.5
        j_ref[2, z] = ((east[1] - west[1]) - (north[0] - south[0])) * 0.5
        for c in range(3):
            lap = below[c] + above[c] + south[c] + north[c] + west[c] + east[c] - 6.0 * b[c]
            next_ref[c, z] = b[c] + 0.05 * lap
            copy_ref[c, z] = b[c]


def edge_rows(p, ref, nxt, prv, at):
    y = iota((p.ny, p.nx), 0)
    north = jnp.where(y == p.ny - 1, row_of(p, ref, nxt, at), 0.0)
    return north, jnp.where(y == 0, row_of(p, ref, prv, at), 0.0)


def field_kernel(p, r_ref, b_ref, j_ref, lo_ref, hi_ref, out_ref, e_ref, up_ref, down_ref, e_rows):
    n, k, zc = p.n, p.k, p.zc
    me = lax.axis_index("xy")
    nxt, prv = lax.rem(me + 1, n), lax.rem(me + n - 1, n)
    cols = r_ref[:, p.ru + p.rb, :]
    r_l, c_l, _ = lane_route(p)
    shape = (n, p.rows)
    col_l = jnp.sum(jnp.where(iota(shape, 0) == r_l, cols[:, : p.rows], 0.0), axis=0, keepdims=True)
    shape = (p.cz, p.bcols, p.rows)
    g2 = one_hot(
        (iota(shape, 0) == c_l.reshape(1, 1, p.rows))
        & (iota(shape, 1).astype(F32) == col_l.reshape(1, 1, p.rows))
    ).reshape(p.cz * p.bcols, p.rows)
    shape = (n, p.ru, 128)
    col_s = jnp.sum(
        jnp.where((iota(shape, 1) & (k - 1)) == iota(shape, 2), cols[:, None, :128], 0.0), axis=2, keepdims=True
    )
    lanes = p.cz * p.bcols
    shape = (n, p.ru, lanes)
    lane = iota(shape, 2)
    g2t = one_hot(
        ((iota(shape, 1) >> log2(k)) == (lane >> log2(p.bcols)))
        & (col_s == (lane & (p.bcols - 1)).astype(F32))
    ).reshape(p.rows, lanes)
    hi, lo = split(r_ref[:, : p.ru, :].reshape(p.rows, p.area))
    u_blk = dot(g2, hi) + dot(g2, lo)
    u = [
        [blocks_to_grid(p, u_blk[(c * zc + z) * p.bcols : (c * zc + z + 1) * p.bcols]) for z in range(zc)]
        for c in range(3)
    ]
    b = [[b_ref[c, z] for z in range(zc)] for c in range(3)]
    force = []
    zero = jnp.zeros((p.ny, p.nx), F32)
    for z in range(zc):
        bz = [b[c][z] for c in range(3)]
        dy = {}
        for c in (0, 2):
            north, south = edge_rows(p, r_ref, nxt, prv, p.ru + (c * zc + z) * p.wrap)
            dy[c] = north - south
        dz = [zero, zero]
        for c in range(2):
            if z == zc - 1:
                dz[c] = dz[c] + hi_ref[c]
            if z == 0:
                dz[c] = dz[c] - lo_ref[c]
        j0 = j_ref[0, z] + (dy[2] - dz[1]) * 0.5
        j1 = j_ref[1, z] + dz[0] * 0.5
        j2 = j_ref[2, z] - dy[0] * 0.5
        force.append([j1 * bz[2] - j2 * bz[1], j2 * bz[0] - j0 * bz[2], j0 * bz[1] - j1 * bz[0]])
    f_blk = jnp.concatenate([grid_to_blocks(p, force[z][c]) for c in range(3) for z in range(zc)], axis=0)
    hi, lo = split(f_blk)
    out_ref[:, : p.ru, :] = (dot(g2t, hi) + dot(g2t, lo)).reshape(n, p.ru, p.area)
    for z in range(zc):
        uz, bz = [u[c][z] for c in range(3)], [b[c][z] for c in range(3)]
        ez = [uz[1] * bz[2] - uz[2] * bz[1], uz[2] * bz[0] - uz[0] * bz[2], uz[0] * bz[1] - uz[1] * bz[0]]
        for c in range(3):
            e_ref[c, z] = ez[c]
        if z == zc - 1:
            up_ref[0], up_ref[1], up_ref[2] = ez[0], ez[1], bz[2]
        if z == 0:
            down_ref[0], down_ref[1], down_ref[2] = ez[0], ez[1], bz[2]
        for i, c in enumerate((0, 2)):
            for h in range(p.wrap):
                at = (i * zc + z) * p.wrap + h
                w = slice(h * p.area, (h + 1) * p.area)
                e_rows[0, at : at + 1, :] = ez[c][0:1, w]
                e_rows[1, at : at + 1, :] = ez[c][p.ny - 1 : p.ny, w]
    for r in range(n):
        out_ref[r, p.ru : p.ru + p.re, :] = jnp.where(r == nxt, e_rows[1], e_rows[0])


def local_kernel(p, r_ref, b_ref, lo_ref, hi_ref, e_ref, next_ref):
    n, zc = p.n, p.zc
    me = lax.axis_index("xy")
    nxt, prv = lax.rem(me + 1, n), lax.rem(me + n - 1, n)
    zero = jnp.zeros((p.ny, p.nx), F32)
    for z in range(zc):
        e = [e_ref[c, z] for c in range(3)]
        above = [e_ref[c, z + 1] if z < zc - 1 else zero for c in range(2)]
        below = [e_ref[c, z - 1] if z > 0 else zero for c in range(2)]
        curl = [
            (y_next(e[2], 0.0) - y_prev(e[2], 0.0)) - (above[1] - below[1]),
            (above[0] - below[0]) - (x_next(e[2]) - x_prev(e[2])),
            (x_next(e[1]) - x_prev(e[1])) - (y_next(e[0], 0.0) - y_prev(e[0], 0.0)),
        ]
        for c in range(3):
            north, south = edge_rows(p, r_ref, nxt, prv, p.ru + (c * zc + z) * p.wrap)
            total = curl[c] + north + south
            if c < 2 and z == 0:
                total = total + lo_ref[c]
            if c < 2 and z == zc - 1:
                total = total + hi_ref[c]
            next_ref[c, z] = b_ref[c, z] + 0.05 * total


def finish_kernel(p, r_ref, g_ref, v_ref, n_ref, lo_ref, hi_ref, vel_hbm, mag_hbm, vel, mag, sems):
    n, zc = p.n, p.zc
    half_fine = p.edge * p.edge // 2
    half_area = p.area // 2
    ex = log2(p.edge)
    c, f = iota((half_area, half_fine), 0), iota((half_area, half_fine), 1)
    coarse = ((f >> (ex + 1)) << (ex - 1)) + ((f & (p.edge - 1)) >> 1)
    sel = one_hot(coarse == c)
    hi, lo = split(r_ref[:, : p.ru, :].reshape(p.rows, p.area) * 0.1)
    g = g_ref[...]
    sel = jnp.concatenate([sel, sel], axis=0)
    hi, lo = dot(g, hi).astype(BF16), dot(g, lo).astype(BF16)
    ws = [slice(h * half_area, (h + 1) * half_area) for h in range(2)]
    pairs = [jnp.concatenate([hi[:, w], lo[:, w]], axis=1) for w in ws]
    s = p.slots
    m = zc * s
    copies = []
    for c in range(3):
        at = slice(c * m, (c + 1) * m)
        add = dot(jnp.concatenate([x[at] for x in pairs], axis=0), sel)
        for z in range(zc):
            for h in range(2):
                fw = slice(h * half_fine, (h + 1) * half_fine)
                part = add[h * m + z * s : h * m + (z + 1) * s]
                for d in range(2):
                    vel[c, 2 * z + d, :, fw] = v_ref[c, 2 * z + d, :, fw] + part
        copies.append(pltpu.make_async_copy(vel.at[c], vel_hbm.at[c], sems.at[c]))
        copies[-1].start()
    me = lax.axis_index("xy")
    nxt, prv = lax.rem(me + 1, n), lax.rem(me + n - 1, n)

    def dy(i, z):
        north, south = edge_rows(p, r_ref, nxt, prv, p.ru + (i * zc + z) * p.wrap)
        return north - south

    for z in range(zc):
        dz = [jnp.zeros((p.ny, p.nx), F32)] * 2
        outer = dz[0]
        if z == zc - 1:
            dz = [dz[c] + hi_ref[c] for c in range(2)]
            outer = outer + hi_ref[2]
        if z == 0:
            dz = [dz[c] - lo_ref[c] for c in range(2)]
            outer = outer + lo_ref[2]
        mag[0, z] = n_ref[0, z] + 0.05 * (dy(1, z) - dz[1])
        mag[1, z] = n_ref[1, z] + 0.05 * dz[0]
        mag[2, z] = n_ref[2, z] + 0.05 * (outer - dy(0, z))
    copies.append(pltpu.make_async_copy(mag, mag_hbm, sems.at[3]))
    copies[-1].start()
    for copy in copies:
        copy.wait()


def struct(*shape, dtype=F32):
    return jax.ShapeDtypeStruct(shape, dtype)


def call(kernel, ins, outs, scratch=(), grant=20 << 20):
    return pl.pallas_call(
        kernel,
        out_shape=[o for o, _ in outs],
        in_specs=ins,
        out_specs=[spec for _, spec in outs],
        scratch_shapes=list(scratch),
        cost_estimate=pl.CostEstimate(flops=1 << 24, bytes_accessed=1 << 20, transcendentals=0),
        compiler_params=pltpu.CompilerParams(vmem_limit_bytes=grant),
    )


def ring(axis, step):
    n = lax.axis_size(axis)
    return [(i, (i + step) % n) for i in range(n)]


def planes(up, down):
    below = lax.ppermute(up, "gz", ring("gz", 1))
    above = lax.ppermute(down, "gz", ring("gz", -1))
    return below, above


def body(velocity, magnetic, slot_block_table):
    p = Plan(velocity.shape, magnetic.shape, lax.axis_size("xy"))
    plane = (p.ny, p.nx)
    dma = pltpu.SemaphoreType.DMA
    table = slot_block_table.reshape(1, p.slots)
    sent, up, down = call(
        functools.partial(restrict_kernel, p),
        [HBM] * 3,
        [
            (struct(p.n, p.r1, p.area), VMEM),
            (struct(2, *plane), VMEM),
            (struct(2, *plane), VMEM),
        ],
        [
            pltpu.VMEM(velocity.shape, F32),
            pltpu.VMEM((1, p.slots), jnp.int32),
            pltpu.VMEM(magnetic.shape, F32),
            pltpu.VMEM((-(-p.rb // 8) * 8, p.area), F32),
            pltpu.VMEM((-(-p.rb // 8) * 8, p.area), F32),
            dma((5,)),
        ],
        ALL_VMEM,
    )(velocity, table, magnetic)
    got = lax.all_to_all(sent, "xy", 0, 0, tiled=True)
    below, above = planes(up, down)
    held, held_table, _ = lax.optimization_barrier((magnetic, table, up))
    field, current, diffused, g3 = call(
        functools.partial(interior_kernel, p),
        [VMEM] * 2,
        [(struct(*magnetic.shape), VMEM)] * 3 + [(struct(p.cz * p.slots, p.rows, dtype=BF16), VMEM)],
    )(held, held_table)
    sent, emf, up, down = call(
        functools.partial(field_kernel, p),
        [VMEM] * 5,
        [
            (struct(p.n, p.r2, p.area), VMEM),
            (struct(*magnetic.shape), VMEM),
            (struct(3, *plane), VMEM),
            (struct(3, *plane), VMEM),
        ],
        [pltpu.VMEM((2, p.re, p.area), F32)],
    )(got, field, current, below, above)
    got_force = lax.all_to_all(sent, "xy", 0, 0, tiled=True)
    emf_below, emf_above = planes(up, down)
    (partial,) = call(
        functools.partial(local_kernel, p), [VMEM] * 5, [(struct(*magnetic.shape), VMEM)]
    )(got, diffused, below, above, emf)
    return tuple(
        call(
            functools.partial(finish_kernel, p),
            [VMEM] * 6,
            [(struct(*velocity.shape), HBM), (struct(*magnetic.shape), HBM)],
            [pltpu.VMEM(velocity.shape, F32), pltpu.VMEM(magnetic.shape, F32), dma((4,))],
        )(got_force, g3, velocity, partial, emf_below, emf_above)
    )


def solution(mesh):
    return jax.shard_map(
        body,
        mesh=mesh,
        in_specs=(P(None, "gz", "xy", None), P(None, "gz", "xy", None), P("xy")),
        out_specs=(P(None, "gz", "xy", None), P(None, "gz", "xy", None)),
        check_vma=False,
    )
```

```python
import functools
import math

import jax
import jax.numpy as jnp
from jax import lax
from jax.experimental import pallas as pl
from jax.experimental.pallas import tpu as pltpu
from jax.sharding import PartitionSpec as P

F32, BF16 = jnp.float32, jnp.bfloat16
VMEM = pl.BlockSpec(memory_space=pltpu.VMEM)
ALL_VMEM = 67043328
HBM = pl.BlockSpec(memory_space=pltpu.HBM)


def split(x):
    hi = x.astype(BF16)
    return hi, (x - hi.astype(F32)).astype(BF16)


def dot(a, b):
    return jnp.dot(a, b, preferred_element_type=F32)


def iota(shape, dim):
    return lax.broadcasted_iota(jnp.int32, shape, dim)


def one_hot(mask):
    return jnp.where(mask, 1.0, 0.0).astype(BF16)


def log2(x):
    assert x == 1 << (x.bit_length() - 1)
    return x.bit_length() - 1


class Plan:
    def __init__(self, vshape, bshape, n):
        self.n = n
        self.slots = vshape[2]
        self.k = self.slots // n
        self.zc = bshape[1]
        self.ny, self.nx = bshape[2:]
        self.edge = math.isqrt(vshape[3])
        self.half = self.edge // 2
        self.area = self.half * self.half
        self.bcols = self.nx // self.half
        self.rc = -(-self.zc * self.k // 8) * 8
        self.ru = 3 * self.rc
        self.rows = n * self.rc
        self.rb = 3 * self.zc * self.nx // self.area
        self.r1 = -(-(self.ru + self.rb + 1) // 8) * 8
        self.re = 2 * self.zc * self.nx // self.area
        self.r2 = -(-(self.ru + self.re) // 8) * 8
        self.wrap = self.nx // self.area


def send_positions(p, table):
    s = p.slots
    row = jnp.broadcast_to((table >> log2(p.bcols)).astype(F32), (s, s))
    i, j = iota((s, s), 0), iota((s, s), 1)
    row_s = jnp.sum(jnp.where(i == j, row, 0.0), axis=1, keepdims=True)
    rank = jnp.sum(jnp.where((row_s == row) & (i < j), 1.0, 0.0), axis=0, keepdims=True)
    q = row[0:1] * p.k + rank
    q_s = jnp.sum(jnp.where(i == j, jnp.broadcast_to(q, (s, s)), 0.0), axis=1, keepdims=True)
    return q, q_s


def select(g, x):
    hi, lo = split(x)
    out = dot(g, jnp.concatenate([hi, lo], axis=1))
    return out[:, : x.shape[1]] + out[:, x.shape[1] :]


def lane_route(p):
    lane = iota((1, 1, p.rows), 2)
    i = lane & (p.rc - 1)
    return lane >> log2(p.rc), i >> log2(p.k), i & (p.k - 1)


def restrict_kernel(p, v_hbm, t_hbm, b_hbm, out_hbm, up_hbm, down_hbm, v_ref, t_ref, b_ref, out, last, first, sems):
    n, k, s, zc = p.n, p.k, p.slots, p.zc
    me = lax.axis_index("xy")
    t_copy = pltpu.make_async_copy(t_hbm, t_ref, sems.at[0])
    b_copy = pltpu.make_async_copy(b_hbm, b_ref, sems.at[1])
    v_copies = [pltpu.make_async_copy(v_hbm.at[c], v_ref.at[c], sems.at[2 + c]) for c in range(3)]
    t_copy.start()
    b_copy.start()
    for copy in v_copies:
        copy.start()
    half_fine = p.edge * p.edge // 2
    half_area = p.area // 2
    f, c = iota((half_fine, half_area), 0), iota((half_fine, half_area), 1)
    e = log2(p.edge)
    coarse = ((f >> (e + 1)) << (e - 1)) + ((f & (p.edge - 1)) >> 1)
    sel = one_hot(coarse == c)
    t_copy.wait()
    table = t_ref[...]
    q, _ = send_positions(p, table)
    lanes = zc * s
    rep = one_hot((iota((s, lanes), 1) & (s - 1)) == iota((s, lanes), 0))
    qt = dot(jnp.broadcast_to(q, (8, s)).astype(BF16), rep)[0:1]
    shape = (n, p.rc, lanes)
    i = iota(shape, 1)
    target = (iota(shape, 0) * k + (i & (k - 1))).astype(F32)
    g = one_hot(((i >> log2(k)) == (iota(shape, 2) >> log2(s))) & (target == qt.reshape(1, 1, lanes)))
    g = g.reshape(p.rows, lanes)
    col = jnp.broadcast_to((table & (p.bcols - 1)).astype(F32), (s, s))
    qi = iota((s, s), 0).astype(F32)
    col_q = jnp.sum(jnp.where(qi == jnp.broadcast_to(q, (s, s)), col, 0.0), axis=1, keepdims=True)
    qa, la = iota((s, p.area), 0), iota((s, p.area), 1)
    spread = jnp.where((qa & (k - 1)) == (la & (k - 1)), col_q, 0.0).astype(BF16)
    gather = one_hot((iota((n, s), 1) >> log2(k)) == iota((n, s), 0))
    cols = dot(gather, spread)
    at = p.ru + p.rb
    for r in range(n):
        out[r, at : at + 1, :] = cols[r : r + 1]
    b_copy.wait()
    sends = [
        pltpu.make_async_copy(b_ref.at[0:2, zc - 1], up_hbm, sems.at[5]),
        pltpu.make_async_copy(b_ref.at[0:2, 0], down_hbm, sems.at[6]),
    ]
    for c in range(3):
        for z in range(zc):
            for h in range(p.wrap):
                at = (c * zc + z) * p.wrap + h
                w = slice(h * p.area, (h + 1) * p.area)
                last[at : at + 1, :] = b_ref[c, z, p.ny - 1 : p.ny, w]
                first[at : at + 1, :] = b_ref[c, z, 0:1, w]
    nxt = lax.rem(me + 1, n)
    for r in range(n):
        out[r, p.ru : p.ru + p.rb, :] = jnp.where(r == nxt, last[: p.rb], first[: p.rb])
    tail = pl.ds(p.ru, p.r1 - p.ru)
    sends.append(pltpu.make_async_copy(out.at[:, tail, :], out_hbm.at[:, tail, :], sems.at[7]))
    for send in sends:
        send.start()
    m = zc * s
    ws = [slice(h * half_fine, (h + 1) * half_fine) for h in range(2)]
    for c in range(3):
        v_copies[c].wait()
        z_sum = jnp.concatenate([v_ref[c, 2 * z] + v_ref[c, 2 * z + 1] for z in range(zc)], axis=0)
        hi, lo = split(z_sum)
        o = dot(jnp.concatenate([x[:, w] for w in ws for x in (hi, lo)], axis=0), sel)
        u = [o[2 * h * m : (2 * h + 1) * m] + o[(2 * h + 1) * m : (2 * h + 2) * m] for h in range(2)]
        u = jnp.concatenate(u, axis=1) * 0.125
        out[:, c * p.rc : (c + 1) * p.rc, :] = select(g, u).reshape(n, p.rc, p.area)
        rows = pl.ds(c * p.rc, p.rc)
        sends.append(pltpu.make_async_copy(out.at[:, rows, :], out_hbm.at[:, rows, :], sems.at[8 + c]))
        sends[-1].start()
    for send in sends:
        send.wait()


def tile_transpose(p, t):
    ax = t.ndim - 2
    s, g = iota(t.shape, ax), iota(t.shape, ax + 1) >> log2(p.half)
    for b in (1, 2, 4):
        w = b * p.half
        up = pltpu.roll(pltpu.roll(t, 8 - b, ax), w, ax + 1)
        dn = up if b == 4 else pltpu.roll(pltpu.roll(t, b, ax), 128 - w, ax + 1)
        sb, gb = (s & b) != 0, (g & b) != 0
        t = jnp.where(sb == gb, t, jnp.where(gb, up, dn))
    return t


def blocks_to_grid(p, blk):
    rows = []
    for yh in range(p.half // 8):
        rows.append(
            jnp.concatenate(
                [
                    tile_transpose(p, blk[8 * c : 8 * c + 8, 128 * yh : 128 * yh + 128])
                    for c in range(p.bcols // 8)
                ],
                axis=1,
            )
        )
    return jnp.concatenate(rows, axis=0)


def grid_to_blocks(p, grid):
    rows = []
    for c in range(p.bcols // 8):
        rows.append(
            jnp.concatenate(
                [
                    tile_transpose(p, grid[8 * yh : 8 * yh + 8, 128 * c : 128 * c + 128])
                    for yh in range(p.half // 8)
                ],
                axis=1,
            )
        )
    return jnp.concatenate(rows, axis=0)


def x_next(f):
    return pltpu.roll(f, f.shape[1] - 1, 1)


def x_prev(f):
    return pltpu.roll(f, 1, 1)


def y_next(f, halo):
    return jnp.where(iota(f.shape, 0) == f.shape[0] - 1, halo, pltpu.roll(f, f.shape[0] - 1, 0))


def y_prev(f, halo):
    return jnp.where(iota(f.shape, 0) == 0, halo, pltpu.roll(f, 1, 0))


def row_of(p, ref, src, at):
    return jnp.concatenate([ref[src, pl.ds(at + h, 1), :] for h in range(p.wrap)], axis=1)


def interior_kernel(p, b_ref, t_ref, copy_ref, j_ref, next_ref, g3_ref):
    s, k = p.slots, p.k
    _, q_s = send_positions(p, t_ref[...])
    r_l, z_l, j_l = lane_route(p)
    shape = (p.zc, s, p.rows)
    g3 = (iota(shape, 0) == z_l) & (q_s.reshape(1, s, 1) == (r_l * k + j_l).astype(F32))
    g3_ref[...] = one_hot(g3).reshape(p.zc * s, p.rows)
    zero = jnp.zeros((p.ny, p.nx), F32)
    for z in range(p.zc):
        b = [b_ref[c, z] for c in range(3)]
        below = [b_ref[c, z - 1] if z > 0 else zero for c in range(3)]
        above = [b_ref[c, z + 1] if z < p.zc - 1 else zero for c in range(3)]
        south, north = [y_prev(f, 0.0) for f in b], [y_next(f, 0.0) for f in b]
        west, east = [x_prev(f) for f in b], [x_next(f) for f in b]
        j_ref[0, z] = ((north[2] - south[2]) - (above[1] - below[1])) * 0.5
        j_ref[1, z] = ((above[0] - below[0]) - (east[2] - west[2])) * 0.5
        j_ref[2, z] = ((east[1] - west[1]) - (north[0] - south[0])) * 0.5
        for c in range(3):
            lap = below[c] + above[c] + south[c] + north[c] + west[c] + east[c] - 6.0 * b[c]
            next_ref[c, z] = b[c] + 0.05 * lap
            copy_ref[c, z] = b[c]


def edge_rows(p, ref, nxt, prv, at):
    y = iota((p.ny, p.nx), 0)
    north = jnp.where(y == p.ny - 1, row_of(p, ref, nxt, at), 0.0)
    return north, jnp.where(y == 0, row_of(p, ref, prv, at), 0.0)


def field_kernel(p, r_ref, b_ref, j_ref, lo_ref, hi_ref, out_hbm, e_ref, up_ref, down_ref, out, e_rows, sems):
    n, k, zc = p.n, p.k, p.zc
    me = lax.axis_index("xy")
    nxt, prv = lax.rem(me + 1, n), lax.rem(me + n - 1, n)
    b = [[b_ref[c, z] for z in range(zc)] for c in range(3)]
    cols = r_ref[:, p.ru + p.rb, :]
    shape = (n, p.rc, 128)
    col_s = jnp.sum(
        jnp.where((iota(shape, 1) & (k - 1)) == iota(shape, 2), cols[:, None, :128], 0.0), axis=2, keepdims=True
    )
    shape = (n, p.rc, zc * p.bcols)
    lane = iota(shape, 2)
    g = one_hot(
        ((iota(shape, 1) >> log2(k)) == (lane >> log2(p.bcols)))
        & (col_s == (lane & (p.bcols - 1)).astype(F32))
    ).reshape(p.rows, zc * p.bcols)
    force = []
    zero = jnp.zeros((p.ny, p.nx), F32)
    for z in range(zc):
        bz = [b[c][z] for c in range(3)]
        dy = {}
        for c in (0, 2):
            north, south = edge_rows(p, r_ref, nxt, prv, p.ru + (c * zc + z) * p.wrap)
            dy[c] = north - south
        dz = [zero, zero]
        for c in range(2):
            if z == zc - 1:
                dz[c] = dz[c] + hi_ref[c]
            if z == 0:
                dz[c] = dz[c] - lo_ref[c]
        j0 = j_ref[0, z] + (dy[2] - dz[1]) * 0.5
        j1 = j_ref[1, z] + dz[0] * 0.5
        j2 = j_ref[2, z] - dy[0] * 0.5
        force.append([j1 * bz[2] - j2 * bz[1], j2 * bz[0] - j0 * bz[2], j0 * bz[1] - j1 * bz[0]])
    sends = []
    for c in range(3):
        f_blk = jnp.concatenate([grid_to_blocks(p, force[z][c]) for z in range(zc)], axis=0)
        out[:, c * p.rc : (c + 1) * p.rc, :] = select(g, f_blk).reshape(n, p.rc, p.area)
        rows = pl.ds(c * p.rc, p.rc)
        sends.append(pltpu.make_async_copy(out.at[:, rows, :], out_hbm.at[:, rows, :], sems.at[c]))
        sends[-1].start()
    p_l, z_l, _ = lane_route(p)
    shape = (n, p.rows)
    col_l = jnp.sum(
        jnp.where(iota(shape, 0) == p_l.reshape(1, p.rows), cols[:, : p.rows], 0.0), axis=0, keepdims=True
    )
    shape = (zc, p.bcols, p.rows)
    g = one_hot(
        (iota(shape, 0) == z_l) & (iota(shape, 1).astype(F32) == col_l.reshape(1, 1, p.rows))
    ).reshape(zc * p.bcols, p.rows)
    u = []
    for c in range(3):
        blk = select(g, r_ref[:, c * p.rc : (c + 1) * p.rc, :].reshape(p.rows, p.area))
        u.append([blocks_to_grid(p, blk[z * p.bcols : (z + 1) * p.bcols]) for z in range(zc)])
    for z in range(zc):
        uz, bz = [u[c][z] for c in range(3)], [b[c][z] for c in range(3)]
        ez = [uz[1] * bz[2] - uz[2] * bz[1], uz[2] * bz[0] - uz[0] * bz[2], uz[0] * bz[1] - uz[1] * bz[0]]
        for c in range(3):
            e_ref[c, z] = ez[c]
        if z == zc - 1:
            up_ref[0], up_ref[1], up_ref[2] = ez[0], ez[1], bz[2]
        if z == 0:
            down_ref[0], down_ref[1], down_ref[2] = ez[0], ez[1], bz[2]
        for i, c in enumerate((0, 2)):
            for h in range(p.wrap):
                at = (i * zc + z) * p.wrap + h
                w = slice(h * p.area, (h + 1) * p.area)
                e_rows[0, at : at + 1, :] = ez[c][0:1, w]
                e_rows[1, at : at + 1, :] = ez[c][p.ny - 1 : p.ny, w]
    for r in range(n):
        out[r, p.ru : p.ru + p.re, :] = jnp.where(r == nxt, e_rows[1], e_rows[0])
    rows = pl.ds(p.ru, p.r2 - p.ru)
    sends.append(pltpu.make_async_copy(out.at[:, rows, :], out_hbm.at[:, rows, :], sems.at[3]))
    sends[-1].start()
    for send in sends:
        send.wait()


def local_kernel(p, r_ref, b_ref, lo_ref, hi_ref, e_ref, next_ref):
    n, zc = p.n, p.zc
    me = lax.axis_index("xy")
    nxt, prv = lax.rem(me + 1, n), lax.rem(me + n - 1, n)
    zero = jnp.zeros((p.ny, p.nx), F32)
    for z in range(zc):
        e = [e_ref[c, z] for c in range(3)]
        above = [e_ref[c, z + 1] if z < zc - 1 else zero for c in range(2)]
        below = [e_ref[c, z - 1] if z > 0 else zero for c in range(2)]
        curl = [
            (y_next(e[2], 0.0) - y_prev(e[2], 0.0)) - (above[1] - below[1]),
            (above[0] - below[0]) - (x_next(e[2]) - x_prev(e[2])),
            (x_next(e[1]) - x_prev(e[1])) - (y_next(e[0], 0.0) - y_prev(e[0], 0.0)),
        ]
        for c in range(3):
            north, south = edge_rows(p, r_ref, nxt, prv, p.ru + (c * zc + z) * p.wrap)
            total = curl[c] + north + south
            if c < 2 and z == 0:
                total = total + lo_ref[c]
            if c < 2 and z == zc - 1:
                total = total + hi_ref[c]
            next_ref[c, z] = b_ref[c, z] + 0.05 * total


def finish_kernel(p, r_ref, g_ref, v_ref, n_ref, lo_ref, hi_ref, vel_hbm, mag_hbm, vel, mag, sems):
    n, zc = p.n, p.zc
    half_fine = p.edge * p.edge // 2
    half_area = p.area // 2
    ex = log2(p.edge)
    c, f = iota((half_area, half_fine), 0), iota((half_area, half_fine), 1)
    coarse = ((f >> (ex + 1)) << (ex - 1)) + ((f & (p.edge - 1)) >> 1)
    sel = one_hot(coarse == c)
    sel = jnp.concatenate([sel, sel], axis=0)
    g = g_ref[...]
    ws = [slice(h * half_area, (h + 1) * half_area) for h in range(2)]
    s = p.slots
    m = zc * s
    copies = []
    for c in range(3):
        hi, lo = split(r_ref[:, c * p.rc : (c + 1) * p.rc, :].reshape(p.rows, p.area) * 0.1)
        parts = dot(g, jnp.concatenate([hi, lo], axis=1)).astype(BF16)
        hi, lo = parts[:, : p.area], parts[:, p.area :]
        pairs = [jnp.concatenate([hi[:, w], lo[:, w]], axis=1) for w in ws]
        add = dot(jnp.concatenate(pairs, axis=0), sel)
        for z in range(zc):
            for h in range(2):
                fw = slice(h * half_fine, (h + 1) * half_fine)
                part = add[h * m + z * s : h * m + (z + 1) * s]
                for d in range(2):
                    vel[c, 2 * z + d, :, fw] = v_ref[c, 2 * z + d, :, fw] + part
        copies.append(pltpu.make_async_copy(vel.at[c], vel_hbm.at[c], sems.at[c]))
        copies[-1].start()
    me = lax.axis_index("xy")
    nxt, prv = lax.rem(me + 1, n), lax.rem(me + n - 1, n)

    def dy(i, z):
        north, south = edge_rows(p, r_ref, nxt, prv, p.ru + (i * zc + z) * p.wrap)
        return north - south

    for z in range(zc):
        dz = [jnp.zeros((p.ny, p.nx), F32)] * 2
        outer = dz[0]
        if z == zc - 1:
            dz = [dz[c] + hi_ref[c] for c in range(2)]
            outer = outer + hi_ref[2]
        if z == 0:
            dz = [dz[c] - lo_ref[c] for c in range(2)]
            outer = outer + lo_ref[2]
        mag[0, z] = n_ref[0, z] + 0.05 * (dy(1, z) - dz[1])
        mag[1, z] = n_ref[1, z] + 0.05 * dz[0]
        mag[2, z] = n_ref[2, z] + 0.05 * (outer - dy(0, z))
    copies.append(pltpu.make_async_copy(mag, mag_hbm, sems.at[3]))
    copies[-1].start()
    for copy in copies:
        copy.wait()


def struct(*shape, dtype=F32):
    return jax.ShapeDtypeStruct(shape, dtype)


def call(kernel, ins, outs, scratch=(), grant=20 << 20):
    return pl.pallas_call(
        kernel,
        out_shape=[o for o, _ in outs],
        in_specs=ins,
        out_specs=[spec for _, spec in outs],
        scratch_shapes=list(scratch),
        cost_estimate=pl.CostEstimate(flops=1 << 24, bytes_accessed=1 << 20, transcendentals=0),
        compiler_params=pltpu.CompilerParams(vmem_limit_bytes=grant),
    )


def ring(axis, step):
    n = lax.axis_size(axis)
    return [(i, (i + step) % n) for i in range(n)]


def planes(up, down):
    below = lax.ppermute(up, "gz", ring("gz", 1))
    above = lax.ppermute(down, "gz", ring("gz", -1))
    return below, above


def body(velocity, magnetic, slot_block_table):
    p = Plan(velocity.shape, magnetic.shape, lax.axis_size("xy"))
    plane = (p.ny, p.nx)
    dma = pltpu.SemaphoreType.DMA
    table = slot_block_table.reshape(1, p.slots)
    sent, up, down = call(
        functools.partial(restrict_kernel, p),
        [HBM] * 3,
        [(struct(p.n, p.r1, p.area), HBM), (struct(2, *plane), HBM), (struct(2, *plane), HBM)],
        [
            pltpu.VMEM(velocity.shape, F32),
            pltpu.VMEM((1, p.slots), jnp.int32),
            pltpu.VMEM(magnetic.shape, F32),
            pltpu.VMEM((p.n, p.r1, p.area), F32),
            pltpu.VMEM((-(-p.rb // 8) * 8, p.area), F32),
            pltpu.VMEM((-(-p.rb // 8) * 8, p.area), F32),
            dma((11,)),
        ],
        ALL_VMEM,
    )(velocity, table, magnetic)
    got = lax.all_to_all(sent, "xy", 0, 0, tiled=True)
    below, above = planes(up, down)
    held, held_table, _ = lax.optimization_barrier((magnetic, table, up))
    field, current, diffused, g3 = call(
        functools.partial(interior_kernel, p),
        [VMEM] * 2,
        [(struct(*magnetic.shape), VMEM)] * 3 + [(struct(p.zc * p.slots, p.rows, dtype=BF16), VMEM)],
    )(held, held_table)
    sent, emf, up, down = call(
        functools.partial(field_kernel, p),
        [VMEM] * 5,
        [
            (struct(p.n, p.r2, p.area), HBM),
            (struct(*magnetic.shape), VMEM),
            (struct(3, *plane), VMEM),
            (struct(3, *plane), VMEM),
        ],
        [pltpu.VMEM((p.n, p.r2, p.area), F32), pltpu.VMEM((2, p.re, p.area), F32), dma((4,))],
    )(got, field, current, below, above)
    got_force = lax.all_to_all(sent, "xy", 0, 0, tiled=True)
    emf_below, emf_above = planes(up, down)
    (partial,) = call(
        functools.partial(local_kernel, p), [VMEM] * 5, [(struct(*magnetic.shape), VMEM)]
    )(got, diffused, below, above, emf)
    return tuple(
        call(
            functools.partial(finish_kernel, p),
            [VMEM] * 6,
            [(struct(*velocity.shape), HBM), (struct(*magnetic.shape), HBM)],
            [pltpu.VMEM(velocity.shape, F32), pltpu.VMEM(magnetic.shape, F32), dma((4,))],
        )(got_force, g3, velocity, partial, emf_below, emf_above)
    )


def solution(mesh):
    return jax.shard_map(
        body,
        mesh=mesh,
        in_specs=(P(None, "gz", "xy", None), P(None, "gz", "xy", None), P("xy")),
        out_specs=(P(None, "gz", "xy", None), P(None, "gz", "xy", None)),
        check_vma=False,
    )
```

```python
import functools
import math

import jax
import jax.numpy as jnp
from jax import lax
from jax.experimental import pallas as pl
from jax.experimental.pallas import tpu as pltpu
from jax.sharding import PartitionSpec as P

F32, BF16 = jnp.float32, jnp.bfloat16
VMEM = pl.BlockSpec(memory_space=pltpu.VMEM)
ALL_VMEM = 67043328
HBM = pl.BlockSpec(memory_space=pltpu.HBM)


def split(x):
    hi = x.astype(BF16)
    return hi, (x - hi.astype(F32)).astype(BF16)


def dot(a, b):
    return jnp.dot(a, b, preferred_element_type=F32)


def iota(shape, dim):
    return lax.broadcasted_iota(jnp.int32, shape, dim)


def one_hot(mask):
    return jnp.where(mask, 1.0, 0.0).astype(BF16)


def log2(x):
    assert x == 1 << (x.bit_length() - 1)
    return x.bit_length() - 1


class Plan:
    def __init__(self, vshape, bshape, n):
        self.n = n
        self.slots = vshape[2]
        self.k = self.slots // n
        self.zc = bshape[1]
        self.ny, self.nx = bshape[2:]
        self.edge = math.isqrt(vshape[3])
        self.half = self.edge // 2
        self.area = self.half * self.half
        self.bcols = self.nx // self.half
        self.rc = -(-self.zc * self.k // 8) * 8
        self.ru = 3 * self.rc
        self.rows = n * self.rc
        self.rb = 3 * self.zc * self.nx // self.area
        self.r1 = -(-(self.ru + self.rb + 1) // 8) * 8
        self.re = 2 * self.zc * self.nx // self.area
        self.r2 = -(-(self.ru + self.re) // 8) * 8
        self.wrap = self.nx // self.area


def mirror(i):
    return (i & ~7) | ((8 - (i & 7)) & 7)


def send_positions(p, table):
    s = p.slots
    row = jnp.broadcast_to((table >> log2(p.bcols)).astype(F32), (s, s))
    i, j = iota((s, s), 0), iota((s, s), 1)
    row_s = jnp.sum(jnp.where(i == j, row, 0.0), axis=1, keepdims=True)
    rank = jnp.sum(jnp.where((row_s == row) & (i < j), 1.0, 0.0), axis=0, keepdims=True)
    q = row[0:1] * p.k + rank
    q_s = jnp.sum(jnp.where(i == j, jnp.broadcast_to(q, (s, s)), 0.0), axis=1, keepdims=True)
    return q, q_s


def select(g, x):
    hi, lo = split(x)
    out = dot(g, jnp.concatenate([hi, lo], axis=1))
    return out[:, : x.shape[1]] + out[:, x.shape[1] :]


def lane_route(p):
    lane = iota((1, 1, p.rows), 2)
    i = lane & (p.rc - 1)
    return lane >> log2(p.rc), i >> log2(p.k), i & (p.k - 1)


def restrict_kernel(p, v_hbm, t_hbm, b_hbm, out_hbm, up_hbm, down_hbm, v_ref, t_ref, b_ref, out, last, first, sems):
    n, k, s, zc = p.n, p.k, p.slots, p.zc
    me = lax.axis_index("xy")
    t_copy = pltpu.make_async_copy(t_hbm, t_ref, sems.at[0])
    b_copy = pltpu.make_async_copy(b_hbm, b_ref, sems.at[1])
    v_copies = [pltpu.make_async_copy(v_hbm.at[c], v_ref.at[c], sems.at[2 + c]) for c in range(3)]
    t_copy.start()
    b_copy.start()
    for copy in v_copies:
        copy.start()
    half_fine = p.edge * p.edge // 2
    half_area = p.area // 2
    f, c = iota((half_fine, half_area), 0), iota((half_fine, half_area), 1)
    e = log2(p.edge)
    coarse = (mirror(f >> (e + 1)) << (e - 1)) + ((f & (p.edge - 1)) >> 1)
    sel = one_hot(coarse == c)
    t_copy.wait()
    table = t_ref[...]
    q, _ = send_positions(p, table)
    lanes = zc * s
    rep = one_hot((iota((s, lanes), 1) & (s - 1)) == iota((s, lanes), 0))
    qt = dot(jnp.broadcast_to(q, (8, s)).astype(BF16), rep)[0:1]
    shape = (n, p.rc, lanes)
    i = iota(shape, 1)
    target = (iota(shape, 0) * k + (i & (k - 1))).astype(F32)
    g = one_hot(((i >> log2(k)) == (iota(shape, 2) >> log2(s))) & (target == qt.reshape(1, 1, lanes)))
    g = g.reshape(p.rows, lanes)
    col = jnp.broadcast_to((table & (p.bcols - 1)).astype(F32), (s, s))
    qi = iota((s, s), 0).astype(F32)
    col_q = jnp.sum(jnp.where(qi == jnp.broadcast_to(q, (s, s)), col, 0.0), axis=1, keepdims=True)
    qa, la = iota((s, p.area), 0), iota((s, p.area), 1)
    spread = jnp.where((qa & (k - 1)) == (la & (k - 1)), col_q, 0.0).astype(BF16)
    gather = one_hot((iota((n, s), 1) >> log2(k)) == iota((n, s), 0))
    cols = dot(gather, spread)
    at = p.ru + p.rb
    for r in range(n):
        out[r, at : at + 1, :] = cols[r : r + 1]
    b_copy.wait()
    sends = [
        pltpu.make_async_copy(b_ref.at[0:2, zc - 1], up_hbm, sems.at[5]),
        pltpu.make_async_copy(b_ref.at[0:2, 0], down_hbm, sems.at[6]),
    ]
    for c in range(3):
        for z in range(zc):
            for h in range(p.wrap):
                at = (c * zc + z) * p.wrap + h
                w = slice(h * p.area, (h + 1) * p.area)
                last[at : at + 1, :] = b_ref[c, z, p.ny - 1 : p.ny, w]
                first[at : at + 1, :] = b_ref[c, z, 0:1, w]
    nxt = lax.rem(me + 1, n)
    for r in range(n):
        out[r, p.ru : p.ru + p.rb, :] = jnp.where(r == nxt, last[: p.rb], first[: p.rb])
    tail = pl.ds(p.ru, p.r1 - p.ru)
    sends.append(pltpu.make_async_copy(out.at[:, tail, :], out_hbm.at[:, tail, :], sems.at[7]))
    for send in sends:
        send.start()
    averages = []
    m = zc * s
    ws = [slice(h * half_fine, (h + 1) * half_fine) for h in range(2)]
    for c in range(3):
        v_copies[c].wait()
        z_sum = jnp.concatenate([v_ref[c, 2 * z] + v_ref[c, 2 * z + 1] for z in range(zc)], axis=0)
        hi, lo = split(z_sum)
        o = dot(jnp.concatenate([x[:, w] for w in ws for x in (hi, lo)], axis=0), sel)
        u = [o[2 * h * m : (2 * h + 1) * m] + o[(2 * h + 1) * m : (2 * h + 2) * m] for h in range(2)]
        averages.append(jnp.concatenate(u, axis=1) * 0.125)
    for c in range(3):
        out[:, c * p.rc : (c + 1) * p.rc, :] = select(g, averages[c]).reshape(n, p.rc, p.area)
        rows = pl.ds(c * p.rc, p.rc)
        sends.append(pltpu.make_async_copy(out.at[:, rows, :], out_hbm.at[:, rows, :], sems.at[8 + c]))
        sends[-1].start()
    for send in sends:
        send.wait()


def tile_transpose(p, t):
    g = iota(t.shape, 1) >> log2(p.half)
    t = pltpu.roll(t, 0, 1, stride=p.half, stride_axis=0)
    for b in (1, 2, 4):
        t = jnp.where((g & b) != 0, pltpu.roll(t, 8 - b, 0), t)
    return pltpu.roll(t, 0, 1, stride=p.half, stride_axis=0)


def blocks_to_grid(p, blk):
    rows = []
    for yh in range(p.half // 8):
        rows.append(
            jnp.concatenate(
                [
                    tile_transpose(p, blk[8 * c : 8 * c + 8, 128 * yh : 128 * yh + 128])
                    for c in range(p.bcols // 8)
                ],
                axis=1,
            )
        )
    return jnp.concatenate(rows, axis=0)


def grid_to_blocks(p, grid):
    rows = []
    for c in range(p.bcols // 8):
        rows.append(
            jnp.concatenate(
                [
                    tile_transpose(p, grid[8 * yh : 8 * yh + 8, 128 * c : 128 * c + 128])
                    for yh in range(p.half // 8)
                ],
                axis=1,
            )
        )
    return jnp.concatenate(rows, axis=0)


def x_next(f):
    return pltpu.roll(f, f.shape[1] - 1, 1)


def x_prev(f):
    return pltpu.roll(f, 1, 1)


def y_next(f, halo):
    return jnp.where(iota(f.shape, 0) == f.shape[0] - 1, halo, pltpu.roll(f, f.shape[0] - 1, 0))


def y_prev(f, halo):
    return jnp.where(iota(f.shape, 0) == 0, halo, pltpu.roll(f, 1, 0))


def row_of(p, ref, src, at):
    return jnp.concatenate([ref[src, pl.ds(at + h, 1), :] for h in range(p.wrap)], axis=1)


def interior_kernel(p, b_ref, t_ref, copy_ref, j_ref, next_ref, g3_ref):
    s, k = p.slots, p.k
    _, q_s = send_positions(p, t_ref[...])
    r_l, z_l, j_l = lane_route(p)
    shape = (p.zc, s, p.rows)
    g3 = (iota(shape, 0) == z_l) & (q_s.reshape(1, s, 1) == (r_l * k + j_l).astype(F32))
    g3_ref[...] = one_hot(g3).reshape(p.zc * s, p.rows)
    zero = jnp.zeros((p.ny, p.nx), F32)
    for z in range(p.zc):
        b = [b_ref[c, z] for c in range(3)]
        below = [b_ref[c, z - 1] if z > 0 else zero for c in range(3)]
        above = [b_ref[c, z + 1] if z < p.zc - 1 else zero for c in range(3)]
        south, north = [y_prev(f, 0.0) for f in b], [y_next(f, 0.0) for f in b]
        west, east = [x_prev(f) for f in b], [x_next(f) for f in b]
        j_ref[0, z] = ((north[2] - south[2]) - (above[1] - below[1])) * 0.5
        j_ref[1, z] = ((above[0] - below[0]) - (east[2] - west[2])) * 0.5
        j_ref[2, z] = ((east[1] - west[1]) - (north[0] - south[0])) * 0.5
        for c in range(3):
            lap = below[c] + above[c] + south[c] + north[c] + west[c] + east[c] - 6.0 * b[c]
            next_ref[c, z] = b[c] + 0.05 * lap
            copy_ref[c, z] = b[c]


def edge_rows(p, ref, nxt, prv, at):
    y = iota((p.ny, p.nx), 0)
    north = jnp.where(y == p.ny - 1, row_of(p, ref, nxt, at), 0.0)
    return north, jnp.where(y == 0, row_of(p, ref, prv, at), 0.0)


def field_kernel(p, r_ref, b_ref, j_ref, lo_ref, hi_ref, out, e_ref, up_ref, down_ref, e_rows):
    n, k, zc = p.n, p.k, p.zc
    me = lax.axis_index("xy")
    nxt, prv = lax.rem(me + 1, n), lax.rem(me + n - 1, n)
    b = [[b_ref[c, z] for z in range(zc)] for c in range(3)]
    cols = r_ref[:, p.ru + p.rb, :]
    shape = (n, p.rc, 128)
    col_s = jnp.sum(
        jnp.where((iota(shape, 1) & (k - 1)) == iota(shape, 2), cols[:, None, :128], 0.0), axis=2, keepdims=True
    )
    shape = (n, p.rc, zc * p.bcols)
    lane = iota(shape, 2)
    g = one_hot(
        ((iota(shape, 1) >> log2(k)) == (lane >> log2(p.bcols)))
        & (col_s == mirror(lane & (p.bcols - 1)).astype(F32))
    ).reshape(p.rows, zc * p.bcols)
    force = []
    zero = jnp.zeros((p.ny, p.nx), F32)
    for z in range(zc):
        bz = [b[c][z] for c in range(3)]
        dy = {}
        for c in (0, 2):
            north, south = edge_rows(p, r_ref, nxt, prv, p.ru + (c * zc + z) * p.wrap)
            dy[c] = north - south
        dz = [zero, zero]
        for c in range(2):
            if z == zc - 1:
                dz[c] = dz[c] + hi_ref[c]
            if z == 0:
                dz[c] = dz[c] - lo_ref[c]
        j0 = j_ref[0, z] + (dy[2] - dz[1]) * 0.5
        j1 = j_ref[1, z] + dz[0] * 0.5
        j2 = j_ref[2, z] - dy[0] * 0.5
        force.append([j1 * bz[2] - j2 * bz[1], j2 * bz[0] - j0 * bz[2], j0 * bz[1] - j1 * bz[0]])
    for c in range(3):
        f_blk = jnp.concatenate([grid_to_blocks(p, force[z][c]) for z in range(zc)], axis=0)
        out[:, c * p.rc : (c + 1) * p.rc, :] = select(g, f_blk).reshape(n, p.rc, p.area)
    p_l, z_l, _ = lane_route(p)
    shape = (n, p.rows)
    col_l = jnp.sum(
        jnp.where(iota(shape, 0) == p_l.reshape(1, p.rows), cols[:, : p.rows], 0.0), axis=0, keepdims=True
    )
    shape = (zc, p.bcols, p.rows)
    g = one_hot(
        (iota(shape, 0) == z_l) & (iota(shape, 1).astype(F32) == col_l.reshape(1, 1, p.rows))
    ).reshape(zc * p.bcols, p.rows)
    u = []
    for c in range(3):
        blk = select(g, r_ref[:, c * p.rc : (c + 1) * p.rc, :].reshape(p.rows, p.area))
        u.append([blocks_to_grid(p, blk[z * p.bcols : (z + 1) * p.bcols]) for z in range(zc)])
    for z in range(zc):
        uz, bz = [u[c][z] for c in range(3)], [b[c][z] for c in range(3)]
        ez = [uz[1] * bz[2] - uz[2] * bz[1], uz[2] * bz[0] - uz[0] * bz[2], uz[0] * bz[1] - uz[1] * bz[0]]
        for c in range(3):
            e_ref[c, z] = ez[c]
        if z == zc - 1:
            up_ref[0], up_ref[1], up_ref[2] = ez[0], ez[1], bz[2]
        if z == 0:
            down_ref[0], down_ref[1], down_ref[2] = ez[0], ez[1], bz[2]
        for i, c in enumerate((0, 2)):
            for h in range(p.wrap):
                at = (i * zc + z) * p.wrap + h
                w = slice(h * p.area, (h + 1) * p.area)
                e_rows[0, at : at + 1, :] = ez[c][0:1, w]
                e_rows[1, at : at + 1, :] = ez[c][p.ny - 1 : p.ny, w]
    for r in range(n):
        out[r, p.ru : p.ru + p.re, :] = jnp.where(r == nxt, e_rows[1], e_rows[0])


def local_kernel(p, r_ref, b_ref, lo_ref, hi_ref, e_ref, next_ref):
    n, zc = p.n, p.zc
    me = lax.axis_index("xy")
    nxt, prv = lax.rem(me + 1, n), lax.rem(me + n - 1, n)
    zero = jnp.zeros((p.ny, p.nx), F32)
    for z in range(zc):
        e = [e_ref[c, z] for c in range(3)]
        above = [e_ref[c, z + 1] if z < zc - 1 else zero for c in range(2)]
        below = [e_ref[c, z - 1] if z > 0 else zero for c in range(2)]
        curl = [
            (y_next(e[2], 0.0) - y_prev(e[2], 0.0)) - (above[1] - below[1]),
            (above[0] - below[0]) - (x_next(e[2]) - x_prev(e[2])),
            (x_next(e[1]) - x_prev(e[1])) - (y_next(e[0], 0.0) - y_prev(e[0], 0.0)),
        ]
        for c in range(3):
            north, south = edge_rows(p, r_ref, nxt, prv, p.ru + (c * zc + z) * p.wrap)
            total = curl[c] + north + south
            if c < 2 and z == 0:
                total = total + lo_ref[c]
            if c < 2 and z == zc - 1:
                total = total + hi_ref[c]
            next_ref[c, z] = b_ref[c, z] + 0.05 * total


def widen_kernel(p, r_ref, g_ref, v_ref, vel_hbm, vel, sems):
    zc = p.zc
    half_fine = p.edge * p.edge // 2
    half_area = p.area // 2
    ex = log2(p.edge)
    c, f = iota((half_area, half_fine), 0), iota((half_area, half_fine), 1)
    coarse = ((f >> (ex + 1)) << (ex - 1)) + ((f & (p.edge - 1)) >> 1)
    sel = one_hot(coarse == c)
    sel = jnp.concatenate([sel, sel], axis=0)
    g = g_ref[...]
    ws = [slice(h * half_area, (h + 1) * half_area) for h in range(2)]
    s = p.slots
    m = zc * s
    copies = []
    for c in range(3):
        hi, lo = split(r_ref[:, c * p.rc : (c + 1) * p.rc, :].reshape(p.rows, p.area) * 0.1)
        parts = dot(g, jnp.concatenate([hi, lo], axis=1)).astype(BF16)
        hi, lo = parts[:, : p.area], parts[:, p.area :]
        pairs = [jnp.concatenate([hi[:, w], lo[:, w]], axis=1) for w in ws]
        add = dot(jnp.concatenate(pairs, axis=0), sel)
        for z in range(zc):
            for h in range(2):
                fw = slice(h * half_fine, (h + 1) * half_fine)
                part = add[h * m + z * s : h * m + (z + 1) * s]
                for d in range(2):
                    vel[c, 2 * z + d, :, fw] = v_ref[c, 2 * z + d, :, fw] + part
        copies.append(pltpu.make_async_copy(vel.at[c], vel_hbm.at[c], sems.at[c]))
        copies[-1].start()
    for copy in copies:
        copy.wait()


def finish_kernel(p, r_ref, n_ref, lo_ref, hi_ref, mag):
    n, zc = p.n, p.zc
    me = lax.axis_index("xy")
    nxt, prv = lax.rem(me + 1, n), lax.rem(me + n - 1, n)

    def dy(i, z):
        north, south = edge_rows(p, r_ref, nxt, prv, p.ru + (i * zc + z) * p.wrap)
        return north - south

    for z in range(zc):
        dz = [jnp.zeros((p.ny, p.nx), F32)] * 2
        outer = dz[0]
        if z == zc - 1:
            dz = [dz[c] + hi_ref[c] for c in range(2)]
            outer = outer + hi_ref[2]
        if z == 0:
            dz = [dz[c] - lo_ref[c] for c in range(2)]
            outer = outer + lo_ref[2]
        mag[0, z] = n_ref[0, z] + 0.05 * (dy(1, z) - dz[1])
        mag[1, z] = n_ref[1, z] + 0.05 * dz[0]
        mag[2, z] = n_ref[2, z] + 0.05 * (outer - dy(0, z))


def struct(*shape, dtype=F32):
    return jax.ShapeDtypeStruct(shape, dtype)


def call(kernel, ins, outs, scratch=(), grant=20 << 20):
    return pl.pallas_call(
        kernel,
        out_shape=[o for o, _ in outs],
        in_specs=ins,
        out_specs=[spec for _, spec in outs],
        scratch_shapes=list(scratch),
        cost_estimate=pl.CostEstimate(flops=1 << 24, bytes_accessed=1 << 20, transcendentals=0),
        compiler_params=pltpu.CompilerParams(vmem_limit_bytes=grant),
    )


def ring(axis, step):
    n = lax.axis_size(axis)
    return [(i, (i + step) % n) for i in range(n)]


def planes(up, down):
    below = lax.ppermute(up, "gz", ring("gz", 1))
    above = lax.ppermute(down, "gz", ring("gz", -1))
    return below, above


def body(velocity, magnetic, slot_block_table):
    p = Plan(velocity.shape, magnetic.shape, lax.axis_size("xy"))
    plane = (p.ny, p.nx)
    dma = pltpu.SemaphoreType.DMA
    table = slot_block_table.reshape(1, p.slots)
    sent, up, down = call(
        functools.partial(restrict_kernel, p),
        [HBM] * 3,
        [(struct(p.n, p.r1, p.area), HBM), (struct(2, *plane), HBM), (struct(2, *plane), HBM)],
        [
            pltpu.VMEM(velocity.shape, F32),
            pltpu.VMEM((1, p.slots), jnp.int32),
            pltpu.VMEM(magnetic.shape, F32),
            pltpu.VMEM((p.n, p.r1, p.area), F32),
            pltpu.VMEM((-(-p.rb // 8) * 8, p.area), F32),
            pltpu.VMEM((-(-p.rb // 8) * 8, p.area), F32),
            dma((11,)),
        ],
        ALL_VMEM,
    )(velocity, table, magnetic)
    got = lax.all_to_all(sent, "xy", 0, 0, tiled=True)
    below, above = planes(up, down)
    held, held_table, _ = lax.optimization_barrier((magnetic, table, up))
    field, current, diffused, g3 = call(
        functools.partial(interior_kernel, p),
        [VMEM] * 2,
        [(struct(*magnetic.shape), VMEM)] * 3 + [(struct(p.zc * p.slots, p.rows, dtype=BF16), VMEM)],
    )(held, held_table)
    sent, emf, up, down = call(
        functools.partial(field_kernel, p),
        [VMEM] * 5,
        [
            (struct(p.n, p.r2, p.area), VMEM),
            (struct(*magnetic.shape), VMEM),
            (struct(3, *plane), VMEM),
            (struct(3, *plane), VMEM),
        ],
        [pltpu.VMEM((2, p.re, p.area), F32)],
    )(got, field, current, below, above)
    got_force = lax.all_to_all(sent, "xy", 0, 0, tiled=True)
    emf_below, emf_above = planes(up, down)
    (partial,) = call(
        functools.partial(local_kernel, p), [VMEM] * 5, [(struct(*magnetic.shape), VMEM)]
    )(got, diffused, below, above, emf)
    (updated,) = call(
        functools.partial(widen_kernel, p),
        [VMEM] * 3,
        [(struct(*velocity.shape), HBM)],
        [pltpu.VMEM(velocity.shape, F32), dma((3,))],
    )(got_force, g3, velocity)
    (finished,) = call(
        functools.partial(finish_kernel, p), [VMEM] * 4, [(struct(*magnetic.shape), VMEM)]
    )(got_force, partial, emf_below, emf_above)
    return updated, finished


def solution(mesh):
    return jax.shard_map(
        body,
        mesh=mesh,
        in_specs=(P(None, "gz", "xy", None), P(None, "gz", "xy", None), P("xy")),
        out_specs=(P(None, "gz", "xy", None), P(None, "gz", "xy", None)),
        check_vma=False,
    )
```

```python
import functools
import math

import jax
import jax.numpy as jnp
from jax import lax
from jax.experimental import pallas as pl
from jax.experimental.pallas import tpu as pltpu
from jax.sharding import PartitionSpec as P

F32, BF16 = jnp.float32, jnp.bfloat16
VMEM = pl.BlockSpec(memory_space=pltpu.VMEM)
ALL_VMEM = 67043328
HBM = pl.BlockSpec(memory_space=pltpu.HBM)


def split(x):
    hi = x.astype(BF16)
    return hi, (x - hi.astype(F32)).astype(BF16)


def dot(a, b):
    return jnp.dot(a, b, preferred_element_type=F32)


def iota(shape, dim):
    return lax.broadcasted_iota(jnp.int32, shape, dim)


def one_hot(mask):
    return jnp.where(mask, 1.0, 0.0).astype(BF16)


def log2(x):
    assert x == 1 << (x.bit_length() - 1)
    return x.bit_length() - 1


class Plan:
    def __init__(self, vshape, bshape, n):
        self.n = n
        self.slots = vshape[2]
        self.k = self.slots // n
        self.zc = bshape[1]
        self.ny, self.nx = bshape[2:]
        self.edge = math.isqrt(vshape[3])
        self.half = self.edge // 2
        self.area = self.half * self.half
        self.bcols = self.nx // self.half
        self.rc = -(-self.zc * self.k // 8) * 8
        self.ru = 3 * self.rc
        self.rows = n * self.rc
        self.r1 = self.ru + 8
        self.ry = -(-3 * self.zc // 8) * 8


def mirror(i):
    return (i & ~7) | ((8 - (i & 7)) & 7)


def send_positions(p, table):
    s = p.slots
    row = jnp.broadcast_to((table >> log2(p.bcols)).astype(F32), (s, s))
    i, j = iota((s, s), 0), iota((s, s), 1)
    row_s = jnp.sum(jnp.where(i == j, row, 0.0), axis=1, keepdims=True)
    rank = jnp.sum(jnp.where((row_s == row) & (i < j), 1.0, 0.0), axis=0, keepdims=True)
    q = row[0:1] * p.k + rank
    q_s = jnp.sum(jnp.where(i == j, jnp.broadcast_to(q, (s, s)), 0.0), axis=1, keepdims=True)
    return q, q_s


def select(g, x):
    return dot(g, jnp.concatenate(split(x), axis=0))


def lane_route(p, times=1):
    lane = iota((1, 1, times * p.rows), 2)
    i = lane & (p.rc - 1)
    return (lane >> log2(p.rc)) & (p.n - 1), i >> log2(p.k), i & (p.k - 1)


def restrict_kernel(p, v_hbm, t_hbm, b_hbm, out_hbm, up_hbm, down_hbm, last_hbm, first_hbm, v_ref, t_ref, b_ref, out, last, first, sems):
    n, k, s, zc = p.n, p.k, p.slots, p.zc
    t_copy = pltpu.make_async_copy(t_hbm, t_ref, sems.at[0])
    b_copy = pltpu.make_async_copy(b_hbm, b_ref, sems.at[1])
    v_copies = [pltpu.make_async_copy(v_hbm.at[c], v_ref.at[c], sems.at[2 + c]) for c in range(3)]
    t_copy.start()
    for copy in v_copies:
        copy.start()
    b_copy.start()
    half_fine = p.edge * p.edge // 2
    half_area = p.area // 2
    f, c = iota((half_fine, half_area), 0), iota((half_fine, half_area), 1)
    e = log2(p.edge)
    coarse = (mirror(f >> (e + 1)) << (e - 1)) + ((f & (p.edge - 1)) >> 1)
    sel = one_hot(coarse == c)
    t_copy.wait()
    table = t_ref[...]
    q, _ = send_positions(p, table)
    lanes = 2 * zc * s
    rep = one_hot((iota((s, lanes), 1) & (s - 1)) == iota((s, lanes), 0))
    qt = dot(jnp.broadcast_to(q, (8, s)).astype(BF16), rep)[0:1]
    shape = (n, p.rc, lanes)
    i = iota(shape, 1)
    target = (iota(shape, 0) * k + (i & (k - 1))).astype(F32)
    g = one_hot(((i >> log2(k)) == ((iota(shape, 2) >> log2(s)) & (zc - 1))) & (target == qt.reshape(1, 1, lanes)))
    g = g.reshape(p.rows, lanes)
    col = jnp.broadcast_to((table & (p.bcols - 1)).astype(F32), (s, s))
    qi = iota((s, s), 0).astype(F32)
    col_q = jnp.sum(jnp.where(qi == jnp.broadcast_to(q, (s, s)), col, 0.0), axis=1, keepdims=True)
    qa, la = iota((s, p.area), 0), iota((s, p.area), 1)
    spread = jnp.where((qa & (k - 1)) == (la & (k - 1)), col_q, 0.0).astype(BF16)
    gather = one_hot((iota((n, s), 1) >> log2(k)) == iota((n, s), 0))
    cols = dot(gather, spread)
    for r in range(n):
        out[r, p.ru : p.ru + 1, :] = cols[r : r + 1]
    averages = []
    m = zc * s
    ws = [slice(h * half_fine, (h + 1) * half_fine) for h in range(2)]
    for c in range(3):
        v_copies[c].wait()
        u = []
        for w in ws:
            z_sum = [v_ref[c, 2 * z, :, w] + v_ref[c, 2 * z + 1, :, w] for z in range(zc)]
            o = dot(jnp.concatenate(split(jnp.concatenate(z_sum, axis=0)), axis=0), sel)
            u.append(o[:m] + o[m:])
        averages.append(jnp.concatenate(u, axis=1) * 0.125)
    b_copy.wait()
    sends = [
        pltpu.make_async_copy(b_ref.at[0:2, zc - 1], up_hbm, sems.at[5]),
        pltpu.make_async_copy(b_ref.at[0:2, 0], down_hbm, sems.at[6]),
    ]
    for c in range(3):
        for z in range(zc):
            at = c * zc + z
            last[at : at + 1, :] = b_ref[c, z, p.ny - 1 : p.ny, :]
            first[at : at + 1, :] = b_ref[c, z, 0:1, :]
    sends.append(pltpu.make_async_copy(last, last_hbm, sems.at[11]))
    sends.append(pltpu.make_async_copy(first, first_hbm, sems.at[12]))
    tail = pl.ds(p.ru, p.r1 - p.ru)
    sends.append(pltpu.make_async_copy(out.at[:, tail, :], out_hbm.at[:, tail, :], sems.at[7]))
    for send in sends:
        send.start()
    for c in range(3):
        out[:, c * p.rc : (c + 1) * p.rc, :] = select(g, averages[c]).reshape(n, p.rc, p.area)
        rows = pl.ds(c * p.rc, p.rc)
        sends.append(pltpu.make_async_copy(out.at[:, rows, :], out_hbm.at[:, rows, :], sems.at[8 + c]))
        sends[-1].start()
    for send in sends:
        send.wait()


def tile_transpose(p, t):
    g = iota(t.shape, 1) >> log2(p.half)
    t = pltpu.roll(t, 0, 1, stride=p.half, stride_axis=0)
    for b in (1, 2, 4):
        t = jnp.where((g & b) != 0, pltpu.roll(t, 8 - b, 0), t)
    return pltpu.roll(t, 0, 1, stride=p.half, stride_axis=0)


def blocks_to_grid(p, blk):
    rows = []
    for yh in range(p.half // 8):
        rows.append(
            jnp.concatenate(
                [
                    tile_transpose(p, blk[8 * c : 8 * c + 8, 128 * yh : 128 * yh + 128])
                    for c in range(p.bcols // 8)
                ],
                axis=1,
            )
        )
    return jnp.concatenate(rows, axis=0)


def grid_to_blocks(p, grid):
    rows = []
    for c in range(p.bcols // 8):
        rows.append(
            jnp.concatenate(
                [
                    tile_transpose(p, grid[8 * yh : 8 * yh + 8, 128 * c : 128 * c + 128])
                    for yh in range(p.half // 8)
                ],
                axis=1,
            )
        )
    return jnp.concatenate(rows, axis=0)


def x_next(f):
    return pltpu.roll(f, f.shape[1] - 1, 1)


def x_prev(f):
    return pltpu.roll(f, 1, 1)


def y_next(f, halo):
    return jnp.where(iota(f.shape, 0) == f.shape[0] - 1, halo, pltpu.roll(f, f.shape[0] - 1, 0))


def y_prev(f, halo):
    return jnp.where(iota(f.shape, 0) == 0, halo, pltpu.roll(f, 1, 0))


def interior_kernel(p, b_ref, t_ref, copy_ref, j_ref, next_ref, g3_ref):
    s, k = p.slots, p.k
    _, q_s = send_positions(p, t_ref[...])
    r_l, z_l, j_l = lane_route(p)
    shape = (p.zc, s, p.rows)
    g3 = (iota(shape, 0) == z_l) & (q_s.reshape(1, s, 1) == (r_l * k + j_l).astype(F32))
    g3_ref[...] = one_hot(g3).reshape(p.zc * s, p.rows)
    zero = jnp.zeros((p.ny, p.nx), F32)
    for z in range(p.zc):
        b = [b_ref[c, z] for c in range(3)]
        below = [b_ref[c, z - 1] if z > 0 else zero for c in range(3)]
        above = [b_ref[c, z + 1] if z < p.zc - 1 else zero for c in range(3)]
        south, north = [y_prev(f, 0.0) for f in b], [y_next(f, 0.0) for f in b]
        west, east = [x_prev(f) for f in b], [x_next(f) for f in b]
        j_ref[0, z] = ((north[2] - south[2]) - (above[1] - below[1])) * 0.5
        j_ref[1, z] = ((above[0] - below[0]) - (east[2] - west[2])) * 0.5
        j_ref[2, z] = ((east[1] - west[1]) - (north[0] - south[0])) * 0.5
        for c in range(3):
            lap = below[c] + above[c] + south[c] + north[c] + west[c] + east[c] - 6.0 * b[c]
            next_ref[c, z] = b[c] + 0.05 * lap
            copy_ref[c, z] = b[c]


def edge_rows(p, n_ref, s_ref, at):
    y = iota((p.ny, p.nx), 0)
    north = jnp.where(y == p.ny - 1, n_ref[at : at + 1, :], 0.0)
    return north, jnp.where(y == 0, s_ref[at : at + 1, :], 0.0)


def field_kernel(p, r_ref, b_ref, j_ref, lo_ref, hi_ref, n_ref, s_ref, out, e_ref, up_ref, down_ref, last, first):
    n, k, zc = p.n, p.k, p.zc
    b = [[b_ref[c, z] for z in range(zc)] for c in range(3)]
    cols = r_ref[:, p.ru, :]
    shape = (n, p.rc, 128)
    col_s = jnp.sum(
        jnp.where((iota(shape, 1) & (k - 1)) == iota(shape, 2), cols[:, None, :128], 0.0), axis=2, keepdims=True
    )
    shape = (n, p.rc, 2 * zc * p.bcols)
    lane = iota(shape, 2)
    g = one_hot(
        ((iota(shape, 1) >> log2(k)) == ((lane >> log2(p.bcols)) & (zc - 1)))
        & (col_s == mirror(lane & (p.bcols - 1)).astype(F32))
    ).reshape(p.rows, 2 * zc * p.bcols)
    force = []
    zero = jnp.zeros((p.ny, p.nx), F32)
    for z in range(zc):
        bz = [b[c][z] for c in range(3)]
        dy = {}
        for c in (0, 2):
            north, south = edge_rows(p, n_ref, s_ref, c * zc + z)
            dy[c] = north - south
        dz = [zero, zero]
        for c in range(2):
            if z == zc - 1:
                dz[c] = dz[c] + hi_ref[c]
            if z == 0:
                dz[c] = dz[c] - lo_ref[c]
        j0 = j_ref[0, z] + (dy[2] - dz[1]) * 0.5
        j1 = j_ref[1, z] + dz[0] * 0.5
        j2 = j_ref[2, z] - dy[0] * 0.5
        force.append([j1 * bz[2] - j2 * bz[1], j2 * bz[0] - j0 * bz[2], j0 * bz[1] - j1 * bz[0]])
    for c in range(3):
        f_blk = jnp.concatenate([grid_to_blocks(p, force[z][c]) for z in range(zc)], axis=0)
        out[:, c * p.rc : (c + 1) * p.rc, :] = select(g, f_blk).reshape(n, p.rc, p.area)
    times = 2 if 2 * p.rows <= p.area else 1
    width = times * p.rows
    p_l, z_l, _ = lane_route(p, times)
    shape = (n, width)
    col_l = jnp.sum(
        jnp.where(iota(shape, 0) == p_l.reshape(1, width), cols[:, :width], 0.0), axis=0, keepdims=True
    )
    shape = (zc, p.bcols, width)
    g = one_hot(
        (iota(shape, 0) == z_l) & (iota(shape, 1).astype(F32) == col_l.reshape(1, 1, width))
    ).reshape(zc * p.bcols, width)
    g = jnp.concatenate([g] * (2 // times), axis=1)
    u = []
    for c in range(3):
        blk = select(g, r_ref[:, c * p.rc : (c + 1) * p.rc, :].reshape(p.rows, p.area))
        u.append([blocks_to_grid(p, blk[z * p.bcols : (z + 1) * p.bcols]) for z in range(zc)])
    for z in range(zc):
        uz, bz = [u[c][z] for c in range(3)], [b[c][z] for c in range(3)]
        ez = [uz[1] * bz[2] - uz[2] * bz[1], uz[2] * bz[0] - uz[0] * bz[2], uz[0] * bz[1] - uz[1] * bz[0]]
        for c in range(3):
            e_ref[c, z] = ez[c]
        if z == zc - 1:
            up_ref[0], up_ref[1], up_ref[2] = ez[0], ez[1], bz[2]
        if z == 0:
            down_ref[0], down_ref[1], down_ref[2] = ez[0], ez[1], bz[2]
        for i, c in enumerate((0, 2)):
            at = i * zc + z
            first[at : at + 1, :] = ez[c][0:1]
            last[at : at + 1, :] = ez[c][p.ny - 1 : p.ny]


def local_kernel(p, b_ref, lo_ref, hi_ref, n_ref, s_ref, e_ref, next_ref):
    zc = p.zc
    zero = jnp.zeros((p.ny, p.nx), F32)
    for z in range(zc):
        e = [e_ref[c, z] for c in range(3)]
        above = [e_ref[c, z + 1] if z < zc - 1 else zero for c in range(2)]
        below = [e_ref[c, z - 1] if z > 0 else zero for c in range(2)]
        curl = [
            (y_next(e[2], 0.0) - y_prev(e[2], 0.0)) - (above[1] - below[1]),
            (above[0] - below[0]) - (x_next(e[2]) - x_prev(e[2])),
            (x_next(e[1]) - x_prev(e[1])) - (y_next(e[0], 0.0) - y_prev(e[0], 0.0)),
        ]
        for c in range(3):
            north, south = edge_rows(p, n_ref, s_ref, c * zc + z)
            total = curl[c] + north + south
            if c < 2 and z == 0:
                total = total + lo_ref[c]
            if c < 2 and z == zc - 1:
                total = total + hi_ref[c]
            next_ref[c, z] = b_ref[c, z] + 0.05 * total


def widen_kernel(p, r_ref, g_ref, v_ref, vel_hbm, vel, sems):
    zc = p.zc
    half_fine = p.edge * p.edge // 2
    half_area = p.area // 2
    ex = log2(p.edge)
    c, f = iota((half_area, half_fine), 0), iota((half_area, half_fine), 1)
    coarse = ((f >> (ex + 1)) << (ex - 1)) + ((f & (p.edge - 1)) >> 1)
    sel = one_hot(coarse == c)
    sel = jnp.concatenate([sel, sel], axis=0)
    g = g_ref[...]
    ws = [slice(h * half_area, (h + 1) * half_area) for h in range(2)]
    s = p.slots
    m = zc * s
    copies = []
    for c in range(3):
        hi, lo = split(r_ref[:, c * p.rc : (c + 1) * p.rc, :].reshape(p.rows, p.area) * 0.1)
        parts = dot(g, jnp.concatenate([hi, lo], axis=1)).astype(BF16)
        hi, lo = parts[:, : p.area], parts[:, p.area :]
        pairs = [jnp.concatenate([hi[:, w], lo[:, w]], axis=1) for w in ws]
        add = dot(jnp.concatenate(pairs, axis=0), sel)
        for z in range(zc):
            for h in range(2):
                fw = slice(h * half_fine, (h + 1) * half_fine)
                part = add[h * m + z * s : h * m + (z + 1) * s]
                for d in range(2):
                    vel[c, 2 * z + d, :, fw] = v_ref[c, 2 * z + d, :, fw] + part
        copies.append(pltpu.make_async_copy(vel.at[c], vel_hbm.at[c], sems.at[c]))
        copies[-1].start()
    for copy in copies:
        copy.wait()


def finish_kernel(p, m_ref, lo_ref, hi_ref, n_ref, s_ref, mag):
    zc = p.zc

    def dy(i, z):
        north, south = edge_rows(p, n_ref, s_ref, i * zc + z)
        return north - south

    for z in range(zc):
        dz = [jnp.zeros((p.ny, p.nx), F32)] * 2
        outer = dz[0]
        if z == zc - 1:
            dz = [dz[c] + hi_ref[c] for c in range(2)]
            outer = outer + hi_ref[2]
        if z == 0:
            dz = [dz[c] - lo_ref[c] for c in range(2)]
            outer = outer + lo_ref[2]
        mag[0, z] = m_ref[0, z] + 0.05 * (dy(1, z) - dz[1])
        mag[1, z] = m_ref[1, z] + 0.05 * dz[0]
        mag[2, z] = m_ref[2, z] + 0.05 * (outer - dy(0, z))


def struct(*shape, dtype=F32):
    return jax.ShapeDtypeStruct(shape, dtype)


def call(kernel, ins, outs, scratch=(), grant=20 << 20):
    return pl.pallas_call(
        kernel,
        out_shape=[o for o, _ in outs],
        in_specs=ins,
        out_specs=[spec for _, spec in outs],
        scratch_shapes=list(scratch),
        cost_estimate=pl.CostEstimate(flops=1 << 24, bytes_accessed=1 << 20, transcendentals=0),
        compiler_params=pltpu.CompilerParams(vmem_limit_bytes=grant),
    )


def ring(axis, step):
    n = lax.axis_size(axis)
    return [(i, (i + step) % n) for i in range(n)]


def exchange(up, down, last, first):
    below = lax.ppermute(up, "gz", ring("gz", 1))
    above = lax.ppermute(down, "gz", ring("gz", -1))
    south = lax.ppermute(last, "xy", ring("xy", 1))
    north = lax.ppermute(first, "xy", ring("xy", -1))
    return below, above, north, south


def body(velocity, magnetic, slot_block_table):
    p = Plan(velocity.shape, magnetic.shape, lax.axis_size("xy"))
    plane = (p.ny, p.nx)
    dma = pltpu.SemaphoreType.DMA
    table = slot_block_table.reshape(1, p.slots)
    sent, up, down, last, first = call(
        functools.partial(restrict_kernel, p),
        [HBM] * 3,
        [(struct(p.n, p.r1, p.area), HBM)] + [(struct(2, *plane), HBM)] * 2 + [(struct(p.ry, p.nx), HBM)] * 2,
        [
            pltpu.VMEM(velocity.shape, F32),
            pltpu.VMEM((1, p.slots), jnp.int32),
            pltpu.VMEM(magnetic.shape, F32),
            pltpu.VMEM((p.n, p.r1, p.area), F32),
            pltpu.VMEM((p.ry, p.nx), F32),
            pltpu.VMEM((p.ry, p.nx), F32),
            dma((13,)),
        ],
        ALL_VMEM,
    )(velocity, table, magnetic)
    got = lax.all_to_all(sent, "xy", 0, 0, tiled=True)
    below, above, north, south = exchange(up, down, last, first)
    held, held_table, _ = lax.optimization_barrier((magnetic, table, up))
    field, current, diffused, g3 = call(
        functools.partial(interior_kernel, p),
        [VMEM] * 2,
        [(struct(*magnetic.shape), VMEM)] * 3 + [(struct(p.zc * p.slots, p.rows, dtype=BF16), VMEM)],
    )(held, held_table)
    sent, emf, up, down, last, first = call(
        functools.partial(field_kernel, p),
        [VMEM] * 7,
        [(struct(p.n, p.ru, p.area), VMEM), (struct(*magnetic.shape), VMEM)]
        + [(struct(3, *plane), VMEM)] * 2
        + [(struct(p.ry, p.nx), VMEM)] * 2,
    )(got, field, current, below, above, north, south)
    got_force = lax.all_to_all(sent, "xy", 0, 0, tiled=True)
    outer = exchange(up, down, last, first)
    (partial,) = call(
        functools.partial(local_kernel, p), [VMEM] * 6, [(struct(*magnetic.shape), VMEM)]
    )(diffused, below, above, north, south, emf)
    (updated,) = call(
        functools.partial(widen_kernel, p),
        [VMEM] * 3,
        [(struct(*velocity.shape), HBM)],
        [pltpu.VMEM(velocity.shape, F32), dma((3,))],
    )(got_force, g3, velocity)
    partial, _ = lax.optimization_barrier((partial, updated))
    (finished,) = call(
        functools.partial(finish_kernel, p), [VMEM] * 5, [(struct(*magnetic.shape), VMEM)]
    )(partial, *outer)
    return updated, finished


def solution(mesh):
    return jax.shard_map(
        body,
        mesh=mesh,
        in_specs=(P(None, "gz", "xy", None), P(None, "gz", "xy", None), P("xy")),
        out_specs=(P(None, "gz", "xy", None), P(None, "gz", "xy", None)),
        check_vma=False,
    )
```

```python
import functools
import math

import jax
import jax.numpy as jnp
from jax import lax
from jax.experimental import pallas as pl
from jax.experimental.pallas import tpu as pltpu
from jax.sharding import PartitionSpec as P

F32, BF16 = jnp.float32, jnp.bfloat16
VMEM = pl.BlockSpec(memory_space=pltpu.VMEM)
ALL_VMEM = 67043328
HBM = pl.BlockSpec(memory_space=pltpu.HBM)


def split(x):
    hi = x.astype(BF16)
    return hi, (x - hi.astype(F32)).astype(BF16)


def dot(a, b):
    return jnp.dot(a, b, preferred_element_type=F32)


def iota(shape, dim):
    return lax.broadcasted_iota(jnp.int32, shape, dim)


def one_hot(mask):
    return jnp.where(mask, 1.0, 0.0).astype(BF16)


def log2(x):
    assert x == 1 << (x.bit_length() - 1)
    return x.bit_length() - 1


class Plan:
    def __init__(self, vshape, bshape, n):
        self.n = n
        self.slots = vshape[2]
        self.k = self.slots // n
        self.zc = bshape[1]
        self.ny, self.nx = bshape[2:]
        self.edge = math.isqrt(vshape[3])
        self.half = self.edge // 2
        self.area = self.half * self.half
        self.bcols = self.nx // self.half
        self.rc = -(-self.zc * self.k // 8) * 8
        self.ru = 3 * self.rc
        self.rows = n * self.rc
        self.rb = 3 * self.zc * self.nx // self.area
        self.r1 = -(-(self.ru + self.rb + 1) // 8) * 8
        self.re = 2 * self.zc * self.nx // self.area
        self.r2 = -(-(self.ru + self.re) // 8) * 8
        self.wrap = self.nx // self.area


def mirror(i):
    return (i & ~7) | ((8 - (i & 7)) & 7)


def send_positions(p, table):
    s = p.slots
    row = jnp.broadcast_to((table >> log2(p.bcols)).astype(F32), (s, s))
    i, j = iota((s, s), 0), iota((s, s), 1)
    row_s = jnp.sum(jnp.where(i == j, row, 0.0), axis=1, keepdims=True)
    rank = jnp.sum(jnp.where((row_s == row) & (i < j), 1.0, 0.0), axis=0, keepdims=True)
    q = row[0:1] * p.k + rank
    q_s = jnp.sum(jnp.where(i == j, jnp.broadcast_to(q, (s, s)), 0.0), axis=1, keepdims=True)
    return q, q_s


def select(g, x):
    hi, lo = split(x)
    out = dot(g, jnp.concatenate([hi, lo], axis=1))
    return out[:, : x.shape[1]] + out[:, x.shape[1] :]


def lane_route(p):
    lane = iota((1, 1, p.rows), 2)
    i = lane & (p.rc - 1)
    return lane >> log2(p.rc), i >> log2(p.k), i & (p.k - 1)


def restrict_kernel(p, v_hbm, t_hbm, b_hbm, out_hbm, up_hbm, down_hbm, up2_hbm, down2_hbm, v_ref, t_ref, b_ref, out, last, first, sems):
    n, k, s, zc = p.n, p.k, p.slots, p.zc
    me = lax.axis_index("xy")
    t_copy = pltpu.make_async_copy(t_hbm, t_ref, sems.at[0])
    b_copy = pltpu.make_async_copy(b_hbm, b_ref, sems.at[1])
    v_copies = [pltpu.make_async_copy(v_hbm.at[c], v_ref.at[c], sems.at[2 + c]) for c in range(3)]
    t_copy.start()
    b_copy.start()
    for copy in v_copies:
        copy.start()
    half_fine = p.edge * p.edge // 2
    half_area = p.area // 2
    f, c = iota((half_fine, half_area), 0), iota((half_fine, half_area), 1)
    e = log2(p.edge)
    coarse = (mirror(f >> (e + 1)) << (e - 1)) + ((f & (p.edge - 1)) >> 1)
    sel = one_hot(coarse == c)
    t_copy.wait()
    table = t_ref[...]
    q, _ = send_positions(p, table)
    lanes = zc * s
    rep = one_hot((iota((s, lanes), 1) & (s - 1)) == iota((s, lanes), 0))
    qt = dot(jnp.broadcast_to(q, (8, s)).astype(BF16), rep)[0:1]
    shape = (n, p.rc, lanes)
    i = iota(shape, 1)
    target = (iota(shape, 0) * k + (i & (k - 1))).astype(F32)
    g = one_hot(((i >> log2(k)) == (iota(shape, 2) >> log2(s))) & (target == qt.reshape(1, 1, lanes)))
    g = g.reshape(p.rows, lanes)
    col = jnp.broadcast_to((table & (p.bcols - 1)).astype(F32), (s, s))
    qi = iota((s, s), 0).astype(F32)
    col_q = jnp.sum(jnp.where(qi == jnp.broadcast_to(q, (s, s)), col, 0.0), axis=1, keepdims=True)
    qa, la = iota((s, p.area), 0), iota((s, p.area), 1)
    spread = jnp.where((qa & (k - 1)) == (la & (k - 1)), col_q, 0.0).astype(BF16)
    gather = one_hot((iota((n, s), 1) >> log2(k)) == iota((n, s), 0))
    cols = dot(gather, spread)
    at = p.ru + p.rb
    for r in range(n):
        out[r, at : at + 1, :] = cols[r : r + 1]
    b_copy.wait()
    sends = [
        pltpu.make_async_copy(b_ref.at[0:2, zc - 1], up_hbm, sems.at[5]),
        pltpu.make_async_copy(b_ref.at[0:2, 0], down_hbm, sems.at[6]),
        pltpu.make_async_copy(b_ref.at[2, zc - 1], up2_hbm, sems.at[11]),
        pltpu.make_async_copy(b_ref.at[2, 0], down2_hbm, sems.at[12]),
    ]
    for c in range(3):
        for z in range(zc):
            for h in range(p.wrap):
                at = (c * zc + z) * p.wrap + h
                w = slice(h * p.area, (h + 1) * p.area)
                last[at : at + 1, :] = b_ref[c, z, p.ny - 1 : p.ny, w]
                first[at : at + 1, :] = b_ref[c, z, 0:1, w]
    nxt = lax.rem(me + 1, n)
    for r in range(n):
        out[r, p.ru : p.ru + p.rb, :] = jnp.where(r == nxt, last[: p.rb], first[: p.rb])
    tail = pl.ds(p.ru, p.r1 - p.ru)
    sends.append(pltpu.make_async_copy(out.at[:, tail, :], out_hbm.at[:, tail, :], sems.at[7]))
    for send in sends:
        send.start()
    averages = []
    m = zc * s
    ws = [slice(h * half_fine, (h + 1) * half_fine) for h in range(2)]
    for c in range(3):
        v_copies[c].wait()
        z_sum = jnp.concatenate([v_ref[c, 2 * z] + v_ref[c, 2 * z + 1] for z in range(zc)], axis=0)
        hi, lo = split(z_sum)
        o = dot(jnp.concatenate([x[:, w] for w in ws for x in (hi, lo)], axis=0), sel)
        u = [o[2 * h * m : (2 * h + 1) * m] + o[(2 * h + 1) * m : (2 * h + 2) * m] for h in range(2)]
        averages.append(jnp.concatenate(u, axis=1) * 0.125)
    for c in range(3):
        out[:, c * p.rc : (c + 1) * p.rc, :] = select(g, averages[c]).reshape(n, p.rc, p.area)
        rows = pl.ds(c * p.rc, p.rc)
        sends.append(pltpu.make_async_copy(out.at[:, rows, :], out_hbm.at[:, rows, :], sems.at[8 + c]))
        sends[-1].start()
    for send in sends:
        send.wait()


def tile_transpose(p, t):
    g = iota(t.shape, 1) >> log2(p.half)
    t = pltpu.roll(t, 0, 1, stride=p.half, stride_axis=0)
    for b in (1, 2, 4):
        t = jnp.where((g & b) != 0, pltpu.roll(t, 8 - b, 0), t)
    return pltpu.roll(t, 0, 1, stride=p.half, stride_axis=0)


def blocks_to_grid(p, blk):
    rows = []
    for yh in range(p.half // 8):
        rows.append(
            jnp.concatenate(
                [
                    tile_transpose(p, blk[8 * c : 8 * c + 8, 128 * yh : 128 * yh + 128])
                    for c in range(p.bcols // 8)
                ],
                axis=1,
            )
        )
    return jnp.concatenate(rows, axis=0)


def grid_to_blocks(p, grid):
    rows = []
    for c in range(p.bcols // 8):
        rows.append(
            jnp.concatenate(
                [
                    tile_transpose(p, grid[8 * yh : 8 * yh + 8, 128 * c : 128 * c + 128])
                    for yh in range(p.half // 8)
                ],
                axis=1,
            )
        )
    return jnp.concatenate(rows, axis=0)


def x_next(f):
    return pltpu.roll(f, f.shape[1] - 1, 1)


def x_prev(f):
    return pltpu.roll(f, 1, 1)


def y_next(f, halo):
    return jnp.where(iota(f.shape, 0) == f.shape[0] - 1, halo, pltpu.roll(f, f.shape[0] - 1, 0))


def y_prev(f, halo):
    return jnp.where(iota(f.shape, 0) == 0, halo, pltpu.roll(f, 1, 0))


def row_of(p, ref, src, at):
    return jnp.concatenate([ref[src, pl.ds(at + h, 1), :] for h in range(p.wrap)], axis=1)


def interior_kernel(p, b_ref, copy_ref, j_ref, next_ref):
    zero = jnp.zeros((p.ny, p.nx), F32)
    for z in range(p.zc):
        b = [b_ref[c, z] for c in range(3)]
        below = [b_ref[c, z - 1] if z > 0 else zero for c in range(3)]
        above = [b_ref[c, z + 1] if z < p.zc - 1 else zero for c in range(3)]
        south, north = [y_prev(f, 0.0) for f in b], [y_next(f, 0.0) for f in b]
        west, east = [x_prev(f) for f in b], [x_next(f) for f in b]
        j_ref[0, z] = ((north[2] - south[2]) - (above[1] - below[1])) * 0.5
        j_ref[1, z] = ((above[0] - below[0]) - (east[2] - west[2])) * 0.5
        j_ref[2, z] = ((east[1] - west[1]) - (north[0] - south[0])) * 0.5
        for c in range(3):
            lap = below[c] + above[c] + south[c] + north[c] + west[c] + east[c] - 6.0 * b[c]
            next_ref[c, z] = b[c] + 0.05 * lap
            copy_ref[c, z] = b[c]


def edge_rows(p, ref, nxt, prv, at):
    y = iota((p.ny, p.nx), 0)
    north = jnp.where(y == p.ny - 1, row_of(p, ref, nxt, at), 0.0)
    return north, jnp.where(y == 0, row_of(p, ref, prv, at), 0.0)


def field_kernel(p, r_ref, b_ref, j_ref, lo_ref, hi_ref, out, e_ref, up_ref, down_ref, e_rows):
    n, k, zc = p.n, p.k, p.zc
    me = lax.axis_index("xy")
    nxt, prv = lax.rem(me + 1, n), lax.rem(me + n - 1, n)
    b = [[b_ref[c, z] for z in range(zc)] for c in range(3)]
    cols = r_ref[:, p.ru + p.rb, :]
    shape = (n, p.rc, 128)
    col_s = jnp.sum(
        jnp.where((iota(shape, 1) & (k - 1)) == iota(shape, 2), cols[:, None, :128], 0.0), axis=2, keepdims=True
    )
    shape = (n, p.rc, zc * p.bcols)
    lane = iota(shape, 2)
    g = one_hot(
        ((iota(shape, 1) >> log2(k)) == (lane >> log2(p.bcols)))
        & (col_s == mirror(lane & (p.bcols - 1)).astype(F32))
    ).reshape(p.rows, zc * p.bcols)
    force = []
    zero = jnp.zeros((p.ny, p.nx), F32)
    for z in range(zc):
        bz = [b[c][z] for c in range(3)]
        dy = {}
        for c in (0, 2):
            north, south = edge_rows(p, r_ref, nxt, prv, p.ru + (c * zc + z) * p.wrap)
            dy[c] = north - south
        dz = [zero, zero]
        for c in range(2):
            if z == zc - 1:
                dz[c] = dz[c] + hi_ref[c]
            if z == 0:
                dz[c] = dz[c] - lo_ref[c]
        j0 = j_ref[0, z] + (dy[2] - dz[1]) * 0.5
        j1 = j_ref[1, z] + dz[0] * 0.5
        j2 = j_ref[2, z] - dy[0] * 0.5
        force.append([j1 * bz[2] - j2 * bz[1], j2 * bz[0] - j0 * bz[2], j0 * bz[1] - j1 * bz[0]])
    for c in range(3):
        f_blk = jnp.concatenate([grid_to_blocks(p, force[z][c]) for z in range(zc)], axis=0)
        out[:, c * p.rc : (c + 1) * p.rc, :] = select(g, f_blk).reshape(n, p.rc, p.area)
    p_l, z_l, _ = lane_route(p)
    shape = (n, p.rows)
    col_l = jnp.sum(
        jnp.where(iota(shape, 0) == p_l.reshape(1, p.rows), cols[:, : p.rows], 0.0), axis=0, keepdims=True
    )
    shape = (zc, p.bcols, p.rows)
    g = one_hot(
        (iota(shape, 0) == z_l) & (iota(shape, 1).astype(F32) == col_l.reshape(1, 1, p.rows))
    ).reshape(zc * p.bcols, p.rows)
    u = []
    for c in range(3):
        blk = select(g, r_ref[:, c * p.rc : (c + 1) * p.rc, :].reshape(p.rows, p.area))
        u.append([blocks_to_grid(p, blk[z * p.bcols : (z + 1) * p.bcols]) for z in range(zc)])
    for z in range(zc):
        uz, bz = [u[c][z] for c in range(3)], [b[c][z] for c in range(3)]
        ez = [uz[1] * bz[2] - uz[2] * bz[1], uz[2] * bz[0] - uz[0] * bz[2], uz[0] * bz[1] - uz[1] * bz[0]]
        for c in range(3):
            e_ref[c, z] = ez[c]
        if z == zc - 1:
            up_ref[0], up_ref[1] = ez[0], ez[1]
        if z == 0:
            down_ref[0], down_ref[1] = ez[0], ez[1]
        for i, c in enumerate((0, 2)):
            for h in range(p.wrap):
                at = (i * zc + z) * p.wrap + h
                w = slice(h * p.area, (h + 1) * p.area)
                e_rows[0, at : at + 1, :] = ez[c][0:1, w]
                e_rows[1, at : at + 1, :] = ez[c][p.ny - 1 : p.ny, w]
    for r in range(n):
        out[r, p.ru : p.ru + p.re, :] = jnp.where(r == nxt, e_rows[1], e_rows[0])


def local_kernel(p, r_ref, b_ref, lo_ref, hi_ref, lo2_ref, hi2_ref, e_ref, t_ref, next_ref, g3_ref):
    s, k = p.slots, p.k
    _, q_s = send_positions(p, t_ref[...])
    r_l, z_l, j_l = lane_route(p)
    shape = (p.zc, s, p.rows)
    g3 = (iota(shape, 0) == z_l) & (q_s.reshape(1, s, 1) == (r_l * k + j_l).astype(F32))
    g3_ref[...] = one_hot(g3).reshape(p.zc * s, p.rows)
    n, zc = p.n, p.zc
    me = lax.axis_index("xy")
    nxt, prv = lax.rem(me + 1, n), lax.rem(me + n - 1, n)
    zero = jnp.zeros((p.ny, p.nx), F32)
    for z in range(zc):
        e = [e_ref[c, z] for c in range(3)]
        above = [e_ref[c, z + 1] if z < zc - 1 else zero for c in range(2)]
        below = [e_ref[c, z - 1] if z > 0 else zero for c in range(2)]
        curl = [
            (y_next(e[2], 0.0) - y_prev(e[2], 0.0)) - (above[1] - below[1]),
            (above[0] - below[0]) - (x_next(e[2]) - x_prev(e[2])),
            (x_next(e[1]) - x_prev(e[1])) - (y_next(e[0], 0.0) - y_prev(e[0], 0.0)),
        ]
        for c in range(3):
            north, south = edge_rows(p, r_ref, nxt, prv, p.ru + (c * zc + z) * p.wrap)
            total = curl[c] + north + south
            if z == 0:
                total = total + (lo_ref[c] if c < 2 else lo2_ref[...])
            if z == zc - 1:
                total = total + (hi_ref[c] if c < 2 else hi2_ref[...])
            next_ref[c, z] = b_ref[c, z] + 0.05 * total


def finish_kernel(p, r_ref, g_ref, v_ref, n_ref, lo_ref, hi_ref, vel_hbm, mag_hbm, vel, mag, sems):
    n, zc = p.n, p.zc
    half_fine = p.edge * p.edge // 2
    half_area = p.area // 2
    ex = log2(p.edge)
    c, f = iota((half_area, half_fine), 0), iota((half_area, half_fine), 1)
    coarse = ((f >> (ex + 1)) << (ex - 1)) + ((f & (p.edge - 1)) >> 1)
    sel = one_hot(coarse == c)
    sel = jnp.concatenate([sel, sel], axis=0)
    g = g_ref[...]
    ws = [slice(h * half_area, (h + 1) * half_area) for h in range(2)]
    s = p.slots
    m = zc * s
    copies = []
    for c in range(3):
        hi, lo = split(r_ref[:, c * p.rc : (c + 1) * p.rc, :].reshape(p.rows, p.area) * 0.1)
        parts = dot(g, jnp.concatenate([hi, lo], axis=1)).astype(BF16)
        hi, lo = parts[:, : p.area], parts[:, p.area :]
        pairs = [jnp.concatenate([hi[:, w], lo[:, w]], axis=1) for w in ws]
        add = dot(jnp.concatenate(pairs, axis=0), sel)
        for z in range(zc):
            for h in range(2):
                fw = slice(h * half_fine, (h + 1) * half_fine)
                part = add[h * m + z * s : h * m + (z + 1) * s]
                for d in range(2):
                    vel[c, 2 * z + d, :, fw] = v_ref[c, 2 * z + d, :, fw] + part
        copies.append(pltpu.make_async_copy(vel.at[c], vel_hbm.at[c], sems.at[c]))
        copies[-1].start()
    me = lax.axis_index("xy")
    nxt, prv = lax.rem(me + 1, n), lax.rem(me + n - 1, n)

    def dy(i, z):
        north, south = edge_rows(p, r_ref, nxt, prv, p.ru + (i * zc + z) * p.wrap)
        return north - south

    for z in range(zc):
        dz = [jnp.zeros((p.ny, p.nx), F32)] * 2
        if z == zc - 1:
            dz = [dz[c] + hi_ref[c] for c in range(2)]
        if z == 0:
            dz = [dz[c] - lo_ref[c] for c in range(2)]
        mag[0, z] = n_ref[0, z] + 0.05 * (dy(1, z) - dz[1])
        mag[1, z] = n_ref[1, z] + 0.05 * dz[0]
        mag[2, z] = n_ref[2, z] - 0.05 * dy(0, z)
    copies.append(pltpu.make_async_copy(mag, mag_hbm, sems.at[3]))
    copies[-1].start()
    for copy in copies:
        copy.wait()


def struct(*shape, dtype=F32):
    return jax.ShapeDtypeStruct(shape, dtype)


def call(kernel, ins, outs, scratch=(), grant=20 << 20):
    return pl.pallas_call(
        kernel,
        out_shape=[o for o, _ in outs],
        in_specs=ins,
        out_specs=[spec for _, spec in outs],
        scratch_shapes=list(scratch),
        cost_estimate=pl.CostEstimate(flops=1 << 24, bytes_accessed=1 << 20, transcendentals=0),
        compiler_params=pltpu.CompilerParams(vmem_limit_bytes=grant),
    )


def ring(axis, step):
    n = lax.axis_size(axis)
    return [(i, (i + step) % n) for i in range(n)]


def planes(up, down):
    below = lax.ppermute(up, "gz", ring("gz", 1))
    above = lax.ppermute(down, "gz", ring("gz", -1))
    return below, above


def body(velocity, magnetic, slot_block_table):
    p = Plan(velocity.shape, magnetic.shape, lax.axis_size("xy"))
    plane = (p.ny, p.nx)
    dma = pltpu.SemaphoreType.DMA
    table = slot_block_table.reshape(1, p.slots)
    sent, up, down, up2, down2 = call(
        functools.partial(restrict_kernel, p),
        [HBM] * 3,
        [(struct(p.n, p.r1, p.area), HBM)] + [(struct(2, *plane), HBM)] * 2 + [(struct(*plane), HBM)] * 2,
        [
            pltpu.VMEM(velocity.shape, F32),
            pltpu.VMEM((1, p.slots), jnp.int32),
            pltpu.VMEM(magnetic.shape, F32),
            pltpu.VMEM((p.n, p.r1, p.area), F32),
            pltpu.VMEM((-(-p.rb // 8) * 8, p.area), F32),
            pltpu.VMEM((-(-p.rb // 8) * 8, p.area), F32),
            dma((13,)),
        ],
        ALL_VMEM,
    )(velocity, table, magnetic)
    got = lax.all_to_all(sent, "xy", 0, 0, tiled=True)
    below, above = planes(up, down)
    below2, above2 = planes(up2, down2)
    held, _ = lax.optimization_barrier((magnetic, up))
    field, current, diffused = call(
        functools.partial(interior_kernel, p), [VMEM], [(struct(*magnetic.shape), VMEM)] * 3
    )(held)
    sent, emf, up, down = call(
        functools.partial(field_kernel, p),
        [VMEM] * 5,
        [
            (struct(p.n, p.r2, p.area), VMEM),
            (struct(*magnetic.shape), VMEM),
            (struct(2, *plane), VMEM),
            (struct(2, *plane), VMEM),
        ],
        [pltpu.VMEM((2, p.re, p.area), F32)],
    )(got, field, current, below, above)
    got_force = lax.all_to_all(sent, "xy", 0, 0, tiled=True)
    emf_below, emf_above = planes(up, down)
    held_table, _ = lax.optimization_barrier((table, up))
    partial, g3 = call(
        functools.partial(local_kernel, p),
        [VMEM] * 8,
        [(struct(*magnetic.shape), VMEM), (struct(p.zc * p.slots, p.rows, dtype=BF16), VMEM)],
    )(got, diffused, below, above, below2, above2, emf, held_table)
    return tuple(
        call(
            functools.partial(finish_kernel, p),
            [VMEM] * 6,
            [(struct(*velocity.shape), HBM), (struct(*magnetic.shape), HBM)],
            [pltpu.VMEM(velocity.shape, F32), pltpu.VMEM(magnetic.shape, F32), dma((4,))],
        )(got_force, g3, velocity, partial, emf_below, emf_above)
    )


def solution(mesh):
    return jax.shard_map(
        body,
        mesh=mesh,
        in_specs=(P(None, "gz", "xy", None), P(None, "gz", "xy", None), P("xy")),
        out_specs=(P(None, "gz", "xy", None), P(None, "gz", "xy", None)),
        check_vma=False,
    )
```

```python
import functools
import math

import jax
import jax.numpy as jnp
from jax import lax
from jax.experimental import pallas as pl
from jax.experimental.pallas import tpu as pltpu
from jax.sharding import PartitionSpec as P

F32, BF16 = jnp.float32, jnp.bfloat16
VMEM = pl.BlockSpec(memory_space=pltpu.VMEM)
ALL_VMEM = 67043328
HBM = pl.BlockSpec(memory_space=pltpu.HBM)


def split(x):
    hi = x.astype(BF16)
    return hi, (x - hi.astype(F32)).astype(BF16)


def dot(a, b):
    return jnp.dot(a, b, preferred_element_type=F32)


def iota(shape, dim):
    return lax.broadcasted_iota(jnp.int32, shape, dim)


def one_hot(mask):
    return jnp.where(mask, 1.0, 0.0).astype(BF16)


def log2(x):
    assert x == 1 << (x.bit_length() - 1)
    return x.bit_length() - 1


class Plan:
    def __init__(self, vshape, bshape, n):
        self.n = n
        self.slots = vshape[2]
        self.k = self.slots // n
        self.zc = bshape[1]
        self.ny, self.nx = bshape[2:]
        self.edge = math.isqrt(vshape[3])
        self.half = self.edge // 2
        self.area = self.half * self.half
        self.bcols = self.nx // self.half
        self.rc = -(-self.zc * self.k // 8) * 8
        self.ru = 3 * self.rc
        self.rows = n * self.rc
        self.rb = 3 * self.zc * self.nx // self.area
        self.r1 = -(-(self.ru + self.rb + 4) // 8) * 8
        self.wrap = self.nx // self.area
        assert self.rc == 8 and self.area == 256 and self.half == 16


def mirror(i):
    return (i & ~7) | ((8 - (i & 7)) & 7)


def send_positions(p, table):
    s = p.slots
    row = jnp.broadcast_to((table >> log2(p.bcols)).astype(F32), (s, s))
    i, j = iota((s, s), 0), iota((s, s), 1)
    row_s = jnp.sum(jnp.where(i == j, row, 0.0), axis=1, keepdims=True)
    rank = jnp.sum(jnp.where((row_s == row) & (i < j), 1.0, 0.0), axis=0, keepdims=True)
    q = row[0:1] * p.k + rank
    q_s = jnp.sum(jnp.where(i == j, jnp.broadcast_to(q, (s, s)), 0.0), axis=1, keepdims=True)
    return q, q_s


def select(g, x):
    hi, lo = split(x)
    out = dot(g, jnp.concatenate([hi, lo], axis=1))
    return out[:, : x.shape[1]] + out[:, x.shape[1] :]


def spin(t):
    return pltpu.roll(t, 0, 1, stride=16, stride_axis=0)


def lay_out(t, first):
    t = spin(t)
    here = (iota(t.shape, 1) >> 4) == ((iota(t.shape, 0) + first) & 7)
    return jnp.sum(jnp.where(here, t, 0.0), axis=0, keepdims=True)


def tile_lanes(x, width):
    return x[:, :width] if width <= 128 else jnp.concatenate([x] * (width // 128), axis=1)


def lane_route(p):
    lane = iota((1, 1, p.rows), 2)
    i = lane & (p.rc - 1)
    return lane >> log2(p.rc), i >> log2(p.k), i & (p.k - 1)


def restrict_kernel(p, v_hbm, t_hbm, b_hbm, out_hbm, up_hbm, down_hbm, v_ref, t_ref, b_ref, out, last, first, sems):
    n, k, s, zc = p.n, p.k, p.slots, p.zc
    me = lax.axis_index("xy")
    t_copy = pltpu.make_async_copy(t_hbm, t_ref, sems.at[0])
    b_copy = pltpu.make_async_copy(b_hbm, b_ref, sems.at[1])
    v_copies = [pltpu.make_async_copy(v_hbm.at[c], v_ref.at[c], sems.at[2 + c]) for c in range(3)]
    t_copy.start()
    b_copy.start()
    for copy in v_copies:
        copy.start()
    half_fine = p.edge * p.edge // 2
    half_area = p.area // 2
    f, c = iota((half_fine, half_area), 0), iota((half_fine, half_area), 1)
    e = log2(p.edge)
    coarse = (mirror(f >> (e + 1)) << (e - 1)) + ((f & (p.edge - 1)) >> 1)
    sel = one_hot(coarse == c)
    t_copy.wait()
    table = t_ref[...]
    q, _ = send_positions(p, table)
    lanes = zc * s
    rep = one_hot((iota((s, lanes), 1) & (s - 1)) == iota((s, lanes), 0))
    qt = dot(jnp.broadcast_to(q, (8, s)).astype(BF16), rep)[0:1]
    shape = (n, p.rc, lanes)
    i = iota(shape, 1)
    target = (iota(shape, 0) * k + (i & (k - 1))).astype(F32)
    g = one_hot(((i >> log2(k)) == (iota(shape, 2) >> log2(s))) & (target == qt.reshape(1, 1, lanes)))
    g = g.reshape(p.rows, lanes)
    col = jnp.broadcast_to((table & (p.bcols - 1)).astype(F32), (s, s))
    qi = iota((s, s), 0).astype(F32)
    col_q = jnp.sum(jnp.where(qi == jnp.broadcast_to(q, (s, s)), col, 0.0), axis=1, keepdims=True)
    qa, la = iota((s, p.area), 0), iota((s, p.area), 1)
    place = jnp.where(la < 128, la, jnp.where(la < 192, -la, -1 - la)) & (k - 1)
    spread = jnp.where((qa & (k - 1)) == place, col_q, 0.0).astype(BF16)
    gather = one_hot((iota((n, s), 1) >> log2(k)) == iota((n, s), 0))
    cols = dot(gather, spread)
    at = p.ru + p.rb
    for r in range(n):
        north, south = (r + 1) % n, (r - 1) % n
        out[r, at : at + 1, :128] = cols[r : r + 1, :128]
        outer = jnp.where(iota((1, 128), 1) < 64, cols[north : north + 1, 128:], cols[south : south + 1, 128:])
        out[r, at : at + 1, 128:] = outer
    b_copy.wait()
    sends = [
        pltpu.make_async_copy(b_ref.at[0:2, zc - 1], up_hbm, sems.at[5]),
        pltpu.make_async_copy(b_ref.at[0:2, 0], down_hbm, sems.at[6]),
    ]
    for c in range(3):
        for z in range(zc):
            for h in range(p.wrap):
                at = (c * zc + z) * p.wrap + h
                w = slice(h * p.area, (h + 1) * p.area)
                last[at : at + 1, :] = b_ref[c, z, p.ny - 1 : p.ny, w]
                first[at : at + 1, :] = b_ref[c, z, 0:1, w]
    nxt = lax.rem(me + 1, n)
    for r in range(n):
        out[r, p.ru : p.ru + p.rb, :] = jnp.where(r == nxt, last[: p.rb], first[: p.rb])
    early = pl.ds(p.ru, 8)
    sends.append(pltpu.make_async_copy(out.at[:, early, :], out_hbm.at[:, early, :], sems.at[7]))
    for send in sends:
        send.start()
    averages = []
    m = zc * s
    ws = [slice(h * half_fine, (h + 1) * half_fine) for h in range(2)]
    for c in range(3):
        v_copies[c].wait()
        z_sum = jnp.concatenate([v_ref[c, 2 * z] + v_ref[c, 2 * z + 1] for z in range(zc)], axis=0)
        hi, lo = split(z_sum)
        o = dot(jnp.concatenate([x[:, w] for w in ws for x in (hi, lo)], axis=0), sel)
        u = [o[2 * h * m : (2 * h + 1) * m] + o[(2 * h + 1) * m : (2 * h + 2) * m] for h in range(2)]
        averages.append(jnp.concatenate(u, axis=1) * 0.125)
    for c in range(3):
        blocks = select(g, averages[c])
        out[:, c * p.rc : (c + 1) * p.rc, :] = blocks.reshape(n, p.rc, p.area)
        rows = pl.ds(c * p.rc, p.rc)
        sends.append(pltpu.make_async_copy(out.at[:, rows, :], out_hbm.at[:, rows, :], sems.at[8 + c]))
        sends[-1].start()
        at = p.ru + p.rb + 1 + c
        for r in range(n):
            tile = blocks[r * p.rc : (r + 1) * p.rc]
            out[(r - 1) % n, at : at + 1, :128] = lay_out(tile[:, :128], 0)
            out[(r + 1) % n, at : at + 1, 128:] = lay_out(tile[:, 128:], 1)
    late = pl.ds(p.ru + 8, p.r1 - p.ru - 8)
    sends.append(pltpu.make_async_copy(out.at[:, late, :], out_hbm.at[:, late, :], sems.at[11]))
    sends[-1].start()
    for send in sends:
        send.wait()


def tile_transpose(p, t):
    g = iota(t.shape, 1) >> log2(p.half)
    t = pltpu.roll(t, 0, 1, stride=p.half, stride_axis=0)
    for b in (1, 2, 4):
        t = jnp.where((g & b) != 0, pltpu.roll(t, 8 - b, 0), t)
    return pltpu.roll(t, 0, 1, stride=p.half, stride_axis=0)


def blocks_to_grid(p, blk):
    rows = []
    for yh in range(p.half // 8):
        rows.append(
            jnp.concatenate(
                [
                    tile_transpose(p, blk[8 * c : 8 * c + 8, 128 * yh : 128 * yh + 128])
                    for c in range(p.bcols // 8)
                ],
                axis=1,
            )
        )
    return jnp.concatenate(rows, axis=0)


def grid_to_blocks(p, grid):
    rows = []
    for c in range(p.bcols // 8):
        rows.append(
            jnp.concatenate(
                [
                    tile_transpose(p, grid[8 * yh : 8 * yh + 8, 128 * c : 128 * c + 128])
                    for yh in range(p.half // 8)
                ],
                axis=1,
            )
        )
    return jnp.concatenate(rows, axis=0)


def x_next(f):
    return pltpu.roll(f, f.shape[1] - 1, 1)


def x_prev(f):
    return pltpu.roll(f, 1, 1)


def y_next(f, halo):
    return jnp.where(iota(f.shape, 0) == f.shape[0] - 1, halo, pltpu.roll(f, f.shape[0] - 1, 0))


def y_prev(f, halo):
    return jnp.where(iota(f.shape, 0) == 0, halo, pltpu.roll(f, 1, 0))


def row_of(p, ref, src, at):
    return jnp.concatenate([ref[src, pl.ds(at + h, 1), :] for h in range(p.wrap)], axis=1)


def interior_kernel(p, b_ref, t_ref, copy_ref, j_ref, next_ref, g3_ref):
    s, k = p.slots, p.k
    _, q_s = send_positions(p, t_ref[...])
    r_l, z_l, j_l = lane_route(p)
    shape = (p.zc, s, p.rows)
    g3 = (iota(shape, 0) == z_l) & (q_s.reshape(1, s, 1) == (r_l * k + j_l).astype(F32))
    g3_ref[...] = one_hot(g3).reshape(p.zc * s, p.rows)
    zero = jnp.zeros((p.ny, p.nx), F32)
    for z in range(p.zc):
        b = [b_ref[c, z] for c in range(3)]
        below = [b_ref[c, z - 1] if z > 0 else zero for c in range(3)]
        above = [b_ref[c, z + 1] if z < p.zc - 1 else zero for c in range(3)]
        south, north = [y_prev(f, 0.0) for f in b], [y_next(f, 0.0) for f in b]
        west, east = [x_prev(f) for f in b], [x_next(f) for f in b]
        j_ref[0, z] = ((north[2] - south[2]) - (above[1] - below[1])) * 0.5
        j_ref[1, z] = ((above[0] - below[0]) - (east[2] - west[2])) * 0.5
        j_ref[2, z] = ((east[1] - west[1]) - (north[0] - south[0])) * 0.5
        for c in range(3):
            lap = below[c] + above[c] + south[c] + north[c] + west[c] + east[c] - 6.0 * b[c]
            next_ref[c, z] = b[c] + 0.05 * lap
            copy_ref[c, z] = b[c]


def edge_rows(p, ref, nxt, prv, at):
    y = iota((p.ny, p.nx), 0)
    north = jnp.where(y == p.ny - 1, row_of(p, ref, nxt, at), 0.0)
    return north, jnp.where(y == 0, row_of(p, ref, prv, at), 0.0)


def field_kernel(p, r_ref, b_ref, j_ref, lo_ref, hi_ref, out, e_ref, up_ref, down_ref):
    n, k, zc = p.n, p.k, p.zc
    me = lax.axis_index("xy")
    nxt, prv = lax.rem(me + 1, n), lax.rem(me + n - 1, n)
    b = [[b_ref[c, z] for z in range(zc)] for c in range(3)]
    cols = r_ref[:, p.ru + p.rb, :]
    shape = (n, p.rc, 128)
    col_s = jnp.sum(
        jnp.where((iota(shape, 1) & (k - 1)) == iota(shape, 2), cols[:, None, :128], 0.0), axis=2, keepdims=True
    )
    shape = (n, p.rc, zc * p.bcols)
    lane = iota(shape, 2)
    g = one_hot(
        ((iota(shape, 1) >> log2(k)) == (lane >> log2(p.bcols)))
        & (col_s == mirror(lane & (p.bcols - 1)).astype(F32))
    ).reshape(p.rows, zc * p.bcols)
    force = []
    zero = jnp.zeros((p.ny, p.nx), F32)
    for z in range(zc):
        bz = [b[c][z] for c in range(3)]
        dy = {}
        for c in (0, 2):
            north, south = edge_rows(p, r_ref, nxt, prv, p.ru + (c * zc + z) * p.wrap)
            dy[c] = north - south
        dz = [zero, zero]
        for c in range(2):
            if z == zc - 1:
                dz[c] = dz[c] + hi_ref[c]
            if z == 0:
                dz[c] = dz[c] - lo_ref[c]
        j0 = j_ref[0, z] + (dy[2] - dz[1]) * 0.5
        j1 = j_ref[1, z] + dz[0] * 0.5
        j2 = j_ref[2, z] - dy[0] * 0.5
        force.append([j1 * bz[2] - j2 * bz[1], j2 * bz[0] - j0 * bz[2], j0 * bz[1] - j1 * bz[0]])
    for c in range(3):
        f_blk = jnp.concatenate([grid_to_blocks(p, force[z][c]) for z in range(zc)], axis=0)
        out[:, c * p.rc : (c + 1) * p.rc, :] = select(g, f_blk).reshape(n, p.rc, p.area)
    p_l, z_l, _ = lane_route(p)
    shape = (n, p.rows)
    col_l = jnp.sum(
        jnp.where(iota(shape, 0) == p_l.reshape(1, p.rows), tile_lanes(cols[:, :128], p.rows), 0.0), axis=0, keepdims=True
    )
    shape = (zc, p.bcols, p.rows)
    g = one_hot(
        (iota(shape, 0) == z_l) & (iota(shape, 1).astype(F32) == col_l.reshape(1, 1, p.rows))
    ).reshape(zc * p.bcols, p.rows)
    u = []
    for c in range(3):
        blk = select(g, r_ref[:, c * p.rc : (c + 1) * p.rc, :].reshape(p.rows, p.area))
        u.append([blocks_to_grid(p, blk[z * p.bcols : (z + 1) * p.bcols]) for z in range(zc)])
    for z in range(zc):
        uz, bz = [u[c][z] for c in range(3)], [b[c][z] for c in range(3)]
        ez = [uz[1] * bz[2] - uz[2] * bz[1], uz[2] * bz[0] - uz[0] * bz[2], uz[0] * bz[1] - uz[1] * bz[0]]
        for c in range(3):
            e_ref[c, z] = ez[c]
        if z == zc - 1:
            up_ref[0], up_ref[1], up_ref[2] = ez[0], ez[1], bz[2]
        if z == 0:
            down_ref[0], down_ref[1], down_ref[2] = ez[0], ez[1], bz[2]


def outer_velocity(p, r_ref):
    n, zc = p.n, p.zc
    at = p.ru + p.rb
    x = r_ref[:, at, :][:, 128:]
    spun = pltpu.roll(x, 64, 1)
    low = iota(x.shape, 1) < 64
    lane = iota((1, 1, p.rows), 2)
    place = lane & 7
    shape = (zc, p.bcols, p.rows)
    sides = []
    for d, (cols, i) in enumerate(((jnp.where(low, x, spun), (8 - place) & 7), (jnp.where(low, spun, x), 7 - place))):
        device = iota((n, p.rows), 0) == (lane >> 3).reshape(1, p.rows)
        col = jnp.sum(jnp.where(device, tile_lanes(cols, p.rows), 0.0), axis=0, keepdims=True)
        g = one_hot(
            (iota(shape, 0) == (i >> log2(p.k))) & (iota(shape, 1).astype(F32) == col.reshape(1, 1, p.rows))
        ).reshape(zc * p.bcols, p.rows)
        parts = []
        for c in range(3):
            m = r_ref[:, at + 1 + c, :][:, 128 * d : 128 * d + 128]
            parts.append(jnp.concatenate([spin(jnp.broadcast_to(m[r : r + 1], (8, 128))) for r in range(n)], axis=0))
        o = select(g, jnp.concatenate(parts, axis=1))
        side = []
        for c in range(3):
            blocks = o[:, 128 * c : 128 * c + 128]
            row = [lay_out(blocks[8 * t : 8 * t + 8], 0) for t in range(zc * p.bcols // 8)]
            per = p.bcols // 8
            side.append([jnp.concatenate(row[z * per : (z + 1) * per], axis=1) for z in range(zc)])
        sides.append(side)
    return sides


def local_kernel(p, r_ref, b_ref, lo_ref, hi_ref, e_ref, next_ref):
    n, zc = p.n, p.zc
    me = lax.axis_index("xy")
    nxt, prv = lax.rem(me + 1, n), lax.rem(me + n - 1, n)
    zero = jnp.zeros((p.ny, p.nx), F32)
    outer_u = outer_velocity(p, r_ref)
    for z in range(zc):
        e = [e_ref[c, z] for c in range(3)]
        e0, e2 = [], []
        for u, device in zip(outer_u, (nxt, prv)):
            b = [row_of(p, r_ref, device, p.ru + (c * zc + z) * p.wrap) for c in range(3)]
            e0.append(u[1][z] * b[2] - u[2][z] * b[1])
            e2.append(u[0][z] * b[1] - u[1][z] * b[0])
        above = [e_ref[c, z + 1] if z < zc - 1 else zero for c in range(2)]
        below = [e_ref[c, z - 1] if z > 0 else zero for c in range(2)]
        curl = [
            (y_next(e[2], e2[0]) - y_prev(e[2], e2[1])) - (above[1] - below[1]),
            (above[0] - below[0]) - (x_next(e[2]) - x_prev(e[2])),
            (x_next(e[1]) - x_prev(e[1])) - (y_next(e[0], e0[0]) - y_prev(e[0], e0[1])),
        ]
        for c in range(3):
            north, south = edge_rows(p, r_ref, nxt, prv, p.ru + (c * zc + z) * p.wrap)
            total = curl[c] + north + south
            if c < 2 and z == 0:
                total = total + lo_ref[c]
            if c < 2 and z == zc - 1:
                total = total + hi_ref[c]
            next_ref[c, z] = b_ref[c, z] + 0.05 * total


def widen_kernel(p, r_ref, g_ref, v_ref, vel_hbm, vel, sems):
    zc = p.zc
    half_fine = p.edge * p.edge // 2
    half_area = p.area // 2
    ex = log2(p.edge)
    c, f = iota((half_area, half_fine), 0), iota((half_area, half_fine), 1)
    coarse = ((f >> (ex + 1)) << (ex - 1)) + ((f & (p.edge - 1)) >> 1)
    sel = one_hot(coarse == c)
    sel = jnp.concatenate([sel, sel], axis=0)
    g = g_ref[...]
    ws = [slice(h * half_area, (h + 1) * half_area) for h in range(2)]
    s = p.slots
    m = zc * s
    copies = []
    for c in range(3):
        hi, lo = split(r_ref[:, c * p.rc : (c + 1) * p.rc, :].reshape(p.rows, p.area) * 0.1)
        parts = dot(g, jnp.concatenate([hi, lo], axis=1)).astype(BF16)
        hi, lo = parts[:, : p.area], parts[:, p.area :]
        pairs = [jnp.concatenate([hi[:, w], lo[:, w]], axis=1) for w in ws]
        add = dot(jnp.concatenate(pairs, axis=0), sel)
        for z in range(zc):
            for h in range(2):
                fw = slice(h * half_fine, (h + 1) * half_fine)
                part = add[h * m + z * s : h * m + (z + 1) * s]
                for d in range(2):
                    vel[c, 2 * z + d, :, fw] = v_ref[c, 2 * z + d, :, fw] + part
        copies.append(pltpu.make_async_copy(vel.at[c], vel_hbm.at[c], sems.at[c]))
        copies[-1].start()
    for copy in copies:
        copy.wait()


def finish_kernel(p, n_ref, lo_ref, hi_ref, mag):
    zc = p.zc
    for z in range(zc):
        dz = [jnp.zeros((p.ny, p.nx), F32)] * 2
        outer = dz[0]
        if z == zc - 1:
            dz = [dz[c] + hi_ref[c] for c in range(2)]
            outer = outer + hi_ref[2]
        if z == 0:
            dz = [dz[c] - lo_ref[c] for c in range(2)]
            outer = outer + lo_ref[2]
        mag[0, z] = n_ref[0, z] + 0.05 * -dz[1]
        mag[1, z] = n_ref[1, z] + 0.05 * dz[0]
        mag[2, z] = n_ref[2, z] + 0.05 * outer


def struct(*shape, dtype=F32):
    return jax.ShapeDtypeStruct(shape, dtype)


def call(kernel, ins, outs, scratch=(), grant=20 << 20):
    return pl.pallas_call(
        kernel,
        out_shape=[o for o, _ in outs],
        in_specs=ins,
        out_specs=[spec for _, spec in outs],
        scratch_shapes=list(scratch),
        cost_estimate=pl.CostEstimate(flops=1 << 24, bytes_accessed=1 << 20, transcendentals=0),
        compiler_params=pltpu.CompilerParams(vmem_limit_bytes=grant),
    )


def ring(axis, step):
    n = lax.axis_size(axis)
    return [(i, (i + step) % n) for i in range(n)]


def planes(up, down):
    below = lax.ppermute(up, "gz", ring("gz", 1))
    above = lax.ppermute(down, "gz", ring("gz", -1))
    return below, above


def body(velocity, magnetic, slot_block_table):
    p = Plan(velocity.shape, magnetic.shape, lax.axis_size("xy"))
    plane = (p.ny, p.nx)
    dma = pltpu.SemaphoreType.DMA
    table = slot_block_table.reshape(1, p.slots)
    sent, up, down = call(
        functools.partial(restrict_kernel, p),
        [HBM] * 3,
        [(struct(p.n, p.r1, p.area), HBM), (struct(2, *plane), HBM), (struct(2, *plane), HBM)],
        [
            pltpu.VMEM(velocity.shape, F32),
            pltpu.VMEM((1, p.slots), jnp.int32),
            pltpu.VMEM(magnetic.shape, F32),
            pltpu.VMEM((p.n, p.r1, p.area), F32),
            pltpu.VMEM((-(-p.rb // 8) * 8, p.area), F32),
            pltpu.VMEM((-(-p.rb // 8) * 8, p.area), F32),
            dma((12,)),
        ],
        ALL_VMEM,
    )(velocity, table, magnetic)
    got = lax.all_to_all(sent, "xy", 0, 0, tiled=True)
    below, above = planes(up, down)
    held, held_table, _ = lax.optimization_barrier((magnetic, table, up))
    field, current, diffused, g3 = call(
        functools.partial(interior_kernel, p),
        [VMEM] * 2,
        [(struct(*magnetic.shape), VMEM)] * 3 + [(struct(p.zc * p.slots, p.rows, dtype=BF16), VMEM)],
    )(held, held_table)
    sent, emf, up, down = call(
        functools.partial(field_kernel, p),
        [VMEM] * 5,
        [
            (struct(p.n, p.ru, p.area), VMEM),
            (struct(*magnetic.shape), VMEM),
            (struct(3, *plane), VMEM),
            (struct(3, *plane), VMEM),
        ],
    )(got, field, current, below, above)
    got_force = lax.all_to_all(sent, "xy", 0, 0, tiled=True)
    emf_below, emf_above = planes(up, down)
    (partial,) = call(
        functools.partial(local_kernel, p), [VMEM] * 5, [(struct(*magnetic.shape), VMEM)]
    )(got, diffused, below, above, emf)
    (updated,) = call(
        functools.partial(widen_kernel, p),
        [VMEM] * 3,
        [(struct(*velocity.shape), HBM)],
        [pltpu.VMEM(velocity.shape, F32), dma((3,))],
    )(got_force, g3, velocity)
    partial, _ = lax.optimization_barrier((partial, updated))
    (finished,) = call(
        functools.partial(finish_kernel, p), [VMEM] * 3, [(struct(*magnetic.shape), VMEM)]
    )(partial, emf_below, emf_above)
    return updated, finished


def solution(mesh):
    return jax.shard_map(
        body,
        mesh=mesh,
        in_specs=(P(None, "gz", "xy", None), P(None, "gz", "xy", None), P("xy")),
        out_specs=(P(None, "gz", "xy", None), P(None, "gz", "xy", None)),
        check_vma=False,
    )
```

```python
import functools
import math

import jax
import jax.numpy as jnp
from jax import lax
from jax.experimental import pallas as pl
from jax.experimental.pallas import tpu as pltpu
from jax.sharding import PartitionSpec as P

F32, BF16 = jnp.float32, jnp.bfloat16
VMEM = pl.BlockSpec(memory_space=pltpu.VMEM)
ALL_VMEM = 67043328
HBM = pl.BlockSpec(memory_space=pltpu.HBM)


def split(x):
    hi = x.astype(BF16)
    return hi, (x - hi.astype(F32)).astype(BF16)


def dot(a, b):
    return jnp.dot(a, b, preferred_element_type=F32)


def iota(shape, dim):
    return lax.broadcasted_iota(jnp.int32, shape, dim)


def one_hot(mask):
    return jnp.where(mask, 1.0, 0.0).astype(BF16)


def log2(x):
    assert x == 1 << (x.bit_length() - 1)
    return x.bit_length() - 1


class Plan:
    def __init__(self, vshape, bshape, n):
        self.n = n
        self.slots = vshape[2]
        self.k = self.slots // n
        self.zc = bshape[1]
        self.ny, self.nx = bshape[2:]
        self.edge = math.isqrt(vshape[3])
        self.half = self.edge // 2
        self.area = self.half * self.half
        self.bcols = self.nx // self.half
        self.rc = -(-self.zc * self.k // 8) * 8
        self.ru = 3 * self.rc
        self.rows = n * self.rc
        self.rb = 3 * self.zc * self.nx // self.area
        self.r1 = -(-(self.ru + self.rb + 4) // 8) * 8
        self.wrap = self.nx // self.area
        assert self.rc == 8 and self.area == 256 and self.half == 16


def mirror(i):
    return (i & ~7) | ((8 - (i & 7)) & 7)


def send_positions(p, table):
    s = p.slots
    row = jnp.broadcast_to((table >> log2(p.bcols)).astype(F32), (s, s))
    i, j = iota((s, s), 0), iota((s, s), 1)
    row_s = jnp.sum(jnp.where(i == j, row, 0.0), axis=1, keepdims=True)
    rank = jnp.sum(jnp.where((row_s == row) & (i < j), 1.0, 0.0), axis=0, keepdims=True)
    q = row[0:1] * p.k + rank
    q_s = jnp.sum(jnp.where(i == j, jnp.broadcast_to(q, (s, s)), 0.0), axis=1, keepdims=True)
    return q, q_s


def select(g, x):
    hi, lo = split(x)
    out = dot(g, jnp.concatenate([hi, lo], axis=1))
    return out[:, : x.shape[1]] + out[:, x.shape[1] :]


def spin(t):
    return pltpu.roll(t, 0, 1, stride=16, stride_axis=0)


def lay_out(t, first):
    t = spin(t)
    here = (iota(t.shape, 1) >> 4) == ((iota(t.shape, 0) + first) & 7)
    return jnp.sum(jnp.where(here, t, 0.0), axis=0, keepdims=True)


def tile_lanes(x, width):
    return x[:, :width] if width <= 128 else jnp.concatenate([x] * (width // 128), axis=1)


def lane_route(p):
    lane = iota((1, 1, p.rows), 2)
    i = lane & (p.rc - 1)
    return lane >> log2(p.rc), i >> log2(p.k), i & (p.k - 1)


def restrict_kernel(p, v_hbm, t_hbm, b_hbm, out_hbm, up_hbm, down_hbm, v_ref, t_ref, b_ref, out, last, first, sems):
    n, k, s, zc = p.n, p.k, p.slots, p.zc
    me = lax.axis_index("xy")
    t_copy = pltpu.make_async_copy(t_hbm, t_ref, sems.at[0])
    b_copy = pltpu.make_async_copy(b_hbm, b_ref, sems.at[1])
    v_copies = [pltpu.make_async_copy(v_hbm.at[c], v_ref.at[c], sems.at[2 + c]) for c in range(3)]
    t_copy.start()
    b_copy.start()
    for copy in v_copies:
        copy.start()
    half_fine = p.edge * p.edge // 2
    half_area = p.area // 2
    f, c = iota((half_fine, half_area), 0), iota((half_fine, half_area), 1)
    e = log2(p.edge)
    coarse = (mirror(f >> (e + 1)) << (e - 1)) + ((f & (p.edge - 1)) >> 1)
    sel = one_hot(coarse == c)
    t_copy.wait()
    table = t_ref[...]
    q, _ = send_positions(p, table)
    lanes = zc * s
    rep = one_hot((iota((s, lanes), 1) & (s - 1)) == iota((s, lanes), 0))
    qt = dot(jnp.broadcast_to(q, (8, s)).astype(BF16), rep)[0:1]
    shape = (n, p.rc, lanes)
    i = iota(shape, 1)
    target = (iota(shape, 0) * k + (i & (k - 1))).astype(F32)
    g = one_hot(((i >> log2(k)) == (iota(shape, 2) >> log2(s))) & (target == qt.reshape(1, 1, lanes)))
    g = g.reshape(p.rows, lanes)
    col = jnp.broadcast_to((table & (p.bcols - 1)).astype(F32), (s, s))
    qi = iota((s, s), 0).astype(F32)
    col_q = jnp.sum(jnp.where(qi == jnp.broadcast_to(q, (s, s)), col, 0.0), axis=1, keepdims=True)
    qa, la = iota((s, p.area), 0), iota((s, p.area), 1)
    place = jnp.where(la < 128, la, jnp.where(la < 192, -la, -1 - la)) & (k - 1)
    spread = jnp.where((qa & (k - 1)) == place, col_q, 0.0).astype(BF16)
    gather = one_hot((iota((n, s), 1) >> log2(k)) == iota((n, s), 0))
    cols = dot(gather, spread)
    at = p.ru + p.rb
    for r in range(n):
        north, south = (r + 1) % n, (r - 1) % n
        out[r, at : at + 1, :128] = cols[r : r + 1, :128]
        outer = jnp.where(iota((1, 128), 1) < 64, cols[north : north + 1, 128:], cols[south : south + 1, 128:])
        out[r, at : at + 1, 128:] = outer
    b_copy.wait()
    sends = [
        pltpu.make_async_copy(b_ref.at[0:2, zc - 1], up_hbm, sems.at[5]),
        pltpu.make_async_copy(b_ref.at[0:2, 0], down_hbm, sems.at[6]),
    ]
    for c in range(3):
        for z in range(zc):
            for h in range(p.wrap):
                at = (c * zc + z) * p.wrap + h
                w = slice(h * p.area, (h + 1) * p.area)
                last[at : at + 1, :] = b_ref[c, z, p.ny - 1 : p.ny, w]
                first[at : at + 1, :] = b_ref[c, z, 0:1, w]
    nxt = lax.rem(me + 1, n)
    for r in range(n):
        out[r, p.ru : p.ru + p.rb, :] = jnp.where(r == nxt, last[: p.rb], first[: p.rb])
    early = pl.ds(p.ru, 8)
    sends.append(pltpu.make_async_copy(out.at[:, early, :], out_hbm.at[:, early, :], sems.at[7]))
    for send in sends:
        send.start()
    averages = []
    m = zc * s
    ws = [slice(h * half_fine, (h + 1) * half_fine) for h in range(2)]
    for c in range(3):
        v_copies[c].wait()
        z_sum = jnp.concatenate([v_ref[c, 2 * z] + v_ref[c, 2 * z + 1] for z in range(zc)], axis=0)
        hi, lo = split(z_sum)
        o = dot(jnp.concatenate([x[:, w] for w in ws for x in (hi, lo)], axis=0), sel)
        u = [o[2 * h * m : (2 * h + 1) * m] + o[(2 * h + 1) * m : (2 * h + 2) * m] for h in range(2)]
        averages.append(jnp.concatenate(u, axis=1) * 0.125)
    for c in range(3):
        blocks = select(g, averages[c])
        out[:, c * p.rc : (c + 1) * p.rc, :] = blocks.reshape(n, p.rc, p.area)
        rows = pl.ds(c * p.rc, p.rc)
        sends.append(pltpu.make_async_copy(out.at[:, rows, :], out_hbm.at[:, rows, :], sems.at[8 + c]))
        sends[-1].start()
        at = p.ru + p.rb + 1 + c
        for r in range(n):
            tile = blocks[r * p.rc : (r + 1) * p.rc]
            out[(r - 1) % n, at : at + 1, :128] = lay_out(tile[:, :128], 0)
            out[(r + 1) % n, at : at + 1, 128:] = lay_out(tile[:, 128:], 1)
    late = pl.ds(p.ru + 8, p.r1 - p.ru - 8)
    sends.append(pltpu.make_async_copy(out.at[:, late, :], out_hbm.at[:, late, :], sems.at[11]))
    sends[-1].start()
    for send in sends:
        send.wait()


def tile_transpose(p, t):
    g = iota(t.shape, 1) >> log2(p.half)
    t = pltpu.roll(t, 0, 1, stride=p.half, stride_axis=0)
    for b in (1, 2, 4):
        t = jnp.where((g & b) != 0, pltpu.roll(t, 8 - b, 0), t)
    return pltpu.roll(t, 0, 1, stride=p.half, stride_axis=0)


def blocks_to_grid(p, blk):
    rows = []
    for yh in range(p.half // 8):
        rows.append(
            jnp.concatenate(
                [
                    tile_transpose(p, blk[8 * c : 8 * c + 8, 128 * yh : 128 * yh + 128])
                    for c in range(p.bcols // 8)
                ],
                axis=1,
            )
        )
    return jnp.concatenate(rows, axis=0)


def grid_to_blocks(p, grid):
    rows = []
    for c in range(p.bcols // 8):
        rows.append(
            jnp.concatenate(
                [
                    tile_transpose(p, grid[8 * yh : 8 * yh + 8, 128 * c : 128 * c + 128])
                    for yh in range(p.half // 8)
                ],
                axis=1,
            )
        )
    return jnp.concatenate(rows, axis=0)


def x_next(f):
    return pltpu.roll(f, f.shape[1] - 1, 1)


def x_prev(f):
    return pltpu.roll(f, 1, 1)


def y_next(f, halo):
    return jnp.where(iota(f.shape, 0) == f.shape[0] - 1, halo, pltpu.roll(f, f.shape[0] - 1, 0))


def y_prev(f, halo):
    return jnp.where(iota(f.shape, 0) == 0, halo, pltpu.roll(f, 1, 0))


def row_of(p, ref, src, at):
    return jnp.concatenate([ref[src, pl.ds(at + h, 1), :] for h in range(p.wrap)], axis=1)


def interior_kernel(p, b_ref, t_ref, copy_ref, j_ref, next_ref, g3_ref):
    s, k = p.slots, p.k
    _, q_s = send_positions(p, t_ref[...])
    r_l, z_l, j_l = lane_route(p)
    shape = (p.zc, s, p.rows)
    g3 = (iota(shape, 0) == z_l) & (q_s.reshape(1, s, 1) == (r_l * k + j_l).astype(F32))
    g3_ref[...] = one_hot(g3).reshape(p.zc * s, p.rows)
    zero = jnp.zeros((p.ny, p.nx), F32)
    for z in range(p.zc):
        b = [b_ref[c, z] for c in range(3)]
        below = [b_ref[c, z - 1] if z > 0 else zero for c in range(3)]
        above = [b_ref[c, z + 1] if z < p.zc - 1 else zero for c in range(3)]
        south, north = [y_prev(f, 0.0) for f in b], [y_next(f, 0.0) for f in b]
        west, east = [x_prev(f) for f in b], [x_next(f) for f in b]
        j_ref[0, z] = ((north[2] - south[2]) - (above[1] - below[1])) * 0.5
        j_ref[1, z] = ((above[0] - below[0]) - (east[2] - west[2])) * 0.5
        j_ref[2, z] = ((east[1] - west[1]) - (north[0] - south[0])) * 0.5
        for c in range(3):
            lap = below[c] + above[c] + south[c] + north[c] + west[c] + east[c] - 6.0 * b[c]
            next_ref[c, z] = b[c] + 0.05 * lap
            copy_ref[c, z] = b[c]


def edge_rows(p, ref, nxt, prv, at):
    y = iota((p.ny, p.nx), 0)
    north = jnp.where(y == p.ny - 1, row_of(p, ref, nxt, at), 0.0)
    return north, jnp.where(y == 0, row_of(p, ref, prv, at), 0.0)


def field_kernel(p, r_ref, b_ref, j_ref, lo_ref, hi_ref, out, e_ref, up_ref, down_ref):
    n, k, zc = p.n, p.k, p.zc
    me = lax.axis_index("xy")
    nxt, prv = lax.rem(me + 1, n), lax.rem(me + n - 1, n)
    b = [[b_ref[c, z] for z in range(zc)] for c in range(3)]
    cols = r_ref[:, p.ru + p.rb, :]
    shape = (n, p.rc, 128)
    col_s = jnp.sum(
        jnp.where((iota(shape, 1) & (k - 1)) == iota(shape, 2), cols[:, None, :128], 0.0), axis=2, keepdims=True
    )
    shape = (n, p.rc, zc * p.bcols)
    lane = iota(shape, 2)
    g = one_hot(
        ((iota(shape, 1) >> log2(k)) == (lane >> log2(p.bcols)))
        & (col_s == mirror(lane & (p.bcols - 1)).astype(F32))
    ).reshape(p.rows, zc * p.bcols)
    force = []
    zero = jnp.zeros((p.ny, p.nx), F32)
    for z in range(zc):
        bz = [b[c][z] for c in range(3)]
        dy = {}
        for c in (0, 2):
            north, south = edge_rows(p, r_ref, nxt, prv, p.ru + (c * zc + z) * p.wrap)
            dy[c] = north - south
        dz = [zero, zero]
        for c in range(2):
            if z == zc - 1:
                dz[c] = dz[c] + hi_ref[c]
            if z == 0:
                dz[c] = dz[c] - lo_ref[c]
        j0 = j_ref[0, z] + (dy[2] - dz[1]) * 0.5
        j1 = j_ref[1, z] + dz[0] * 0.5
        j2 = j_ref[2, z] - dy[0] * 0.5
        force.append([j1 * bz[2] - j2 * bz[1], j2 * bz[0] - j0 * bz[2], j0 * bz[1] - j1 * bz[0]])
    for c in range(3):
        f_blk = jnp.concatenate([grid_to_blocks(p, force[z][c]) for z in range(zc)], axis=0)
        out[:, c * p.rc : (c + 1) * p.rc, :] = select(g, f_blk).reshape(n, p.rc, p.area)
    p_l, z_l, _ = lane_route(p)
    shape = (n, p.rows)
    col_l = jnp.sum(
        jnp.where(iota(shape, 0) == p_l.reshape(1, p.rows), tile_lanes(cols[:, :128], p.rows), 0.0), axis=0, keepdims=True
    )
    shape = (zc, p.bcols, p.rows)
    g = one_hot(
        (iota(shape, 0) == z_l) & (iota(shape, 1).astype(F32) == col_l.reshape(1, 1, p.rows))
    ).reshape(zc * p.bcols, p.rows)
    u = []
    for c in range(3):
        blk = select(g, r_ref[:, c * p.rc : (c + 1) * p.rc, :].reshape(p.rows, p.area))
        u.append([blocks_to_grid(p, blk[z * p.bcols : (z + 1) * p.bcols]) for z in range(zc)])
    for z in range(zc):
        uz, bz = [u[c][z] for c in range(3)], [b[c][z] for c in range(3)]
        ez = [uz[1] * bz[2] - uz[2] * bz[1], uz[2] * bz[0] - uz[0] * bz[2], uz[0] * bz[1] - uz[1] * bz[0]]
        for c in range(3):
            e_ref[c, z] = ez[c]
        if z == zc - 1:
            up_ref[0], up_ref[1], up_ref[2] = ez[0], ez[1], bz[2]
        if z == 0:
            down_ref[0], down_ref[1], down_ref[2] = ez[0], ez[1], bz[2]


def outer_velocity(p, r_ref):
    n, zc = p.n, p.zc
    at = p.ru + p.rb
    x = r_ref[:, at, :][:, 128:]
    spun = pltpu.roll(x, 64, 1)
    low = iota(x.shape, 1) < 64
    lane = iota((1, 1, p.rows), 2)
    place = lane & 7
    shape = (zc, p.bcols, p.rows)
    sides = []
    for d, (cols, i) in enumerate(((jnp.where(low, x, spun), (8 - place) & 7), (jnp.where(low, spun, x), 7 - place))):
        device = iota((n, p.rows), 0) == (lane >> 3).reshape(1, p.rows)
        col = jnp.sum(jnp.where(device, tile_lanes(cols, p.rows), 0.0), axis=0, keepdims=True)
        g = one_hot(
            (iota(shape, 0) == (i >> log2(p.k))) & (iota(shape, 1).astype(F32) == col.reshape(1, 1, p.rows))
        ).reshape(zc * p.bcols, p.rows)
        parts = []
        for c in range(3):
            m = r_ref[:, at + 1 + c, :][:, 128 * d : 128 * d + 128]
            parts.append(jnp.concatenate([spin(jnp.broadcast_to(m[r : r + 1], (8, 128))) for r in range(n)], axis=0))
        o = select(g, jnp.concatenate(parts, axis=1))
        side = []
        for c in range(3):
            blocks = o[:, 128 * c : 128 * c + 128]
            row = [lay_out(blocks[8 * t : 8 * t + 8], 0) for t in range(zc * p.bcols // 8)]
            per = p.bcols // 8
            side.append([jnp.concatenate(row[z * per : (z + 1) * per], axis=1) for z in range(zc)])
        sides.append(side)
    return sides


def local_kernel(p, r_ref, b_ref, lo_ref, hi_ref, e_ref, next_ref):
    n, zc = p.n, p.zc
    me = lax.axis_index("xy")
    nxt, prv = lax.rem(me + 1, n), lax.rem(me + n - 1, n)
    zero = jnp.zeros((p.ny, p.nx), F32)
    outer_u = outer_velocity(p, r_ref)
    for z in range(zc):
        e = [e_ref[c, z] for c in range(3)]
        e0, e2 = [], []
        for u, device in zip(outer_u, (nxt, prv)):
            b = [row_of(p, r_ref, device, p.ru + (c * zc + z) * p.wrap) for c in range(3)]
            e0.append(u[1][z] * b[2] - u[2][z] * b[1])
            e2.append(u[0][z] * b[1] - u[1][z] * b[0])
        above = [e_ref[c, z + 1] if z < zc - 1 else zero for c in range(2)]
        below = [e_ref[c, z - 1] if z > 0 else zero for c in range(2)]
        curl = [
            (y_next(e[2], e2[0]) - y_prev(e[2], e2[1])) - (above[1] - below[1]),
            (above[0] - below[0]) - (x_next(e[2]) - x_prev(e[2])),
            (x_next(e[1]) - x_prev(e[1])) - (y_next(e[0], e0[0]) - y_prev(e[0], e0[1])),
        ]
        for c in range(3):
            north, south = edge_rows(p, r_ref, nxt, prv, p.ru + (c * zc + z) * p.wrap)
            total = curl[c] + north + south
            if c < 2 and z == 0:
                total = total + lo_ref[c]
            if c < 2 and z == zc - 1:
                total = total + hi_ref[c]
            next_ref[c, z] = b_ref[c, z] + 0.05 * total


def finish_kernel(p, r_ref, g_ref, v_ref, n_ref, lo_ref, hi_ref, vel_hbm, mag_hbm, vel, mag, sems):
    zc = p.zc
    half_fine = p.edge * p.edge // 2
    half_area = p.area // 2
    ex = log2(p.edge)
    c, f = iota((half_area, half_fine), 0), iota((half_area, half_fine), 1)
    coarse = ((f >> (ex + 1)) << (ex - 1)) + ((f & (p.edge - 1)) >> 1)
    sel = one_hot(coarse == c)
    sel = jnp.concatenate([sel, sel], axis=0)
    g = g_ref[...]
    ws = [slice(h * half_area, (h + 1) * half_area) for h in range(2)]
    s = p.slots
    m = zc * s
    copies = []
    for c in range(3):
        hi, lo = split(r_ref[:, c * p.rc : (c + 1) * p.rc, :].reshape(p.rows, p.area) * 0.1)
        parts = dot(g, jnp.concatenate([hi, lo], axis=1)).astype(BF16)
        hi, lo = parts[:, : p.area], parts[:, p.area :]
        pairs = [jnp.concatenate([hi[:, w], lo[:, w]], axis=1) for w in ws]
        add = dot(jnp.concatenate(pairs, axis=0), sel)
        for z in range(zc):
            for h in range(2):
                fw = slice(h * half_fine, (h + 1) * half_fine)
                part = add[h * m + z * s : h * m + (z + 1) * s]
                for d in range(2):
                    vel[c, 2 * z + d, :, fw] = v_ref[c, 2 * z + d, :, fw] + part
        copies.append(pltpu.make_async_copy(vel.at[c], vel_hbm.at[c], sems.at[c]))
        copies[-1].start()
    for z in range(zc):
        dz = [jnp.zeros((p.ny, p.nx), F32)] * 2
        outer = dz[0]
        if z == zc - 1:
            dz = [dz[c] + hi_ref[c] for c in range(2)]
            outer = outer + hi_ref[2]
        if z == 0:
            dz = [dz[c] - lo_ref[c] for c in range(2)]
            outer = outer + lo_ref[2]
        mag[0, z] = n_ref[0, z] + 0.05 * -dz[1]
        mag[1, z] = n_ref[1, z] + 0.05 * dz[0]
        mag[2, z] = n_ref[2, z] + 0.05 * outer
    copies.append(pltpu.make_async_copy(mag, mag_hbm, sems.at[3]))
    copies[-1].start()
    for copy in copies:
        copy.wait()


def struct(*shape, dtype=F32):
    return jax.ShapeDtypeStruct(shape, dtype)


def call(kernel, ins, outs, scratch=(), grant=20 << 20):
    return pl.pallas_call(
        kernel,
        out_shape=[o for o, _ in outs],
        in_specs=ins,
        out_specs=[spec for _, spec in outs],
        scratch_shapes=list(scratch),
        cost_estimate=pl.CostEstimate(flops=1 << 24, bytes_accessed=1 << 20, transcendentals=0),
        compiler_params=pltpu.CompilerParams(vmem_limit_bytes=grant),
    )


def ring(axis, step):
    n = lax.axis_size(axis)
    return [(i, (i + step) % n) for i in range(n)]


def planes(up, down):
    below = lax.ppermute(up, "gz", ring("gz", 1))
    above = lax.ppermute(down, "gz", ring("gz", -1))
    return below, above


def body(velocity, magnetic, slot_block_table):
    p = Plan(velocity.shape, magnetic.shape, lax.axis_size("xy"))
    plane = (p.ny, p.nx)
    dma = pltpu.SemaphoreType.DMA
    table = slot_block_table.reshape(1, p.slots)
    sent, up, down = call(
        functools.partial(restrict_kernel, p),
        [HBM] * 3,
        [(struct(p.n, p.r1, p.area), HBM), (struct(2, *plane), HBM), (struct(2, *plane), HBM)],
        [
            pltpu.VMEM(velocity.shape, F32),
            pltpu.VMEM((1, p.slots), jnp.int32),
            pltpu.VMEM(magnetic.shape, F32),
            pltpu.VMEM((p.n, p.r1, p.area), F32),
            pltpu.VMEM((-(-p.rb // 8) * 8, p.area), F32),
            pltpu.VMEM((-(-p.rb // 8) * 8, p.area), F32),
            dma((12,)),
        ],
        ALL_VMEM,
    )(velocity, table, magnetic)
    got = lax.all_to_all(sent, "xy", 0, 0, tiled=True)
    below, above = planes(up, down)
    held, held_table, _ = lax.optimization_barrier((magnetic, table, up))
    field, current, diffused, g3 = call(
        functools.partial(interior_kernel, p),
        [VMEM] * 2,
        [(struct(*magnetic.shape), VMEM)] * 3 + [(struct(p.zc * p.slots, p.rows, dtype=BF16), VMEM)],
    )(held, held_table)
    sent, emf, up, down = call(
        functools.partial(field_kernel, p),
        [VMEM] * 5,
        [
            (struct(p.n, p.ru, p.area), VMEM),
            (struct(*magnetic.shape), VMEM),
            (struct(3, *plane), VMEM),
            (struct(3, *plane), VMEM),
        ],
    )(got, field, current, below, above)
    got_force = lax.all_to_all(sent, "xy", 0, 0, tiled=True)
    emf_below, emf_above = planes(up, down)
    (partial,) = call(
        functools.partial(local_kernel, p), [VMEM] * 5, [(struct(*magnetic.shape), VMEM)]
    )(got, diffused, below, above, emf)
    return tuple(
        call(
            functools.partial(finish_kernel, p),
            [VMEM] * 6,
            [(struct(*velocity.shape), HBM), (struct(*magnetic.shape), HBM)],
            [pltpu.VMEM(velocity.shape, F32), pltpu.VMEM(magnetic.shape, F32), dma((4,))],
        )(got_force, g3, velocity, partial, emf_below, emf_above)
    )


def solution(mesh):
    return jax.shard_map(
        body,
        mesh=mesh,
        in_specs=(P(None, "gz", "xy", None), P(None, "gz", "xy", None), P("xy")),
        out_specs=(P(None, "gz", "xy", None), P(None, "gz", "xy", None)),
        check_vma=False,
    )
```

```python
import functools
import math

import jax
import jax.numpy as jnp
from jax import lax
from jax.experimental import pallas as pl
from jax.experimental.pallas import tpu as pltpu
from jax.sharding import PartitionSpec as P

F32, BF16 = jnp.float32, jnp.bfloat16
VMEM = pl.BlockSpec(memory_space=pltpu.VMEM)
ALL_VMEM = 67043328
HBM = pl.BlockSpec(memory_space=pltpu.HBM)


def split(x):
    hi = x.astype(BF16)
    return hi, (x - hi.astype(F32)).astype(BF16)


def dot(a, b):
    return jnp.dot(a, b, preferred_element_type=F32)


def iota(shape, dim):
    return lax.broadcasted_iota(jnp.int32, shape, dim)


def one_hot(mask):
    return jnp.where(mask, 1.0, 0.0).astype(BF16)


def log2(x):
    assert x == 1 << (x.bit_length() - 1)
    return x.bit_length() - 1


class Plan:
    def __init__(self, vshape, bshape, n):
        self.n = n
        self.slots = vshape[2]
        self.k = self.slots // n
        self.zc = bshape[1]
        self.ny, self.nx = bshape[2:]
        self.edge = math.isqrt(vshape[3])
        self.half = self.edge // 2
        self.area = self.half * self.half
        self.bcols = self.nx // self.half
        self.rc = -(-self.zc * self.k // 8) * 8
        self.ru = 3 * self.rc
        self.rows = n * self.rc
        self.rb = 3 * self.zc * self.nx // self.area
        self.r1 = -(-(self.ru + self.rb + 4) // 8) * 8
        self.wrap = self.nx // self.area
        assert self.rc == 8 and self.area == 256 and self.half == 16


def mirror(i):
    return (i & ~7) | ((8 - (i & 7)) & 7)


def send_positions(p, table):
    s = p.slots
    row = jnp.broadcast_to((table >> log2(p.bcols)).astype(F32), (s, s))
    i, j = iota((s, s), 0), iota((s, s), 1)
    row_s = jnp.sum(jnp.where(i == j, row, 0.0), axis=1, keepdims=True)
    rank = jnp.sum(jnp.where((row_s == row) & (i < j), 1.0, 0.0), axis=0, keepdims=True)
    q = row[0:1] * p.k + rank
    q_s = jnp.sum(jnp.where(i == j, jnp.broadcast_to(q, (s, s)), 0.0), axis=1, keepdims=True)
    return q, q_s


def select(g, x):
    hi, lo = split(x)
    out = dot(g, jnp.concatenate([hi, lo], axis=1))
    return out[:, : x.shape[1]] + out[:, x.shape[1] :]


def spin(t):
    return pltpu.roll(t, 0, 1, stride=16, stride_axis=0)


def lay_out(t, first):
    t = spin(t)
    here = (iota(t.shape, 1) >> 4) == ((iota(t.shape, 0) + first) & 7)
    return jnp.sum(jnp.where(here, t, 0.0), axis=0, keepdims=True)


def tile_lanes(x, width):
    return x[:, :width] if width <= 128 else jnp.concatenate([x] * (width // 128), axis=1)


def lane_route(p):
    lane = iota((1, 1, p.rows), 2)
    i = lane & (p.rc - 1)
    return lane >> log2(p.rc), i >> log2(p.k), i & (p.k - 1)


def restrict_kernel(p, v_hbm, t_hbm, b_hbm, out_hbm, up_hbm, down_hbm, v_ref, t_ref, b_ref, out, last, first, sems):
    n, k, s, zc = p.n, p.k, p.slots, p.zc
    me = lax.axis_index("xy")
    t_copy = pltpu.make_async_copy(t_hbm, t_ref, sems.at[0])
    b_copy = pltpu.make_async_copy(b_hbm, b_ref, sems.at[1])
    v_copies = [pltpu.make_async_copy(v_hbm.at[c], v_ref.at[c], sems.at[2 + c]) for c in range(3)]
    t_copy.start()
    b_copy.start()
    for copy in v_copies:
        copy.start()
    half_fine = p.edge * p.edge // 2
    half_area = p.area // 2
    f, c = iota((half_fine, half_area), 0), iota((half_fine, half_area), 1)
    e = log2(p.edge)
    coarse = (mirror(f >> (e + 1)) << (e - 1)) + ((f & (p.edge - 1)) >> 1)
    sel = one_hot(coarse == c)
    t_copy.wait()
    table = t_ref[...]
    q, _ = send_positions(p, table)
    lanes = zc * s
    rep = one_hot((iota((s, lanes), 1) & (s - 1)) == iota((s, lanes), 0))
    qt = dot(jnp.broadcast_to(q, (8, s)).astype(BF16), rep)[0:1]
    shape = (n, p.rc, lanes)
    i = iota(shape, 1)
    target = (iota(shape, 0) * k + (i & (k - 1))).astype(F32)
    g = one_hot(((i >> log2(k)) == (iota(shape, 2) >> log2(s))) & (target == qt.reshape(1, 1, lanes)))
    g = g.reshape(p.rows, lanes)
    col = jnp.broadcast_to((table & (p.bcols - 1)).astype(F32), (s, s))
    qi = iota((s, s), 0).astype(F32)
    col_q = jnp.sum(jnp.where(qi == jnp.broadcast_to(q, (s, s)), col, 0.0), axis=1, keepdims=True)
    qa, la = iota((s, p.area), 0), iota((s, p.area), 1)
    place = jnp.where(la < 128, la, jnp.where(la < 192, -la, -1 - la)) & (k - 1)
    spread = jnp.where((qa & (k - 1)) == place, col_q, 0.0).astype(BF16)
    gather = one_hot((iota((n, s), 1) >> log2(k)) == iota((n, s), 0))
    cols = dot(gather, spread)
    at = p.ru + p.rb
    for r in range(n):
        north, south = (r + 1) % n, (r - 1) % n
        out[r, at : at + 1, :128] = cols[r : r + 1, :128]
        outer = jnp.where(iota((1, 128), 1) < 64, cols[north : north + 1, 128:], cols[south : south + 1, 128:])
        out[r, at : at + 1, 128:] = outer
    b_copy.wait()
    sends = [
        pltpu.make_async_copy(b_ref.at[0:2, zc - 1], up_hbm, sems.at[5]),
        pltpu.make_async_copy(b_ref.at[0:2, 0], down_hbm, sems.at[6]),
    ]
    for c in range(3):
        for z in range(zc):
            for h in range(p.wrap):
                at = (c * zc + z) * p.wrap + h
                w = slice(h * p.area, (h + 1) * p.area)
                last[at : at + 1, :] = b_ref[c, z, p.ny - 1 : p.ny, w]
                first[at : at + 1, :] = b_ref[c, z, 0:1, w]
    nxt = lax.rem(me + 1, n)
    for r in range(n):
        out[r, p.ru : p.ru + p.rb, :] = jnp.where(r == nxt, last[: p.rb], first[: p.rb])
    early = pl.ds(p.ru, 8)
    sends.append(pltpu.make_async_copy(out.at[:, early, :], out_hbm.at[:, early, :], sems.at[7]))
    for send in sends:
        send.start()
    averages = []
    m = zc * s
    ws = [slice(h * half_fine, (h + 1) * half_fine) for h in range(2)]
    for c in range(3):
        v_copies[c].wait()
        z_sum = jnp.concatenate([v_ref[c, 2 * z] + v_ref[c, 2 * z + 1] for z in range(zc)], axis=0)
        hi, lo = split(z_sum)
        o = dot(jnp.concatenate([x[:, w] for w in ws for x in (hi, lo)], axis=0), sel)
        u = [o[2 * h * m : (2 * h + 1) * m] + o[(2 * h + 1) * m : (2 * h + 2) * m] for h in range(2)]
        averages.append(jnp.concatenate(u, axis=1) * 0.125)
    for c in range(3):
        blocks = select(g, averages[c])
        out[:, c * p.rc : (c + 1) * p.rc, :] = blocks.reshape(n, p.rc, p.area)
        rows = pl.ds(c * p.rc, p.rc)
        sends.append(pltpu.make_async_copy(out.at[:, rows, :], out_hbm.at[:, rows, :], sems.at[8 + c]))
        sends[-1].start()
        at = p.ru + p.rb + 1 + c
        for r in range(n):
            tile = blocks[r * p.rc : (r + 1) * p.rc]
            out[(r - 1) % n, at : at + 1, :128] = lay_out(tile[:, :128], 0)
            out[(r + 1) % n, at : at + 1, 128:] = lay_out(tile[:, 128:], 1)
    late = pl.ds(p.ru + 8, p.r1 - p.ru - 8)
    sends.append(pltpu.make_async_copy(out.at[:, late, :], out_hbm.at[:, late, :], sems.at[11]))
    sends[-1].start()
    for send in sends:
        send.wait()


def tile_transpose(p, t):
    g = iota(t.shape, 1) >> log2(p.half)
    t = pltpu.roll(t, 0, 1, stride=p.half, stride_axis=0)
    for b in (1, 2, 4):
        t = jnp.where((g & b) != 0, pltpu.roll(t, 8 - b, 0), t)
    return pltpu.roll(t, 0, 1, stride=p.half, stride_axis=0)


def blocks_to_grid(p, blk):
    rows = []
    for yh in range(p.half // 8):
        rows.append(
            jnp.concatenate(
                [
                    tile_transpose(p, blk[8 * c : 8 * c + 8, 128 * yh : 128 * yh + 128])
                    for c in range(p.bcols // 8)
                ],
                axis=1,
            )
        )
    return jnp.concatenate(rows, axis=0)


def grid_to_blocks(p, grid):
    rows = []
    for c in range(p.bcols // 8):
        rows.append(
            jnp.concatenate(
                [
                    tile_transpose(p, grid[8 * yh : 8 * yh + 8, 128 * c : 128 * c + 128])
                    for yh in range(p.half // 8)
                ],
                axis=1,
            )
        )
    return jnp.concatenate(rows, axis=0)


def x_next(f):
    return pltpu.roll(f, f.shape[1] - 1, 1)


def x_prev(f):
    return pltpu.roll(f, 1, 1)


def y_next(f, halo):
    return jnp.where(iota(f.shape, 0) == f.shape[0] - 1, halo, pltpu.roll(f, f.shape[0] - 1, 0))


def y_prev(f, halo):
    return jnp.where(iota(f.shape, 0) == 0, halo, pltpu.roll(f, 1, 0))


def row_of(p, ref, src, at):
    return jnp.concatenate([ref[src, pl.ds(at + h, 1), :] for h in range(p.wrap)], axis=1)


def interior_kernel(p, b_ref, t_ref, copy_ref, j_ref, next_ref, g3_ref):
    s, k = p.slots, p.k
    _, q_s = send_positions(p, t_ref[...])
    r_l, z_l, j_l = lane_route(p)
    shape = (p.zc, s, p.rows)
    g3 = (iota(shape, 0) == z_l) & (q_s.reshape(1, s, 1) == (r_l * k + j_l).astype(F32))
    g3_ref[...] = one_hot(g3).reshape(p.zc * s, p.rows)
    zero = jnp.zeros((p.ny, p.nx), F32)
    for z in range(p.zc):
        b = [b_ref[c, z] for c in range(3)]
        below = [b_ref[c, z - 1] if z > 0 else zero for c in range(3)]
        above = [b_ref[c, z + 1] if z < p.zc - 1 else zero for c in range(3)]
        south, north = [y_prev(f, 0.0) for f in b], [y_next(f, 0.0) for f in b]
        west, east = [x_prev(f) for f in b], [x_next(f) for f in b]
        j_ref[0, z] = ((north[2] - south[2]) - (above[1] - below[1])) * 0.5
        j_ref[1, z] = ((above[0] - below[0]) - (east[2] - west[2])) * 0.5
        j_ref[2, z] = ((east[1] - west[1]) - (north[0] - south[0])) * 0.5
        for c in range(3):
            lap = below[c] + above[c] + south[c] + north[c] + west[c] + east[c] - 6.0 * b[c]
            next_ref[c, z] = b[c] + 0.05 * lap
            copy_ref[c, z] = b[c]


def edge_rows(p, ref, nxt, prv, at):
    y = iota((p.ny, p.nx), 0)
    north = jnp.where(y == p.ny - 1, row_of(p, ref, nxt, at), 0.0)
    return north, jnp.where(y == 0, row_of(p, ref, prv, at), 0.0)


def field_kernel(p, r_ref, b_ref, j_ref, lo_ref, hi_ref, out_hbm, e_ref, up_ref, down_ref, out, sems):
    n, k, zc = p.n, p.k, p.zc
    me = lax.axis_index("xy")
    nxt, prv = lax.rem(me + 1, n), lax.rem(me + n - 1, n)
    b = [[b_ref[c, z] for z in range(zc)] for c in range(3)]
    cols = r_ref[:, p.ru + p.rb, :]
    shape = (n, p.rc, 128)
    col_s = jnp.sum(
        jnp.where((iota(shape, 1) & (k - 1)) == iota(shape, 2), cols[:, None, :128], 0.0), axis=2, keepdims=True
    )
    shape = (n, p.rc, zc * p.bcols)
    lane = iota(shape, 2)
    g = one_hot(
        ((iota(shape, 1) >> log2(k)) == (lane >> log2(p.bcols)))
        & (col_s == mirror(lane & (p.bcols - 1)).astype(F32))
    ).reshape(p.rows, zc * p.bcols)
    force = []
    zero = jnp.zeros((p.ny, p.nx), F32)
    for z in range(zc):
        bz = [b[c][z] for c in range(3)]
        dy = {}
        for c in (0, 2):
            north, south = edge_rows(p, r_ref, nxt, prv, p.ru + (c * zc + z) * p.wrap)
            dy[c] = north - south
        dz = [zero, zero]
        for c in range(2):
            if z == zc - 1:
                dz[c] = dz[c] + hi_ref[c]
            if z == 0:
                dz[c] = dz[c] - lo_ref[c]
        j0 = j_ref[0, z] + (dy[2] - dz[1]) * 0.5
        j1 = j_ref[1, z] + dz[0] * 0.5
        j2 = j_ref[2, z] - dy[0] * 0.5
        force.append([j1 * bz[2] - j2 * bz[1], j2 * bz[0] - j0 * bz[2], j0 * bz[1] - j1 * bz[0]])
    sends = []
    for c in range(3):
        f_blk = jnp.concatenate([grid_to_blocks(p, force[z][c]) for z in range(zc)], axis=0)
        out[:, c * p.rc : (c + 1) * p.rc, :] = select(g, f_blk).reshape(n, p.rc, p.area)
    sends.append(pltpu.make_async_copy(out, out_hbm, sems.at[0]))
    sends[-1].start()
    p_l, z_l, _ = lane_route(p)
    shape = (n, p.rows)
    col_l = jnp.sum(
        jnp.where(iota(shape, 0) == p_l.reshape(1, p.rows), tile_lanes(cols[:, :128], p.rows), 0.0), axis=0, keepdims=True
    )
    shape = (zc, p.bcols, p.rows)
    g = one_hot(
        (iota(shape, 0) == z_l) & (iota(shape, 1).astype(F32) == col_l.reshape(1, 1, p.rows))
    ).reshape(zc * p.bcols, p.rows)
    u = []
    for c in range(3):
        blk = select(g, r_ref[:, c * p.rc : (c + 1) * p.rc, :].reshape(p.rows, p.area))
        u.append([blocks_to_grid(p, blk[z * p.bcols : (z + 1) * p.bcols]) for z in range(zc)])
    for z in range(zc):
        uz, bz = [u[c][z] for c in range(3)], [b[c][z] for c in range(3)]
        ez = [uz[1] * bz[2] - uz[2] * bz[1], uz[2] * bz[0] - uz[0] * bz[2], uz[0] * bz[1] - uz[1] * bz[0]]
        for c in range(3):
            e_ref[c, z] = ez[c]
        if z == zc - 1:
            up_ref[0], up_ref[1], up_ref[2] = ez[0], ez[1], bz[2]
        if z == 0:
            down_ref[0], down_ref[1], down_ref[2] = ez[0], ez[1], bz[2]
    for send in sends:
        send.wait()


def outer_velocity(p, r_ref):
    n, zc = p.n, p.zc
    at = p.ru + p.rb
    x = r_ref[:, at, :][:, 128:]
    spun = pltpu.roll(x, 64, 1)
    low = iota(x.shape, 1) < 64
    lane = iota((1, 1, p.rows), 2)
    place = lane & 7
    shape = (zc, p.bcols, p.rows)
    sides = []
    for d, (cols, i) in enumerate(((jnp.where(low, x, spun), (8 - place) & 7), (jnp.where(low, spun, x), 7 - place))):
        device = iota((n, p.rows), 0) == (lane >> 3).reshape(1, p.rows)
        col = jnp.sum(jnp.where(device, tile_lanes(cols, p.rows), 0.0), axis=0, keepdims=True)
        g = one_hot(
            (iota(shape, 0) == (i >> log2(p.k))) & (iota(shape, 1).astype(F32) == col.reshape(1, 1, p.rows))
        ).reshape(zc * p.bcols, p.rows)
        parts = []
        for c in range(3):
            m = r_ref[:, at + 1 + c, :][:, 128 * d : 128 * d + 128]
            parts.append(jnp.concatenate([spin(jnp.broadcast_to(m[r : r + 1], (8, 128))) for r in range(n)], axis=0))
        o = select(g, jnp.concatenate(parts, axis=1))
        side = []
        for c in range(3):
            blocks = o[:, 128 * c : 128 * c + 128]
            row = [lay_out(blocks[8 * t : 8 * t + 8], 0) for t in range(zc * p.bcols // 8)]
            per = p.bcols // 8
            side.append([jnp.concatenate(row[z * per : (z + 1) * per], axis=1) for z in range(zc)])
        sides.append(side)
    return sides


def local_kernel(p, r_ref, b_ref, lo_ref, hi_ref, e_ref, next_ref):
    n, zc = p.n, p.zc
    me = lax.axis_index("xy")
    nxt, prv = lax.rem(me + 1, n), lax.rem(me + n - 1, n)
    zero = jnp.zeros((p.ny, p.nx), F32)
    outer_u = outer_velocity(p, r_ref)
    for z in range(zc):
        e = [e_ref[c, z] for c in range(3)]
        e0, e2 = [], []
        for u, device in zip(outer_u, (nxt, prv)):
            b = [row_of(p, r_ref, device, p.ru + (c * zc + z) * p.wrap) for c in range(3)]
            e0.append(u[1][z] * b[2] - u[2][z] * b[1])
            e2.append(u[0][z] * b[1] - u[1][z] * b[0])
        above = [e_ref[c, z + 1] if z < zc - 1 else zero for c in range(2)]
        below = [e_ref[c, z - 1] if z > 0 else zero for c in range(2)]
        curl = [
            (y_next(e[2], e2[0]) - y_prev(e[2], e2[1])) - (above[1] - below[1]),
            (above[0] - below[0]) - (x_next(e[2]) - x_prev(e[2])),
            (x_next(e[1]) - x_prev(e[1])) - (y_next(e[0], e0[0]) - y_prev(e[0], e0[1])),
        ]
        for c in range(3):
            north, south = edge_rows(p, r_ref, nxt, prv, p.ru + (c * zc + z) * p.wrap)
            total = curl[c] + north + south
            if c < 2 and z == 0:
                total = total + lo_ref[c]
            if c < 2 and z == zc - 1:
                total = total + hi_ref[c]
            next_ref[c, z] = b_ref[c, z] + 0.05 * total


def finish_kernel(p, r_ref, g_ref, v_ref, n_ref, lo_ref, hi_ref, vel_hbm, mag_hbm, vel, mag, sems):
    zc = p.zc
    half_fine = p.edge * p.edge // 2
    half_area = p.area // 2
    ex = log2(p.edge)
    c, f = iota((half_area, half_fine), 0), iota((half_area, half_fine), 1)
    coarse = ((f >> (ex + 1)) << (ex - 1)) + ((f & (p.edge - 1)) >> 1)
    sel = one_hot(coarse == c)
    sel = jnp.concatenate([sel, sel], axis=0)
    g = g_ref[...]
    ws = [slice(h * half_area, (h + 1) * half_area) for h in range(2)]
    s = p.slots
    m = zc * s
    copies = []
    for c in range(3):
        hi, lo = split(r_ref[:, c * p.rc : (c + 1) * p.rc, :].reshape(p.rows, p.area) * 0.1)
        parts = dot(g, jnp.concatenate([hi, lo], axis=1)).astype(BF16)
        hi, lo = parts[:, : p.area], parts[:, p.area :]
        pairs = [jnp.concatenate([hi[:, w], lo[:, w]], axis=1) for w in ws]
        add = dot(jnp.concatenate(pairs, axis=0), sel)
        for z in range(zc):
            for h in range(2):
                fw = slice(h * half_fine, (h + 1) * half_fine)
                part = add[h * m + z * s : h * m + (z + 1) * s]
                for d in range(2):
                    vel[c, 2 * z + d, :, fw] = v_ref[c, 2 * z + d, :, fw] + part
        copies.append(pltpu.make_async_copy(vel.at[c], vel_hbm.at[c], sems.at[c]))
        copies[-1].start()
    for z in range(zc):
        dz = [jnp.zeros((p.ny, p.nx), F32)] * 2
        outer = dz[0]
        if z == zc - 1:
            dz = [dz[c] + hi_ref[c] for c in range(2)]
            outer = outer + hi_ref[2]
        if z == 0:
            dz = [dz[c] - lo_ref[c] for c in range(2)]
            outer = outer + lo_ref[2]
        mag[0, z] = n_ref[0, z] + 0.05 * -dz[1]
        mag[1, z] = n_ref[1, z] + 0.05 * dz[0]
        mag[2, z] = n_ref[2, z] + 0.05 * outer
    copies.append(pltpu.make_async_copy(mag, mag_hbm, sems.at[3]))
    copies[-1].start()
    for copy in copies:
        copy.wait()


def struct(*shape, dtype=F32):
    return jax.ShapeDtypeStruct(shape, dtype)


def call(kernel, ins, outs, scratch=(), grant=20 << 20):
    return pl.pallas_call(
        kernel,
        out_shape=[o for o, _ in outs],
        in_specs=ins,
        out_specs=[spec for _, spec in outs],
        scratch_shapes=list(scratch),
        cost_estimate=pl.CostEstimate(flops=1 << 24, bytes_accessed=1 << 20, transcendentals=0),
        compiler_params=pltpu.CompilerParams(vmem_limit_bytes=grant),
    )


def ring(axis, step):
    n = lax.axis_size(axis)
    return [(i, (i + step) % n) for i in range(n)]


def planes(up, down):
    below = lax.ppermute(up, "gz", ring("gz", 1))
    above = lax.ppermute(down, "gz", ring("gz", -1))
    return below, above


def body(velocity, magnetic, slot_block_table):
    p = Plan(velocity.shape, magnetic.shape, lax.axis_size("xy"))
    plane = (p.ny, p.nx)
    dma = pltpu.SemaphoreType.DMA
    table = slot_block_table.reshape(1, p.slots)
    sent, up, down = call(
        functools.partial(restrict_kernel, p),
        [HBM] * 3,
        [(struct(p.n, p.r1, p.area), HBM), (struct(2, *plane), HBM), (struct(2, *plane), HBM)],
        [
            pltpu.VMEM(velocity.shape, F32),
            pltpu.VMEM((1, p.slots), jnp.int32),
            pltpu.VMEM(magnetic.shape, F32),
            pltpu.VMEM((p.n, p.r1, p.area), F32),
            pltpu.VMEM((-(-p.rb // 8) * 8, p.area), F32),
            pltpu.VMEM((-(-p.rb // 8) * 8, p.area), F32),
            dma((12,)),
        ],
        ALL_VMEM,
    )(velocity, table, magnetic)
    got = lax.all_to_all(sent, "xy", 0, 0, tiled=True)
    below, above = planes(up, down)
    held, held_table, _ = lax.optimization_barrier((magnetic, table, up))
    field, current, diffused, g3 = call(
        functools.partial(interior_kernel, p),
        [VMEM] * 2,
        [(struct(*magnetic.shape), VMEM)] * 3 + [(struct(p.zc * p.slots, p.rows, dtype=BF16), VMEM)],
    )(held, held_table)
    sent, emf, up, down = call(
        functools.partial(field_kernel, p),
        [VMEM] * 5,
        [
            (struct(p.n, p.ru, p.area), HBM),
            (struct(*magnetic.shape), VMEM),
            (struct(3, *plane), VMEM),
            (struct(3, *plane), VMEM),
        ],
        [pltpu.VMEM((p.n, p.ru, p.area), F32), dma((1,))],
    )(got, field, current, below, above)
    got_force = lax.all_to_all(sent, "xy", 0, 0, tiled=True)
    emf_below, emf_above = planes(up, down)
    (partial,) = call(
        functools.partial(local_kernel, p), [VMEM] * 5, [(struct(*magnetic.shape), VMEM)]
    )(got, diffused, below, above, emf)
    return tuple(
        call(
            functools.partial(finish_kernel, p),
            [VMEM] * 6,
            [(struct(*velocity.shape), HBM), (struct(*magnetic.shape), HBM)],
            [pltpu.VMEM(velocity.shape, F32), pltpu.VMEM(magnetic.shape, F32), dma((4,))],
        )(got_force, g3, velocity, partial, emf_below, emf_above)
    )


def solution(mesh):
    return jax.shard_map(
        body,
        mesh=mesh,
        in_specs=(P(None, "gz", "xy", None), P(None, "gz", "xy", None), P("xy")),
        out_specs=(P(None, "gz", "xy", None), P(None, "gz", "xy", None)),
        check_vma=False,
    )
```

```python
import functools
import math

import jax
import jax.numpy as jnp
from jax import lax
from jax.experimental import pallas as pl
from jax.experimental.pallas import tpu as pltpu
from jax.sharding import PartitionSpec as P

F32, BF16 = jnp.float32, jnp.bfloat16
VMEM = pl.BlockSpec(memory_space=pltpu.VMEM)
ALL_VMEM = 67043328
HBM = pl.BlockSpec(memory_space=pltpu.HBM)


def split(x):
    hi = x.astype(BF16)
    return hi, (x - hi.astype(F32)).astype(BF16)


def dot(a, b):
    return jnp.dot(a, b, preferred_element_type=F32)


def iota(shape, dim):
    return lax.broadcasted_iota(jnp.int32, shape, dim)


def one_hot(mask):
    return jnp.where(mask, 1.0, 0.0).astype(BF16)


def log2(x):
    assert x == 1 << (x.bit_length() - 1)
    return x.bit_length() - 1


class Plan:
    def __init__(self, vshape, bshape, n):
        self.n = n
        self.slots = vshape[2]
        self.k = self.slots // n
        self.zc = bshape[1]
        self.ny, self.nx = bshape[2:]
        self.edge = math.isqrt(vshape[3])
        self.half = self.edge // 2
        self.area = self.half * self.half
        self.bcols = self.nx // self.half
        self.rc = -(-self.zc * self.k // 8) * 8
        self.ru = 3 * self.rc
        self.rows = n * self.rc
        self.rb = 3 * self.zc * self.nx // self.area
        self.r1 = -(-(self.ru + self.rb + 4) // 8) * 8
        self.wrap = self.nx // self.area
        assert self.rc == 8 and self.area == 256 and self.half == 16


def mirror(i):
    return (i & ~7) | ((8 - (i & 7)) & 7)


def send_positions(p, table):
    s = p.slots
    row = jnp.broadcast_to((table >> log2(p.bcols)).astype(F32), (s, s))
    i, j = iota((s, s), 0), iota((s, s), 1)
    row_s = jnp.sum(jnp.where(i == j, row, 0.0), axis=1, keepdims=True)
    rank = jnp.sum(jnp.where((row_s == row) & (i < j), 1.0, 0.0), axis=0, keepdims=True)
    q = row[0:1] * p.k + rank
    q_s = jnp.sum(jnp.where(i == j, jnp.broadcast_to(q, (s, s)), 0.0), axis=1, keepdims=True)
    return q, q_s


def select(g, x):
    hi, lo = split(x)
    out = dot(g, jnp.concatenate([hi, lo], axis=1))
    return out[:, : x.shape[1]] + out[:, x.shape[1] :]


def spin(t):
    return pltpu.roll(t, 0, 1, stride=16, stride_axis=0)


def lay_out(t, first):
    t = spin(t)
    here = (iota(t.shape, 1) >> 4) == ((iota(t.shape, 0) + first) & 7)
    return jnp.sum(jnp.where(here, t, 0.0), axis=0, keepdims=True)


def tile_lanes(x, width):
    return x[:, :width] if width <= 128 else jnp.concatenate([x] * (width // 128), axis=1)


def lane_route(p):
    lane = iota((1, 1, p.rows), 2)
    i = lane & (p.rc - 1)
    return lane >> log2(p.rc), i >> log2(p.k), i & (p.k - 1)


def restrict_kernel(p, v_hbm, t_hbm, b_hbm, out_hbm, up_hbm, down_hbm, v_ref, t_ref, b_ref, out, last, first, sems):
    n, k, s, zc = p.n, p.k, p.slots, p.zc
    me = lax.axis_index("xy")
    t_copy = pltpu.make_async_copy(t_hbm, t_ref, sems.at[0])
    b_copy = pltpu.make_async_copy(b_hbm, b_ref, sems.at[1])
    v_copies = [pltpu.make_async_copy(v_hbm.at[c], v_ref.at[c], sems.at[2 + c]) for c in range(3)]
    t_copy.start()
    for copy in v_copies:
        copy.start()
    b_copy.start()
    half_fine = p.edge * p.edge // 2
    half_area = p.area // 2
    f, c = iota((half_fine, half_area), 0), iota((half_fine, half_area), 1)
    e = log2(p.edge)
    coarse = (mirror(f >> (e + 1)) << (e - 1)) + ((f & (p.edge - 1)) >> 1)
    sel = one_hot(coarse == c)
    t_copy.wait()
    table = t_ref[...]
    q, _ = send_positions(p, table)
    lanes = zc * s
    rep = one_hot((iota((s, lanes), 1) & (s - 1)) == iota((s, lanes), 0))
    qt = dot(jnp.broadcast_to(q, (8, s)).astype(BF16), rep)[0:1]
    shape = (n, p.rc, lanes)
    i = iota(shape, 1)
    target = (iota(shape, 0) * k + (i & (k - 1))).astype(F32)
    g = one_hot(((i >> log2(k)) == (iota(shape, 2) >> log2(s))) & (target == qt.reshape(1, 1, lanes)))
    g = g.reshape(p.rows, lanes)
    col = jnp.broadcast_to((table & (p.bcols - 1)).astype(F32), (s, s))
    qi = iota((s, s), 0).astype(F32)
    col_q = jnp.sum(jnp.where(qi == jnp.broadcast_to(q, (s, s)), col, 0.0), axis=1, keepdims=True)
    qa, la = iota((s, p.area), 0), iota((s, p.area), 1)
    place = jnp.where(la < 128, la, jnp.where(la < 192, -la, -1 - la)) & (k - 1)
    spread = jnp.where((qa & (k - 1)) == place, col_q, 0.0).astype(BF16)
    gather = one_hot((iota((n, s), 1) >> log2(k)) == iota((n, s), 0))
    cols = dot(gather, spread)
    at = p.ru + p.rb
    for r in range(n):
        north, south = (r + 1) % n, (r - 1) % n
        out[r, at : at + 1, :128] = cols[r : r + 1, :128]
        outer = jnp.where(iota((1, 128), 1) < 64, cols[north : north + 1, 128:], cols[south : south + 1, 128:])
        out[r, at : at + 1, 128:] = outer
    averages = []
    m = zc * s
    ws = [slice(h * half_fine, (h + 1) * half_fine) for h in range(2)]
    for c in range(3):
        v_copies[c].wait()
        u = []
        for w in ws:
            z_sum = [v_ref[c, 2 * z, :, w] + v_ref[c, 2 * z + 1, :, w] for z in range(zc)]
            o = dot(jnp.concatenate(split(jnp.concatenate(z_sum, axis=0)), axis=0), sel)
            u.append(o[:m] + o[m:])
        averages.append(jnp.concatenate(u, axis=1) * 0.125)
    b_copy.wait()
    sends = [
        pltpu.make_async_copy(b_ref.at[0:2, zc - 1], up_hbm, sems.at[5]),
        pltpu.make_async_copy(b_ref.at[0:2, 0], down_hbm, sems.at[6]),
    ]
    for c in range(3):
        for z in range(zc):
            for h in range(p.wrap):
                at = (c * zc + z) * p.wrap + h
                w = slice(h * p.area, (h + 1) * p.area)
                last[at : at + 1, :] = b_ref[c, z, p.ny - 1 : p.ny, w]
                first[at : at + 1, :] = b_ref[c, z, 0:1, w]
    nxt = lax.rem(me + 1, n)
    for r in range(n):
        out[r, p.ru : p.ru + p.rb, :] = jnp.where(r == nxt, last[: p.rb], first[: p.rb])
    early = pl.ds(p.ru, 8)
    sends.append(pltpu.make_async_copy(out.at[:, early, :], out_hbm.at[:, early, :], sems.at[7]))
    for send in sends:
        send.start()
    for c in range(3):
        blocks = select(g, averages[c])
        out[:, c * p.rc : (c + 1) * p.rc, :] = blocks.reshape(n, p.rc, p.area)
        rows = pl.ds(c * p.rc, p.rc)
        sends.append(pltpu.make_async_copy(out.at[:, rows, :], out_hbm.at[:, rows, :], sems.at[8 + c]))
        sends[-1].start()
        at = p.ru + p.rb + 1 + c
        for r in range(n):
            tile = blocks[r * p.rc : (r + 1) * p.rc]
            out[(r - 1) % n, at : at + 1, :128] = lay_out(tile[:, :128], 0)
            out[(r + 1) % n, at : at + 1, 128:] = lay_out(tile[:, 128:], 1)
    late = pl.ds(p.ru + 8, p.r1 - p.ru - 8)
    sends.append(pltpu.make_async_copy(out.at[:, late, :], out_hbm.at[:, late, :], sems.at[11]))
    sends[-1].start()
    for send in sends:
        send.wait()


def tile_transpose(p, t):
    g = iota(t.shape, 1) >> log2(p.half)
    t = pltpu.roll(t, 0, 1, stride=p.half, stride_axis=0)
    for b in (1, 2, 4):
        t = jnp.where((g & b) != 0, pltpu.roll(t, 8 - b, 0), t)
    return pltpu.roll(t, 0, 1, stride=p.half, stride_axis=0)


def blocks_to_grid(p, blk):
    rows = []
    for yh in range(p.half // 8):
        rows.append(
            jnp.concatenate(
                [
                    tile_transpose(p, blk[8 * c : 8 * c + 8, 128 * yh : 128 * yh + 128])
                    for c in range(p.bcols // 8)
                ],
                axis=1,
            )
        )
    return jnp.concatenate(rows, axis=0)


def grid_to_blocks(p, grid):
    rows = []
    for c in range(p.bcols // 8):
        rows.append(
            jnp.concatenate(
                [
                    tile_transpose(p, grid[8 * yh : 8 * yh + 8, 128 * c : 128 * c + 128])
                    for yh in range(p.half // 8)
                ],
                axis=1,
            )
        )
    return jnp.concatenate(rows, axis=0)


def x_next(f):
    return pltpu.roll(f, f.shape[1] - 1, 1)


def x_prev(f):
    return pltpu.roll(f, 1, 1)


def y_next(f, halo):
    return jnp.where(iota(f.shape, 0) == f.shape[0] - 1, halo, pltpu.roll(f, f.shape[0] - 1, 0))


def y_prev(f, halo):
    return jnp.where(iota(f.shape, 0) == 0, halo, pltpu.roll(f, 1, 0))


def row_of(p, ref, src, at):
    return jnp.concatenate([ref[src, pl.ds(at + h, 1), :] for h in range(p.wrap)], axis=1)


def interior_kernel(p, b_ref, t_ref, copy_ref, j_ref, next_ref, g3_ref):
    s, k = p.slots, p.k
    _, q_s = send_positions(p, t_ref[...])
    r_l, z_l, j_l = lane_route(p)
    shape = (p.zc, s, p.rows)
    g3 = (iota(shape, 0) == z_l) & (q_s.reshape(1, s, 1) == (r_l * k + j_l).astype(F32))
    g3_ref[...] = one_hot(g3).reshape(p.zc * s, p.rows)
    zero = jnp.zeros((p.ny, p.nx), F32)
    for z in range(p.zc):
        b = [b_ref[c, z] for c in range(3)]
        below = [b_ref[c, z - 1] if z > 0 else zero for c in range(3)]
        above = [b_ref[c, z + 1] if z < p.zc - 1 else zero for c in range(3)]
        south, north = [y_prev(f, 0.0) for f in b], [y_next(f, 0.0) for f in b]
        west, east = [x_prev(f) for f in b], [x_next(f) for f in b]
        j_ref[0, z] = ((north[2] - south[2]) - (above[1] - below[1])) * 0.5
        j_ref[1, z] = ((above[0] - below[0]) - (east[2] - west[2])) * 0.5
        j_ref[2, z] = ((east[1] - west[1]) - (north[0] - south[0])) * 0.5
        for c in range(3):
            lap = below[c] + above[c] + south[c] + north[c] + west[c] + east[c] - 6.0 * b[c]
            next_ref[c, z] = b[c] + 0.05 * lap
            copy_ref[c, z] = b[c]


def edge_rows(p, ref, nxt, prv, at):
    y = iota((p.ny, p.nx), 0)
    north = jnp.where(y == p.ny - 1, row_of(p, ref, nxt, at), 0.0)
    return north, jnp.where(y == 0, row_of(p, ref, prv, at), 0.0)


def field_kernel(p, r_ref, b_ref, j_ref, lo_ref, hi_ref, out, e_ref, up_ref, down_ref):
    n, k, zc = p.n, p.k, p.zc
    me = lax.axis_index("xy")
    nxt, prv = lax.rem(me + 1, n), lax.rem(me + n - 1, n)
    b = [[b_ref[c, z] for z in range(zc)] for c in range(3)]
    cols = r_ref[:, p.ru + p.rb, :]
    shape = (n, p.rc, 128)
    col_s = jnp.sum(
        jnp.where((iota(shape, 1) & (k - 1)) == iota(shape, 2), cols[:, None, :128], 0.0), axis=2, keepdims=True
    )
    shape = (n, p.rc, zc * p.bcols)
    lane = iota(shape, 2)
    g = one_hot(
        ((iota(shape, 1) >> log2(k)) == (lane >> log2(p.bcols)))
        & (col_s == mirror(lane & (p.bcols - 1)).astype(F32))
    ).reshape(p.rows, zc * p.bcols)
    force = []
    zero = jnp.zeros((p.ny, p.nx), F32)
    for z in range(zc):
        bz = [b[c][z] for c in range(3)]
        dy = {}
        for c in (0, 2):
            north, south = edge_rows(p, r_ref, nxt, prv, p.ru + (c * zc + z) * p.wrap)
            dy[c] = north - south
        dz = [zero, zero]
        for c in range(2):
            if z == zc - 1:
                dz[c] = dz[c] + hi_ref[c]
            if z == 0:
                dz[c] = dz[c] - lo_ref[c]
        j0 = j_ref[0, z] + (dy[2] - dz[1]) * 0.5
        j1 = j_ref[1, z] + dz[0] * 0.5
        j2 = j_ref[2, z] - dy[0] * 0.5
        force.append([j1 * bz[2] - j2 * bz[1], j2 * bz[0] - j0 * bz[2], j0 * bz[1] - j1 * bz[0]])
    for c in range(3):
        f_blk = jnp.concatenate([grid_to_blocks(p, force[z][c]) for z in range(zc)], axis=0)
        out[:, c * p.rc : (c + 1) * p.rc, :] = select(g, f_blk).reshape(n, p.rc, p.area)
    p_l, z_l, _ = lane_route(p)
    shape = (n, p.rows)
    col_l = jnp.sum(
        jnp.where(iota(shape, 0) == p_l.reshape(1, p.rows), tile_lanes(cols[:, :128], p.rows), 0.0), axis=0, keepdims=True
    )
    shape = (zc, p.bcols, p.rows)
    g = one_hot(
        (iota(shape, 0) == z_l) & (iota(shape, 1).astype(F32) == col_l.reshape(1, 1, p.rows))
    ).reshape(zc * p.bcols, p.rows)
    u = []
    for c in range(3):
        blk = select(g, r_ref[:, c * p.rc : (c + 1) * p.rc, :].reshape(p.rows, p.area))
        u.append([blocks_to_grid(p, blk[z * p.bcols : (z + 1) * p.bcols]) for z in range(zc)])
    for z in range(zc):
        uz, bz = [u[c][z] for c in range(3)], [b[c][z] for c in range(3)]
        ez = [uz[1] * bz[2] - uz[2] * bz[1], uz[2] * bz[0] - uz[0] * bz[2], uz[0] * bz[1] - uz[1] * bz[0]]
        for c in range(3):
            e_ref[c, z] = ez[c]
        if z == zc - 1:
            up_ref[0], up_ref[1], up_ref[2] = ez[0], ez[1], bz[2]
        if z == 0:
            down_ref[0], down_ref[1], down_ref[2] = ez[0], ez[1], bz[2]


def outer_velocity(p, r_ref):
    n, zc = p.n, p.zc
    at = p.ru + p.rb
    x = r_ref[:, at, :][:, 128:]
    spun = pltpu.roll(x, 64, 1)
    low = iota(x.shape, 1) < 64
    lane = iota((1, 1, p.rows), 2)
    place = lane & 7
    shape = (zc, p.bcols, p.rows)
    sides = []
    for d, (cols, i) in enumerate(((jnp.where(low, x, spun), (8 - place) & 7), (jnp.where(low, spun, x), 7 - place))):
        device = iota((n, p.rows), 0) == (lane >> 3).reshape(1, p.rows)
        col = jnp.sum(jnp.where(device, tile_lanes(cols, p.rows), 0.0), axis=0, keepdims=True)
        g = one_hot(
            (iota(shape, 0) == (i >> log2(p.k))) & (iota(shape, 1).astype(F32) == col.reshape(1, 1, p.rows))
        ).reshape(zc * p.bcols, p.rows)
        parts = []
        for c in range(3):
            m = r_ref[:, at + 1 + c, :][:, 128 * d : 128 * d + 128]
            parts.append(jnp.concatenate([spin(jnp.broadcast_to(m[r : r + 1], (8, 128))) for r in range(n)], axis=0))
        o = select(g, jnp.concatenate(parts, axis=1))
        side = []
        for c in range(3):
            blocks = o[:, 128 * c : 128 * c + 128]
            row = [lay_out(blocks[8 * t : 8 * t + 8], 0) for t in range(zc * p.bcols // 8)]
            per = p.bcols // 8
            side.append([jnp.concatenate(row[z * per : (z + 1) * per], axis=1) for z in range(zc)])
        sides.append(side)
    return sides


def local_kernel(p, r_ref, b_ref, lo_ref, hi_ref, e_ref, next_ref, w_ref):
    n, zc = p.n, p.zc
    me = lax.axis_index("xy")
    nxt, prv = lax.rem(me + 1, n), lax.rem(me + n - 1, n)
    zero = jnp.zeros((p.ny, p.nx), F32)
    outer_u = outer_velocity(p, r_ref)
    for z in range(zc):
        e = [e_ref[c, z] for c in range(3)]
        e0, e2 = [], []
        for u, device in zip(outer_u, (nxt, prv)):
            b = [row_of(p, r_ref, device, p.ru + (c * zc + z) * p.wrap) for c in range(3)]
            e0.append(u[1][z] * b[2] - u[2][z] * b[1])
            e2.append(u[0][z] * b[1] - u[1][z] * b[0])
        above = [e_ref[c, z + 1] if z < zc - 1 else zero for c in range(2)]
        below = [e_ref[c, z - 1] if z > 0 else zero for c in range(2)]
        curl = [
            (y_next(e[2], e2[0]) - y_prev(e[2], e2[1])) - (above[1] - below[1]),
            (above[0] - below[0]) - (x_next(e[2]) - x_prev(e[2])),
            (x_next(e[1]) - x_prev(e[1])) - (y_next(e[0], e0[0]) - y_prev(e[0], e0[1])),
        ]
        for c in range(3):
            north, south = edge_rows(p, r_ref, nxt, prv, p.ru + (c * zc + z) * p.wrap)
            total = curl[c] + north + south
            if c < 2 and z == 0:
                total = total + lo_ref[c]
            if c < 2 and z == zc - 1:
                total = total + hi_ref[c]
            next_ref[c, z] = b_ref[c, z] + 0.05 * total
    half_fine = p.edge * p.edge // 2
    half_area = p.area // 2
    ex = log2(p.edge)
    c, f = iota((half_area, half_fine), 0), iota((half_area, half_fine), 1)
    coarse = ((f >> (ex + 1)) << (ex - 1)) + ((f & (p.edge - 1)) >> 1)
    sel = one_hot(coarse == c)
    sel = jnp.concatenate([sel, sel], axis=0)
    w_ref[...] = sel


def finish_kernel(p, r_ref, g_ref, w_ref, v_ref, n_ref, lo_ref, hi_ref, vel_hbm, mag_hbm, vel, mag, sems):
    zc = p.zc
    copies = []
    for z in range(zc):
        dz = [jnp.zeros((p.ny, p.nx), F32)] * 2
        outer = dz[0]
        if z == zc - 1:
            dz = [dz[c] + hi_ref[c] for c in range(2)]
            outer = outer + hi_ref[2]
        if z == 0:
            dz = [dz[c] - lo_ref[c] for c in range(2)]
            outer = outer + lo_ref[2]
        mag[0, z] = n_ref[0, z] + 0.05 * -dz[1]
        mag[1, z] = n_ref[1, z] + 0.05 * dz[0]
        mag[2, z] = n_ref[2, z] + 0.05 * outer
    copies.append(pltpu.make_async_copy(mag, mag_hbm, sems.at[3]))
    copies[-1].start()
    half_fine = p.edge * p.edge // 2
    half_area = p.area // 2
    sel = w_ref[...]
    g = g_ref[...]
    ws = [slice(h * half_area, (h + 1) * half_area) for h in range(2)]
    s = p.slots
    m = zc * s
    for c in range(3):
        hi, lo = split(r_ref[:, c * p.rc : (c + 1) * p.rc, :].reshape(p.rows, p.area) * 0.1)
        parts = dot(g, jnp.concatenate([hi, lo], axis=1)).astype(BF16)
        hi, lo = parts[:, : p.area], parts[:, p.area :]
        pairs = [jnp.concatenate([hi[:, w], lo[:, w]], axis=1) for w in ws]
        add = dot(jnp.concatenate(pairs, axis=0), sel)
        for z in range(zc):
            for h in range(2):
                fw = slice(h * half_fine, (h + 1) * half_fine)
                part = add[h * m + z * s : h * m + (z + 1) * s]
                for d in range(2):
                    vel[c, 2 * z + d, :, fw] = v_ref[c, 2 * z + d, :, fw] + part
        copies.append(pltpu.make_async_copy(vel.at[c], vel_hbm.at[c], sems.at[c]))
        copies[-1].start()
    for copy in copies:
        copy.wait()


def struct(*shape, dtype=F32):
    return jax.ShapeDtypeStruct(shape, dtype)


def call(kernel, ins, outs, scratch=(), grant=20 << 20):
    return pl.pallas_call(
        kernel,
        out_shape=[o for o, _ in outs],
        in_specs=ins,
        out_specs=[spec for _, spec in outs],
        scratch_shapes=list(scratch),
        cost_estimate=pl.CostEstimate(flops=1 << 24, bytes_accessed=1 << 20, transcendentals=0),
        compiler_params=pltpu.CompilerParams(vmem_limit_bytes=grant),
    )


def ring(axis, step):
    n = lax.axis_size(axis)
    return [(i, (i + step) % n) for i in range(n)]


def planes(up, down):
    below = lax.ppermute(up, "gz", ring("gz", 1))
    above = lax.ppermute(down, "gz", ring("gz", -1))
    return below, above


def body(velocity, magnetic, slot_block_table):
    p = Plan(velocity.shape, magnetic.shape, lax.axis_size("xy"))
    plane = (p.ny, p.nx)
    dma = pltpu.SemaphoreType.DMA
    table = slot_block_table.reshape(1, p.slots)
    sent, up, down = call(
        functools.partial(restrict_kernel, p),
        [HBM] * 3,
        [(struct(p.n, p.r1, p.area), HBM), (struct(2, *plane), HBM), (struct(2, *plane), HBM)],
        [
            pltpu.VMEM(velocity.shape, F32),
            pltpu.VMEM((1, p.slots), jnp.int32),
            pltpu.VMEM(magnetic.shape, F32),
            pltpu.VMEM((p.n, p.r1, p.area), F32),
            pltpu.VMEM((-(-p.rb // 8) * 8, p.area), F32),
            pltpu.VMEM((-(-p.rb // 8) * 8, p.area), F32),
            dma((12,)),
        ],
        ALL_VMEM,
    )(velocity, table, magnetic)
    got = lax.all_to_all(sent, "xy", 0, 0, tiled=True)
    below, above = planes(up, down)
    held, held_table, _ = lax.optimization_barrier((magnetic, table, up))
    field, current, diffused, g3 = call(
        functools.partial(interior_kernel, p),
        [VMEM] * 2,
        [(struct(*magnetic.shape), VMEM)] * 3 + [(struct(p.zc * p.slots, p.rows, dtype=BF16), VMEM)],
    )(held, held_table)
    sent, emf, up, down = call(
        functools.partial(field_kernel, p),
        [VMEM] * 5,
        [
            (struct(p.n, p.ru, p.area), VMEM),
            (struct(*magnetic.shape), VMEM),
            (struct(3, *plane), VMEM),
            (struct(3, *plane), VMEM),
        ],
    )(got, field, current, below, above)
    got_force = lax.all_to_all(sent, "xy", 0, 0, tiled=True)
    emf_below, emf_above = planes(up, down)
    partial, widen = call(
        functools.partial(local_kernel, p), [VMEM] * 5, [(struct(*magnetic.shape), VMEM), (struct(p.area, p.edge * p.edge // 2, dtype=BF16), VMEM)]
    )(got, diffused, below, above, emf)
    return tuple(
        call(
            functools.partial(finish_kernel, p),
            [VMEM] * 7,
            [(struct(*velocity.shape), HBM), (struct(*magnetic.shape), HBM)],
            [pltpu.VMEM(velocity.shape, F32), pltpu.VMEM(magnetic.shape, F32), dma((4,))],
        )(got_force, g3, widen, velocity, partial, emf_below, emf_above)
    )


def solution(mesh):
    return jax.shard_map(
        body,
        mesh=mesh,
        in_specs=(P(None, "gz", "xy", None), P(None, "gz", "xy", None), P("xy")),
        out_specs=(P(None, "gz", "xy", None), P(None, "gz", "xy", None)),
        check_vma=False,
    )
```

```python
import functools
import math

import jax
import jax.numpy as jnp
from jax import lax
from jax.experimental import pallas as pl
from jax.experimental.pallas import tpu as pltpu
from jax.sharding import PartitionSpec as P

F32, BF16 = jnp.float32, jnp.bfloat16
VMEM = pl.BlockSpec(memory_space=pltpu.VMEM)
ALL_VMEM = 67043328
HBM = pl.BlockSpec(memory_space=pltpu.HBM)


def split(x):
    hi = x.astype(BF16)
    return hi, (x - hi.astype(F32)).astype(BF16)


def dot(a, b):
    return jnp.dot(a, b, preferred_element_type=F32)


def iota(shape, dim):
    return lax.broadcasted_iota(jnp.int32, shape, dim)


def one_hot(mask):
    return jnp.where(mask, 1.0, 0.0).astype(BF16)


def log2(x):
    assert x == 1 << (x.bit_length() - 1)
    return x.bit_length() - 1


class Plan:
    def __init__(self, vshape, bshape, n):
        self.n = n
        self.slots = vshape[2]
        self.k = self.slots // n
        self.zc = bshape[1]
        self.ny, self.nx = bshape[2:]
        self.edge = math.isqrt(vshape[3])
        self.half = self.edge // 2
        self.area = self.half * self.half
        self.bcols = self.nx // self.half
        self.rc = -(-self.zc * self.k // 8) * 8
        self.ru = 3 * self.rc
        self.rows = n * self.rc
        self.rb = 3 * self.zc * self.nx // self.area
        self.r1 = -(-(self.ru + self.rb + 4) // 8) * 8
        self.wrap = self.nx // self.area
        assert self.rc == 8 and self.area == 256 and self.half == 16


def mirror(i):
    return (i & ~7) | ((8 - (i & 7)) & 7)


def send_positions(p, table):
    s = p.slots
    row = jnp.broadcast_to((table >> log2(p.bcols)).astype(F32), (s, s))
    i, j = iota((s, s), 0), iota((s, s), 1)
    row_s = jnp.sum(jnp.where(i == j, row, 0.0), axis=1, keepdims=True)
    rank = jnp.sum(jnp.where((row_s == row) & (i < j), 1.0, 0.0), axis=0, keepdims=True)
    q = row[0:1] * p.k + rank
    q_s = jnp.sum(jnp.where(i == j, jnp.broadcast_to(q, (s, s)), 0.0), axis=1, keepdims=True)
    return q, q_s


def select(g, x):
    hi, lo = split(x)
    out = dot(g, jnp.concatenate([hi, lo], axis=1))
    return out[:, : x.shape[1]] + out[:, x.shape[1] :]


def spin(t):
    return pltpu.roll(t, 0, 1, stride=16, stride_axis=0)


def lay_out(t, first):
    t = spin(t)
    here = (iota(t.shape, 1) >> 4) == ((iota(t.shape, 0) + first) & 7)
    return jnp.sum(jnp.where(here, t, 0.0), axis=0, keepdims=True)


def tile_lanes(x, width):
    return x[:, :width] if width <= 128 else jnp.concatenate([x] * (width // 128), axis=1)


def lane_route(p):
    lane = iota((1, 1, p.rows), 2)
    i = lane & (p.rc - 1)
    return lane >> log2(p.rc), i >> log2(p.k), i & (p.k - 1)


def restrict_kernel(p, v_hbm, t_hbm, b_hbm, out_hbm, up_hbm, down_hbm, v_ref, t_ref, b_ref, out, last, first, sems):
    n, k, s, zc = p.n, p.k, p.slots, p.zc
    me = lax.axis_index("xy")
    t_copy = pltpu.make_async_copy(t_hbm, t_ref, sems.at[0])
    b_copy = pltpu.make_async_copy(b_hbm, b_ref, sems.at[1])
    v_copies = [pltpu.make_async_copy(v_hbm.at[c], v_ref.at[c], sems.at[2 + c]) for c in range(3)]
    t_copy.start()
    b_copy.start()
    for copy in v_copies:
        copy.start()
    half_fine = p.edge * p.edge // 2
    half_area = p.area // 2
    f, c = iota((half_fine, half_area), 0), iota((half_fine, half_area), 1)
    e = log2(p.edge)
    coarse = (mirror(f >> (e + 1)) << (e - 1)) + ((f & (p.edge - 1)) >> 1)
    sel = one_hot(coarse == c)
    t_copy.wait()
    table = t_ref[...]
    q, _ = send_positions(p, table)
    lanes = zc * s
    rep = one_hot((iota((s, lanes), 1) & (s - 1)) == iota((s, lanes), 0))
    qt = dot(jnp.broadcast_to(q, (8, s)).astype(BF16), rep)[0:1]
    shape = (n, p.rc, lanes)
    i = iota(shape, 1)
    target = (iota(shape, 0) * k + (i & (k - 1))).astype(F32)
    g = one_hot(((i >> log2(k)) == (iota(shape, 2) >> log2(s))) & (target == qt.reshape(1, 1, lanes)))
    g = g.reshape(p.rows, lanes)
    col = jnp.broadcast_to((table & (p.bcols - 1)).astype(F32), (s, s))
    qi = iota((s, s), 0).astype(F32)
    col_q = jnp.sum(jnp.where(qi == jnp.broadcast_to(q, (s, s)), col, 0.0), axis=1, keepdims=True)
    qa, la = iota((s, p.area), 0), iota((s, p.area), 1)
    place = jnp.where(la < 128, la, jnp.where(la < 192, -la, -1 - la)) & (k - 1)
    spread = jnp.where((qa & (k - 1)) == place, col_q, 0.0).astype(BF16)
    gather = one_hot((iota((n, s), 1) >> log2(k)) == iota((n, s), 0))
    cols = dot(gather, spread)
    at = p.ru + p.rb
    for r in range(n):
        north, south = (r + 1) % n, (r - 1) % n
        out[r, at : at + 1, :128] = cols[r : r + 1, :128]
        outer = jnp.where(iota((1, 128), 1) < 64, cols[north : north + 1, 128:], cols[south : south + 1, 128:])
        out[r, at : at + 1, 128:] = outer
    b_copy.wait()
    sends = [
        pltpu.make_async_copy(b_ref.at[0:2, zc - 1], up_hbm, sems.at[5]),
        pltpu.make_async_copy(b_ref.at[0:2, 0], down_hbm, sems.at[6]),
    ]
    for c in range(3):
        for z in range(zc):
            for h in range(p.wrap):
                at = (c * zc + z) * p.wrap + h
                w = slice(h * p.area, (h + 1) * p.area)
                last[at : at + 1, :] = b_ref[c, z, p.ny - 1 : p.ny, w]
                first[at : at + 1, :] = b_ref[c, z, 0:1, w]
    nxt = lax.rem(me + 1, n)
    for r in range(n):
        out[r, p.ru : p.ru + p.rb, :] = jnp.where(r == nxt, last[: p.rb], first[: p.rb])
    early = pl.ds(p.ru, 8)
    sends.append(pltpu.make_async_copy(out.at[:, early, :], out_hbm.at[:, early, :], sems.at[7]))
    for send in sends:
        send.start()
    averages = []
    m = zc * s
    ws = [slice(h * half_fine, (h + 1) * half_fine) for h in range(2)]
    for c in range(3):
        v_copies[c].wait()
        z_sum = jnp.concatenate([v_ref[c, 2 * z] + v_ref[c, 2 * z + 1] for z in range(zc)], axis=0)
        hi, lo = split(z_sum)
        o = dot(jnp.concatenate([x[:, w] for w in ws for x in (hi, lo)], axis=0), sel)
        u = [o[2 * h * m : (2 * h + 1) * m] + o[(2 * h + 1) * m : (2 * h + 2) * m] for h in range(2)]
        averages.append(jnp.concatenate(u, axis=1) * 0.125)
    for c in range(3):
        blocks = select(g, averages[c])
        out[:, c * p.rc : (c + 1) * p.rc, :] = blocks.reshape(n, p.rc, p.area)
        rows = pl.ds(c * p.rc, p.rc)
        sends.append(pltpu.make_async_copy(out.at[:, rows, :], out_hbm.at[:, rows, :], sems.at[8 + c]))
        sends[-1].start()
        at = p.ru + p.rb + 1 + c
        for r in range(n):
            tile = blocks[r * p.rc : (r + 1) * p.rc]
            out[(r - 1) % n, at : at + 1, :128] = lay_out(tile[:, :128], 0)
            out[(r + 1) % n, at : at + 1, 128:] = lay_out(tile[:, 128:], 1)
    late = pl.ds(p.ru + 8, p.r1 - p.ru - 8)
    sends.append(pltpu.make_async_copy(out.at[:, late, :], out_hbm.at[:, late, :], sems.at[11]))
    sends[-1].start()
    for send in sends:
        send.wait()


def tile_transpose(p, t):
    g = iota(t.shape, 1) >> log2(p.half)
    t = pltpu.roll(t, 0, 1, stride=p.half, stride_axis=0)
    for b in (1, 2, 4):
        t = jnp.where((g & b) != 0, pltpu.roll(t, 8 - b, 0), t)
    return pltpu.roll(t, 0, 1, stride=p.half, stride_axis=0)


def blocks_to_grid(p, blk):
    rows = []
    for yh in range(p.half // 8):
        rows.append(
            jnp.concatenate(
                [
                    tile_transpose(p, blk[8 * c : 8 * c + 8, 128 * yh : 128 * yh + 128])
                    for c in range(p.bcols // 8)
                ],
                axis=1,
            )
        )
    return jnp.concatenate(rows, axis=0)


def grid_to_blocks(p, grid):
    rows = []
    for c in range(p.bcols // 8):
        rows.append(
            jnp.concatenate(
                [
                    tile_transpose(p, grid[8 * yh : 8 * yh + 8, 128 * c : 128 * c + 128])
                    for yh in range(p.half // 8)
                ],
                axis=1,
            )
        )
    return jnp.concatenate(rows, axis=0)


def x_next(f):
    return pltpu.roll(f, f.shape[1] - 1, 1)


def x_prev(f):
    return pltpu.roll(f, 1, 1)


def y_next(f, halo):
    return jnp.where(iota(f.shape, 0) == f.shape[0] - 1, halo, pltpu.roll(f, f.shape[0] - 1, 0))


def y_prev(f, halo):
    return jnp.where(iota(f.shape, 0) == 0, halo, pltpu.roll(f, 1, 0))


def row_of(p, ref, src, at):
    return jnp.concatenate([ref[src, pl.ds(at + h, 1), :] for h in range(p.wrap)], axis=1)


def interior_kernel(p, b_ref, t_ref, copy_ref, j_ref, next_ref, g3_ref):
    s, k = p.slots, p.k
    _, q_s = send_positions(p, t_ref[...])
    r_l, z_l, j_l = lane_route(p)
    shape = (p.zc, s, p.rows)
    g3 = (iota(shape, 0) == z_l) & (q_s.reshape(1, s, 1) == (r_l * k + j_l).astype(F32))
    g3_ref[...] = one_hot(g3).reshape(p.zc * s, p.rows)
    zero = jnp.zeros((p.ny, p.nx), F32)
    for z in range(p.zc):
        b = [b_ref[c, z] for c in range(3)]
        below = [b_ref[c, z - 1] if z > 0 else zero for c in range(3)]
        above = [b_ref[c, z + 1] if z < p.zc - 1 else zero for c in range(3)]
        south, north = [y_prev(f, 0.0) for f in b], [y_next(f, 0.0) for f in b]
        west, east = [x_prev(f) for f in b], [x_next(f) for f in b]
        j_ref[0, z] = ((north[2] - south[2]) - (above[1] - below[1])) * 0.5
        j_ref[1, z] = ((above[0] - below[0]) - (east[2] - west[2])) * 0.5
        j_ref[2, z] = ((east[1] - west[1]) - (north[0] - south[0])) * 0.5
        for c in range(3):
            lap = below[c] + above[c] + south[c] + north[c] + west[c] + east[c] - 6.0 * b[c]
            next_ref[c, z] = b[c] + 0.05 * lap
            copy_ref[c, z] = b[c]


def edge_rows(p, ref, nxt, prv, at):
    y = iota((p.ny, p.nx), 0)
    north = jnp.where(y == p.ny - 1, row_of(p, ref, nxt, at), 0.0)
    return north, jnp.where(y == 0, row_of(p, ref, prv, at), 0.0)


def field_kernel(p, r_ref, b_ref, j_ref, lo_ref, hi_ref, out, e_ref, up_ref, down_ref):
    n, k, zc = p.n, p.k, p.zc
    me = lax.axis_index("xy")
    nxt, prv = lax.rem(me + 1, n), lax.rem(me + n - 1, n)
    b = [[b_ref[c, z] for z in range(zc)] for c in range(3)]
    cols = r_ref[:, p.ru + p.rb, :]
    shape = (n, p.rc, 128)
    col_s = jnp.sum(
        jnp.where((iota(shape, 1) & (k - 1)) == iota(shape, 2), cols[:, None, :128], 0.0), axis=2, keepdims=True
    )
    shape = (n, p.rc, zc * p.bcols)
    lane = iota(shape, 2)
    g = one_hot(
        ((iota(shape, 1) >> log2(k)) == (lane >> log2(p.bcols)))
        & (col_s == mirror(lane & (p.bcols - 1)).astype(F32))
    ).reshape(p.rows, zc * p.bcols)
    force = []
    zero = jnp.zeros((p.ny, p.nx), F32)
    for z in range(zc):
        bz = [b[c][z] for c in range(3)]
        dy = {}
        for c in (0, 2):
            north, south = edge_rows(p, r_ref, nxt, prv, p.ru + (c * zc + z) * p.wrap)
            dy[c] = north - south
        dz = [zero, zero]
        for c in range(2):
            if z == zc - 1:
                dz[c] = dz[c] + hi_ref[c]
            if z == 0:
                dz[c] = dz[c] - lo_ref[c]
        j0 = j_ref[0, z] + (dy[2] - dz[1]) * 0.5
        j1 = j_ref[1, z] + dz[0] * 0.5
        j2 = j_ref[2, z] - dy[0] * 0.5
        force.append([j1 * bz[2] - j2 * bz[1], j2 * bz[0] - j0 * bz[2], j0 * bz[1] - j1 * bz[0]])
    for c in range(3):
        f_blk = jnp.concatenate([grid_to_blocks(p, force[z][c]) for z in range(zc)], axis=0)
        out[:, c * p.rc : (c + 1) * p.rc, :] = select(g, f_blk).reshape(n, p.rc, p.area)
    p_l, z_l, _ = lane_route(p)
    shape = (n, p.rows)
    col_l = jnp.sum(
        jnp.where(iota(shape, 0) == p_l.reshape(1, p.rows), tile_lanes(cols[:, :128], p.rows), 0.0), axis=0, keepdims=True
    )
    shape = (zc, p.bcols, p.rows)
    g = one_hot(
        (iota(shape, 0) == z_l) & (iota(shape, 1).astype(F32) == col_l.reshape(1, 1, p.rows))
    ).reshape(zc * p.bcols, p.rows)
    u = []
    for c in range(3):
        blk = select(g, r_ref[:, c * p.rc : (c + 1) * p.rc, :].reshape(p.rows, p.area))
        u.append([blocks_to_grid(p, blk[z * p.bcols : (z + 1) * p.bcols]) for z in range(zc)])
    for z in range(zc):
        uz, bz = [u[c][z] for c in range(3)], [b[c][z] for c in range(3)]
        ez = [uz[1] * bz[2] - uz[2] * bz[1], uz[2] * bz[0] - uz[0] * bz[2], uz[0] * bz[1] - uz[1] * bz[0]]
        for c in range(3):
            e_ref[c, z] = ez[c]
        if z == zc - 1:
            up_ref[0], up_ref[1], up_ref[2] = ez[0], ez[1], bz[2]
        if z == 0:
            down_ref[0], down_ref[1], down_ref[2] = ez[0], ez[1], bz[2]


def outer_velocity(p, r_ref):
    n, zc = p.n, p.zc
    at = p.ru + p.rb
    x = r_ref[:, at, :][:, 128:]
    spun = pltpu.roll(x, 64, 1)
    low = iota(x.shape, 1) < 64
    lane = iota((1, 1, p.rows), 2)
    place = lane & 7
    shape = (zc, p.bcols, p.rows)
    sides = []
    for d, (cols, i) in enumerate(((jnp.where(low, x, spun), (8 - place) & 7), (jnp.where(low, spun, x), 7 - place))):
        device = iota((n, p.rows), 0) == (lane >> 3).reshape(1, p.rows)
        col = jnp.sum(jnp.where(device, tile_lanes(cols, p.rows), 0.0), axis=0, keepdims=True)
        g = one_hot(
            (iota(shape, 0) == (i >> log2(p.k))) & (iota(shape, 1).astype(F32) == col.reshape(1, 1, p.rows))
        ).reshape(zc * p.bcols, p.rows)
        parts = []
        for c in range(3):
            m = r_ref[:, at + 1 + c, :][:, 128 * d : 128 * d + 128]
            parts.append(jnp.concatenate([spin(jnp.broadcast_to(m[r : r + 1], (8, 128))) for r in range(n)], axis=0))
        o = select(g, jnp.concatenate(parts, axis=1))
        side = []
        for c in range(3):
            blocks = o[:, 128 * c : 128 * c + 128]
            row = [lay_out(blocks[8 * t : 8 * t + 8], 0) for t in range(zc * p.bcols // 8)]
            per = p.bcols // 8
            side.append([jnp.concatenate(row[z * per : (z + 1) * per], axis=1) for z in range(zc)])
        sides.append(side)
    return sides


def local_kernel(p, r_ref, b_ref, lo_ref, hi_ref, e_ref, next_ref, w_ref):
    n, zc = p.n, p.zc
    me = lax.axis_index("xy")
    nxt, prv = lax.rem(me + 1, n), lax.rem(me + n - 1, n)
    zero = jnp.zeros((p.ny, p.nx), F32)
    outer_u = outer_velocity(p, r_ref)
    for z in range(zc):
        e = [e_ref[c, z] for c in range(3)]
        e0, e2 = [], []
        for u, device in zip(outer_u, (nxt, prv)):
            b = [row_of(p, r_ref, device, p.ru + (c * zc + z) * p.wrap) for c in range(3)]
            e0.append(u[1][z] * b[2] - u[2][z] * b[1])
            e2.append(u[0][z] * b[1] - u[1][z] * b[0])
        above = [e_ref[c, z + 1] if z < zc - 1 else zero for c in range(2)]
        below = [e_ref[c, z - 1] if z > 0 else zero for c in range(2)]
        curl = [
            (y_next(e[2], e2[0]) - y_prev(e[2], e2[1])) - (above[1] - below[1]),
            (above[0] - below[0]) - (x_next(e[2]) - x_prev(e[2])),
            (x_next(e[1]) - x_prev(e[1])) - (y_next(e[0], e0[0]) - y_prev(e[0], e0[1])),
        ]
        for c in range(3):
            north, south = edge_rows(p, r_ref, nxt, prv, p.ru + (c * zc + z) * p.wrap)
            total = curl[c] + north + south
            if c < 2 and z == 0:
                total = total + lo_ref[c]
            if c < 2 and z == zc - 1:
                total = total + hi_ref[c]
            next_ref[c, z] = b_ref[c, z] + 0.05 * total
    half_fine = p.edge * p.edge // 2
    half_area = p.area // 2
    ex = log2(p.edge)
    c, f = iota((half_area, half_fine), 0), iota((half_area, half_fine), 1)
    coarse = ((f >> (ex + 1)) << (ex - 1)) + ((f & (p.edge - 1)) >> 1)
    sel = one_hot(coarse == c)
    sel = jnp.concatenate([sel, sel], axis=0)
    w_ref[...] = sel


def finish_kernel(p, r_ref, g_ref, w_ref, v_ref, n_ref, lo_ref, hi_ref, vel_hbm, mag_hbm, vel, mag, sems):
    zc = p.zc
    copies = []
    for z in range(zc):
        dz = [jnp.zeros((p.ny, p.nx), F32)] * 2
        outer = dz[0]
        if z == zc - 1:
            dz = [dz[c] + hi_ref[c] for c in range(2)]
            outer = outer + hi_ref[2]
        if z == 0:
            dz = [dz[c] - lo_ref[c] for c in range(2)]
            outer = outer + lo_ref[2]
        mag[0, z] = n_ref[0, z] + 0.05 * -dz[1]
        mag[1, z] = n_ref[1, z] + 0.05 * dz[0]
        mag[2, z] = n_ref[2, z] + 0.05 * outer
    copies.append(pltpu.make_async_copy(mag, mag_hbm, sems.at[3]))
    copies[-1].start()
    half_fine = p.edge * p.edge // 2
    half_area = p.area // 2
    sel = w_ref[...]
    g = g_ref[...]
    ws = [slice(h * half_area, (h + 1) * half_area) for h in range(2)]
    s = p.slots
    m = zc * s
    for c in range(3):
        hi, lo = split(r_ref[:, c * p.rc : (c + 1) * p.rc, :].reshape(p.rows, p.area) * 0.1)
        parts = dot(g, jnp.concatenate([hi, lo], axis=1)).astype(BF16)
        hi, lo = parts[:, : p.area], parts[:, p.area :]
        pairs = [jnp.concatenate([hi[:, w], lo[:, w]], axis=1) for w in ws]
        add = dot(jnp.concatenate(pairs, axis=0), sel)
        for z in range(zc):
            for h in range(2):
                fw = slice(h * half_fine, (h + 1) * half_fine)
                part = add[h * m + z * s : h * m + (z + 1) * s]
                for d in range(2):
                    vel[c, 2 * z + d, :, fw] = v_ref[c, 2 * z + d, :, fw] + part
        copies.append(pltpu.make_async_copy(vel.at[c], vel_hbm.at[c], sems.at[c]))
        copies[-1].start()
    for copy in copies:
        copy.wait()


def struct(*shape, dtype=F32):
    return jax.ShapeDtypeStruct(shape, dtype)


def call(kernel, ins, outs, scratch=(), grant=20 << 20):
    return pl.pallas_call(
        kernel,
        out_shape=[o for o, _ in outs],
        in_specs=ins,
        out_specs=[spec for _, spec in outs],
        scratch_shapes=list(scratch),
        cost_estimate=pl.CostEstimate(flops=1 << 24, bytes_accessed=1 << 20, transcendentals=0),
        compiler_params=pltpu.CompilerParams(vmem_limit_bytes=grant),
    )


def ring(axis, step):
    n = lax.axis_size(axis)
    return [(i, (i + step) % n) for i in range(n)]


def planes(up, down):
    below = lax.ppermute(up, "gz", ring("gz", 1))
    above = lax.ppermute(down, "gz", ring("gz", -1))
    return below, above


def body(velocity, magnetic, slot_block_table):
    p = Plan(velocity.shape, magnetic.shape, lax.axis_size("xy"))
    plane = (p.ny, p.nx)
    dma = pltpu.SemaphoreType.DMA
    table = slot_block_table.reshape(1, p.slots)
    sent, up, down = call(
        functools.partial(restrict_kernel, p),
        [HBM] * 3,
        [(struct(p.n, p.r1, p.area), HBM), (struct(2, *plane), HBM), (struct(2, *plane), HBM)],
        [
            pltpu.VMEM(velocity.shape, F32),
            pltpu.VMEM((1, p.slots), jnp.int32),
            pltpu.VMEM(magnetic.shape, F32),
            pltpu.VMEM((p.n, p.r1, p.area), F32),
            pltpu.VMEM((-(-p.rb // 8) * 8, p.area), F32),
            pltpu.VMEM((-(-p.rb // 8) * 8, p.area), F32),
            dma((12,)),
        ],
        ALL_VMEM,
    )(velocity, table, magnetic)
    got = lax.all_to_all(sent, "xy", 0, 0, tiled=True)
    below, above = planes(up, down)
    held, held_table, _ = lax.optimization_barrier((magnetic, table, up))
    field, current, diffused, g3 = call(
        functools.partial(interior_kernel, p),
        [VMEM] * 2,
        [(struct(*magnetic.shape), VMEM)] * 3 + [(struct(p.zc * p.slots, p.rows, dtype=BF16), VMEM)],
    )(held, held_table)
    sent, emf, up, down = call(
        functools.partial(field_kernel, p),
        [VMEM] * 5,
        [
            (struct(p.n, p.ru, p.area), VMEM),
            (struct(*magnetic.shape), VMEM),
            (struct(3, *plane), VMEM),
            (struct(3, *plane), VMEM),
        ],
    )(got, field, current, below, above)
    got_force = lax.all_to_all(sent, "xy", 0, 0, tiled=True)
    emf_below, emf_above = planes(up, down)
    partial, widen = call(
        functools.partial(local_kernel, p), [VMEM] * 5, [(struct(*magnetic.shape), VMEM), (struct(p.area, p.edge * p.edge // 2, dtype=BF16), VMEM)]
    )(got, diffused, below, above, emf)
    return tuple(
        call(
            functools.partial(finish_kernel, p),
            [VMEM] * 7,
            [(struct(*velocity.shape), HBM), (struct(*magnetic.shape), HBM)],
            [pltpu.VMEM(velocity.shape, F32), pltpu.VMEM(magnetic.shape, F32), dma((4,))],
        )(got_force, g3, widen, velocity, partial, emf_below, emf_above)
    )


def solution(mesh):
    return jax.shard_map(
        body,
        mesh=mesh,
        in_specs=(P(None, "gz", "xy", None), P(None, "gz", "xy", None), P("xy")),
        out_specs=(P(None, "gz", "xy", None), P(None, "gz", "xy", None)),
        check_vma=False,
    )
```

```python
import functools
import math

import jax
import jax.numpy as jnp
from jax import lax
from jax.experimental import pallas as pl
from jax.experimental.pallas import tpu as pltpu
from jax.sharding import PartitionSpec as P

F32, BF16 = jnp.float32, jnp.bfloat16
VMEM = pl.BlockSpec(memory_space=pltpu.VMEM)
ALL_VMEM = 67043328
HBM = pl.BlockSpec(memory_space=pltpu.HBM)


def split(x):
    hi = x.astype(BF16)
    return hi, (x - hi.astype(F32)).astype(BF16)


def dot(a, b):
    return jnp.dot(a, b, preferred_element_type=F32)


def iota(shape, dim):
    return lax.broadcasted_iota(jnp.int32, shape, dim)


def one_hot(mask):
    return jnp.where(mask, 1.0, 0.0).astype(BF16)


def log2(x):
    assert x == 1 << (x.bit_length() - 1)
    return x.bit_length() - 1


class Plan:
    def __init__(self, vshape, bshape, n):
        self.n = n
        self.slots = vshape[2]
        self.k = self.slots // n
        self.zc = bshape[1]
        self.ny, self.nx = bshape[2:]
        self.edge = math.isqrt(vshape[3])
        self.half = self.edge // 2
        self.area = self.half * self.half
        self.bcols = self.nx // self.half
        self.rc = -(-self.zc * self.k // 8) * 8
        self.ru = 3 * self.rc
        self.rows = n * self.rc
        self.rb = 3 * self.zc * self.nx // self.area
        self.r1 = -(-(self.ru + self.rb + 4) // 8) * 8
        self.wrap = self.nx // self.area
        assert self.rc == 8 and self.area == 256 and self.half == 16


def mirror(i):
    return (i & ~7) | ((8 - (i & 7)) & 7)


def send_positions(p, table):
    s = p.slots
    row = jnp.broadcast_to((table >> log2(p.bcols)).astype(F32), (s, s))
    i, j = iota((s, s), 0), iota((s, s), 1)
    row_s = jnp.sum(jnp.where(i == j, row, 0.0), axis=1, keepdims=True)
    rank = jnp.sum(jnp.where((row_s == row) & (i < j), 1.0, 0.0), axis=0, keepdims=True)
    q = row[0:1] * p.k + rank
    q_s = jnp.sum(jnp.where(i == j, jnp.broadcast_to(q, (s, s)), 0.0), axis=1, keepdims=True)
    return q, q_s


def select(g, x):
    hi, lo = split(x)
    out = dot(g, jnp.concatenate([hi, lo], axis=1))
    return out[:, : x.shape[1]] + out[:, x.shape[1] :]


def spin(t):
    return pltpu.roll(t, 0, 1, stride=16, stride_axis=0)


def lay_out(t, first):
    t = spin(t)
    here = (iota(t.shape, 1) >> 4) == ((iota(t.shape, 0) + first) & 7)
    return jnp.sum(jnp.where(here, t, 0.0), axis=0, keepdims=True)


def tile_lanes(x, width):
    return x[:, :width] if width <= 128 else jnp.concatenate([x] * (width // 128), axis=1)


def lane_route(p):
    lane = iota((1, 1, p.rows), 2)
    i = lane & (p.rc - 1)
    return lane >> log2(p.rc), i >> log2(p.k), i & (p.k - 1)


def restrict_kernel(p, v_hbm, t_hbm, b_hbm, out_hbm, up_hbm, down_hbm, v_ref, t_ref, b_ref, out, last, first, sems):
    n, k, s, zc = p.n, p.k, p.slots, p.zc
    me = lax.axis_index("xy")
    t_copy = pltpu.make_async_copy(t_hbm, t_ref, sems.at[0])
    b_copy = pltpu.make_async_copy(b_hbm, b_ref, sems.at[1])
    v_copies = [pltpu.make_async_copy(v_hbm.at[c], v_ref.at[c], sems.at[2 + c]) for c in range(3)]
    t_copy.start()
    b_copy.start()
    for copy in v_copies:
        copy.start()
    half_fine = p.edge * p.edge // 2
    half_area = p.area // 2
    f, c = iota((half_fine, half_area), 0), iota((half_fine, half_area), 1)
    e = log2(p.edge)
    coarse = (mirror(f >> (e + 1)) << (e - 1)) + ((f & (p.edge - 1)) >> 1)
    sel = one_hot(coarse == c)
    t_copy.wait()
    table = t_ref[...]
    q, _ = send_positions(p, table)
    lanes = zc * s
    rep = one_hot((iota((s, lanes), 1) & (s - 1)) == iota((s, lanes), 0))
    qt = dot(jnp.broadcast_to(q, (8, s)).astype(BF16), rep)[0:1]
    shape = (n, p.rc, lanes)
    i = iota(shape, 1)
    target = (iota(shape, 0) * k + (i & (k - 1))).astype(F32)
    g = one_hot(((i >> log2(k)) == (iota(shape, 2) >> log2(s))) & (target == qt.reshape(1, 1, lanes)))
    g = g.reshape(p.rows, lanes)
    col = jnp.broadcast_to((table & (p.bcols - 1)).astype(F32), (s, s))
    qi = iota((s, s), 0).astype(F32)
    col_q = jnp.sum(jnp.where(qi == jnp.broadcast_to(q, (s, s)), col, 0.0), axis=1, keepdims=True)
    qa, la = iota((s, p.area), 0), iota((s, p.area), 1)
    place = jnp.where(la < 128, la, jnp.where(la < 192, -la, -1 - la)) & (k - 1)
    spread = jnp.where((qa & (k - 1)) == place, col_q, 0.0).astype(BF16)
    gather = one_hot((iota((n, s), 1) >> log2(k)) == iota((n, s), 0))
    cols = dot(gather, spread)
    at = p.ru + p.rb
    for r in range(n):
        north, south = (r + 1) % n, (r - 1) % n
        out[r, at : at + 1, :128] = cols[r : r + 1, :128]
        outer = jnp.where(iota((1, 128), 1) < 64, cols[north : north + 1, 128:], cols[south : south + 1, 128:])
        out[r, at : at + 1, 128:] = outer
    b_copy.wait()
    sends = [
        pltpu.make_async_copy(b_ref.at[0:2, zc - 1], up_hbm, sems.at[5]),
        pltpu.make_async_copy(b_ref.at[0:2, 0], down_hbm, sems.at[6]),
    ]
    for c in range(3):
        for z in range(zc):
            for h in range(p.wrap):
                at = (c * zc + z) * p.wrap + h
                w = slice(h * p.area, (h + 1) * p.area)
                last[at : at + 1, :] = b_ref[c, z, p.ny - 1 : p.ny, w]
                first[at : at + 1, :] = b_ref[c, z, 0:1, w]
    nxt = lax.rem(me + 1, n)
    for r in range(n):
        out[r, p.ru : p.ru + p.rb, :] = jnp.where(r == nxt, last[: p.rb], first[: p.rb])
    early = pl.ds(p.ru, 8)
    sends.append(pltpu.make_async_copy(out.at[:, early, :], out_hbm.at[:, early, :], sems.at[7]))
    for send in sends:
        send.start()
    averages = []
    m = zc * s
    ws = [slice(h * half_fine, (h + 1) * half_fine) for h in range(2)]
    for c in range(3):
        v_copies[c].wait()
        z_sum = jnp.concatenate([v_ref[c, 2 * z] + v_ref[c, 2 * z + 1] for z in range(zc)], axis=0)
        hi, lo = split(z_sum)
        o = dot(jnp.concatenate([x[:, w] for w in ws for x in (hi, lo)], axis=0), sel)
        u = [o[2 * h * m : (2 * h + 1) * m] + o[(2 * h + 1) * m : (2 * h + 2) * m] for h in range(2)]
        averages.append(jnp.concatenate(u, axis=1) * 0.125)
    for c in range(3):
        blocks = select(g, averages[c])
        out[:, c * p.rc : (c + 1) * p.rc, :] = blocks.reshape(n, p.rc, p.area)
        rows = pl.ds(c * p.rc, p.rc)
        sends.append(pltpu.make_async_copy(out.at[:, rows, :], out_hbm.at[:, rows, :], sems.at[8 + c]))
        sends[-1].start()
        at = p.ru + p.rb + 1 + c
        for r in range(n):
            tile = blocks[r * p.rc : (r + 1) * p.rc]
            out[(r - 1) % n, at : at + 1, :128] = lay_out(tile[:, :128], 0)
            out[(r + 1) % n, at : at + 1, 128:] = lay_out(tile[:, 128:], 1)
    late = pl.ds(p.ru + 8, p.r1 - p.ru - 8)
    sends.append(pltpu.make_async_copy(out.at[:, late, :], out_hbm.at[:, late, :], sems.at[11]))
    sends[-1].start()
    for send in sends:
        send.wait()


def tile_transpose(p, t):
    g = iota(t.shape, 1) >> log2(p.half)
    t = pltpu.roll(t, 0, 1, stride=p.half, stride_axis=0)
    for b in (1, 2, 4):
        t = jnp.where((g & b) != 0, pltpu.roll(t, 8 - b, 0), t)
    return pltpu.roll(t, 0, 1, stride=p.half, stride_axis=0)


def blocks_to_grid(p, blk):
    rows = []
    for yh in range(p.half // 8):
        rows.append(
            jnp.concatenate(
                [
                    tile_transpose(p, blk[8 * c : 8 * c + 8, 128 * yh : 128 * yh + 128])
                    for c in range(p.bcols // 8)
                ],
                axis=1,
            )
        )
    return jnp.concatenate(rows, axis=0)


def grid_to_blocks(p, grid):
    rows = []
    for c in range(p.bcols // 8):
        rows.append(
            jnp.concatenate(
                [
                    tile_transpose(p, grid[8 * yh : 8 * yh + 8, 128 * c : 128 * c + 128])
                    for yh in range(p.half // 8)
                ],
                axis=1,
            )
        )
    return jnp.concatenate(rows, axis=0)


def x_next(f):
    return pltpu.roll(f, f.shape[1] - 1, 1)


def x_prev(f):
    return pltpu.roll(f, 1, 1)


def y_next(f, halo):
    return jnp.where(iota(f.shape, 0) == f.shape[0] - 1, halo, pltpu.roll(f, f.shape[0] - 1, 0))


def y_prev(f, halo):
    return jnp.where(iota(f.shape, 0) == 0, halo, pltpu.roll(f, 1, 0))


def row_of(p, ref, src, at):
    return jnp.concatenate([ref[src, pl.ds(at + h, 1), :] for h in range(p.wrap)], axis=1)


def interior_kernel(p, b_ref, t_ref, copy_ref, j_ref, next_ref, g3_ref):
    s, k = p.slots, p.k
    _, q_s = send_positions(p, t_ref[...])
    r_l, z_l, j_l = lane_route(p)
    shape = (p.zc, s, p.rows)
    g3 = (iota(shape, 0) == z_l) & (q_s.reshape(1, s, 1) == (r_l * k + j_l).astype(F32))
    g3_ref[...] = one_hot(g3).reshape(p.zc * s, p.rows)
    zero = jnp.zeros((p.ny, p.nx), F32)
    for z in range(p.zc):
        b = [b_ref[c, z] for c in range(3)]
        below = [b_ref[c, z - 1] if z > 0 else zero for c in range(3)]
        above = [b_ref[c, z + 1] if z < p.zc - 1 else zero for c in range(3)]
        south, north = [y_prev(f, 0.0) for f in b], [y_next(f, 0.0) for f in b]
        west, east = [x_prev(f) for f in b], [x_next(f) for f in b]
        j_ref[0, z] = ((north[2] - south[2]) - (above[1] - below[1])) * 0.5
        j_ref[1, z] = ((above[0] - below[0]) - (east[2] - west[2])) * 0.5
        j_ref[2, z] = ((east[1] - west[1]) - (north[0] - south[0])) * 0.5
        for c in range(3):
            lap = below[c] + above[c] + south[c] + north[c] + west[c] + east[c] - 6.0 * b[c]
            next_ref[c, z] = b[c] + 0.05 * lap
            copy_ref[c, z] = b[c]


def edge_rows(p, ref, nxt, prv, at):
    y = iota((p.ny, p.nx), 0)
    north = jnp.where(y == p.ny - 1, row_of(p, ref, nxt, at), 0.0)
    return north, jnp.where(y == 0, row_of(p, ref, prv, at), 0.0)


def field_kernel(p, r_ref, b_ref, j_ref, lo_ref, hi_ref, out, e_ref, up_ref, down_ref):
    n, k, zc = p.n, p.k, p.zc
    me = lax.axis_index("xy")
    nxt, prv = lax.rem(me + 1, n), lax.rem(me + n - 1, n)
    b = [[b_ref[c, z] for z in range(zc)] for c in range(3)]
    cols = r_ref[:, p.ru + p.rb, :]
    shape = (n, p.rc, 128)
    col_s = jnp.sum(
        jnp.where((iota(shape, 1) & (k - 1)) == iota(shape, 2), cols[:, None, :128], 0.0), axis=2, keepdims=True
    )
    shape = (n, p.rc, zc * p.bcols)
    lane = iota(shape, 2)
    g = one_hot(
        ((iota(shape, 1) >> log2(k)) == (lane >> log2(p.bcols)))
        & (col_s == mirror(lane & (p.bcols - 1)).astype(F32))
    ).reshape(p.rows, zc * p.bcols)
    force = []
    zero = jnp.zeros((p.ny, p.nx), F32)
    for z in range(zc):
        bz = [b[c][z] for c in range(3)]
        dy = {}
        for c in (0, 2):
            north, south = edge_rows(p, r_ref, nxt, prv, p.ru + (c * zc + z) * p.wrap)
            dy[c] = north - south
        dz = [zero, zero]
        for c in range(2):
            if z == zc - 1:
                dz[c] = dz[c] + hi_ref[c]
            if z == 0:
                dz[c] = dz[c] - lo_ref[c]
        j0 = j_ref[0, z] + (dy[2] - dz[1]) * 0.5
        j1 = j_ref[1, z] + dz[0] * 0.5
        j2 = j_ref[2, z] - dy[0] * 0.5
        force.append([j1 * bz[2] - j2 * bz[1], j2 * bz[0] - j0 * bz[2], j0 * bz[1] - j1 * bz[0]])
    for c in range(3):
        f_blk = jnp.concatenate([grid_to_blocks(p, force[z][c]) for z in range(zc)], axis=0)
        out[:, c * p.rc : (c + 1) * p.rc, :] = select(g, f_blk).reshape(n, p.rc, p.area)
    p_l, z_l, _ = lane_route(p)
    shape = (n, p.rows)
    col_l = jnp.sum(
        jnp.where(iota(shape, 0) == p_l.reshape(1, p.rows), tile_lanes(cols[:, :128], p.rows), 0.0), axis=0, keepdims=True
    )
    shape = (zc, p.bcols, p.rows)
    g = one_hot(
        (iota(shape, 0) == z_l) & (iota(shape, 1).astype(F32) == col_l.reshape(1, 1, p.rows))
    ).reshape(zc * p.bcols, p.rows)
    u = []
    for c in range(3):
        blk = select(g, r_ref[:, c * p.rc : (c + 1) * p.rc, :].reshape(p.rows, p.area))
        u.append([blocks_to_grid(p, blk[z * p.bcols : (z + 1) * p.bcols]) for z in range(zc)])
    for z in range(zc):
        uz, bz = [u[c][z] for c in range(3)], [b[c][z] for c in range(3)]
        ez = [uz[1] * bz[2] - uz[2] * bz[1], uz[2] * bz[0] - uz[0] * bz[2], uz[0] * bz[1] - uz[1] * bz[0]]
        for c in range(3):
            e_ref[c, z] = ez[c]
        if z == zc - 1:
            up_ref[0], up_ref[1], up_ref[2] = ez[0], ez[1], bz[2]
        if z == 0:
            down_ref[0], down_ref[1], down_ref[2] = ez[0], ez[1], bz[2]


def outer_velocity(p, r_ref):
    n, zc = p.n, p.zc
    at = p.ru + p.rb
    x = r_ref[:, at, :][:, 128:]
    spun = pltpu.roll(x, 64, 1)
    low = iota(x.shape, 1) < 64
    lane = iota((1, 1, p.rows), 2)
    place = lane & 7
    shape = (zc, p.bcols, p.rows)
    sides = []
    for d, (cols, i) in enumerate(((jnp.where(low, x, spun), (8 - place) & 7), (jnp.where(low, spun, x), 7 - place))):
        device = iota((n, p.rows), 0) == (lane >> 3).reshape(1, p.rows)
        col = jnp.sum(jnp.where(device, tile_lanes(cols, p.rows), 0.0), axis=0, keepdims=True)
        g = one_hot(
            (iota(shape, 0) == (i >> log2(p.k))) & (iota(shape, 1).astype(F32) == col.reshape(1, 1, p.rows))
        ).reshape(zc * p.bcols, p.rows)
        parts = []
        for c in range(3):
            m = r_ref[:, at + 1 + c, :][:, 128 * d : 128 * d + 128]
            parts.append(jnp.concatenate([spin(jnp.broadcast_to(m[r : r + 1], (8, 128))) for r in range(n)], axis=0))
        o = select(g, jnp.concatenate(parts, axis=1))
        side = []
        for c in range(3):
            blocks = o[:, 128 * c : 128 * c + 128]
            row = [lay_out(blocks[8 * t : 8 * t + 8], 0) for t in range(zc * p.bcols // 8)]
            per = p.bcols // 8
            side.append([jnp.concatenate(row[z * per : (z + 1) * per], axis=1) for z in range(zc)])
        sides.append(side)
    return sides


def local_kernel(p, r_ref, b_ref, lo_ref, hi_ref, e_ref, next_ref, w_ref):
    n, zc = p.n, p.zc
    me = lax.axis_index("xy")
    nxt, prv = lax.rem(me + 1, n), lax.rem(me + n - 1, n)
    zero = jnp.zeros((p.ny, p.nx), F32)
    outer_u = outer_velocity(p, r_ref)
    for z in range(zc):
        e = [e_ref[c, z] for c in range(3)]
        e0, e2 = [], []
        for u, device in zip(outer_u, (nxt, prv)):
            b = [row_of(p, r_ref, device, p.ru + (c * zc + z) * p.wrap) for c in range(3)]
            e0.append(u[1][z] * b[2] - u[2][z] * b[1])
            e2.append(u[0][z] * b[1] - u[1][z] * b[0])
        above = [e_ref[c, z + 1] if z < zc - 1 else zero for c in range(2)]
        below = [e_ref[c, z - 1] if z > 0 else zero for c in range(2)]
        curl = [
            (y_next(e[2], e2[0]) - y_prev(e[2], e2[1])) - (above[1] - below[1]),
            (above[0] - below[0]) - (x_next(e[2]) - x_prev(e[2])),
            (x_next(e[1]) - x_prev(e[1])) - (y_next(e[0], e0[0]) - y_prev(e[0], e0[1])),
        ]
        for c in range(3):
            north, south = edge_rows(p, r_ref, nxt, prv, p.ru + (c * zc + z) * p.wrap)
            total = curl[c] + north + south
            if c < 2 and z == 0:
                total = total + lo_ref[c]
            if c < 2 and z == zc - 1:
                total = total + hi_ref[c]
            next_ref[c, z] = b_ref[c, z] + 0.05 * total
    half_fine = p.edge * p.edge // 2
    half_area = p.area // 2
    ex = log2(p.edge)
    c, f = iota((half_area, half_fine), 0), iota((half_area, half_fine), 1)
    coarse = ((f >> (ex + 1)) << (ex - 1)) + ((f & (p.edge - 1)) >> 1)
    sel = one_hot(coarse == c)
    sel = jnp.concatenate([sel, sel], axis=0)
    w_ref[...] = sel


def finish_kernel(p, r_ref, g_ref, w_ref, v_ref, n_ref, lo_ref, hi_ref, vel_hbm, mag_hbm, vel, mag, sems):
    zc = p.zc
    copies = []
    for z in range(zc):
        dz = [jnp.zeros((p.ny, p.nx), F32)] * 2
        outer = dz[0]
        if z == zc - 1:
            dz = [dz[c] + hi_ref[c] for c in range(2)]
            outer = outer + hi_ref[2]
        if z == 0:
            dz = [dz[c] - lo_ref[c] for c in range(2)]
            outer = outer + lo_ref[2]
        mag[0, z] = n_ref[0, z] + 0.05 * -dz[1]
        mag[1, z] = n_ref[1, z] + 0.05 * dz[0]
        mag[2, z] = n_ref[2, z] + 0.05 * outer
    copies.append(pltpu.make_async_copy(mag, mag_hbm, sems.at[0]))
    copies[-1].start()
    half_fine = p.edge * p.edge // 2
    half_area = p.area // 2
    sel = w_ref[...]
    g = g_ref[...]
    ws = [slice(h * half_area, (h + 1) * half_area) for h in range(2)]
    s = p.slots
    m = zc * s
    for c in range(3):
        hi, lo = split(r_ref[:, c * p.rc : (c + 1) * p.rc, :].reshape(p.rows, p.area) * 0.1)
        parts = dot(g, jnp.concatenate([hi, lo], axis=1)).astype(BF16)
        hi, lo = parts[:, : p.area], parts[:, p.area :]
        pairs = [jnp.concatenate([hi[:, w], lo[:, w]], axis=1) for w in ws]
        add = dot(jnp.concatenate(pairs, axis=0), sel)
        for z in range(zc):
            for h in range(2):
                fw = slice(h * half_fine, (h + 1) * half_fine)
                part = add[h * m + z * s : h * m + (z + 1) * s]
                for d in range(2):
                    vel[c, 2 * z + d, :, fw] = v_ref[c, 2 * z + d, :, fw] + part
            fine = pl.ds(2 * z, 2)
            copies.append(pltpu.make_async_copy(vel.at[c, fine], vel_hbm.at[c, fine], sems.at[1 + c * zc + z]))
            copies[-1].start()
    for copy in copies:
        copy.wait()


def struct(*shape, dtype=F32):
    return jax.ShapeDtypeStruct(shape, dtype)


def call(kernel, ins, outs, scratch=(), grant=20 << 20):
    return pl.pallas_call(
        kernel,
        out_shape=[o for o, _ in outs],
        in_specs=ins,
        out_specs=[spec for _, spec in outs],
        scratch_shapes=list(scratch),
        cost_estimate=pl.CostEstimate(flops=1 << 24, bytes_accessed=1 << 20, transcendentals=0),
        compiler_params=pltpu.CompilerParams(vmem_limit_bytes=grant),
    )


def ring(axis, step):
    n = lax.axis_size(axis)
    return [(i, (i + step) % n) for i in range(n)]


def planes(up, down):
    below = lax.ppermute(up, "gz", ring("gz", 1))
    above = lax.ppermute(down, "gz", ring("gz", -1))
    return below, above


def body(velocity, magnetic, slot_block_table):
    p = Plan(velocity.shape, magnetic.shape, lax.axis_size("xy"))
    plane = (p.ny, p.nx)
    dma = pltpu.SemaphoreType.DMA
    table = slot_block_table.reshape(1, p.slots)
    sent, up, down = call(
        functools.partial(restrict_kernel, p),
        [HBM] * 3,
        [(struct(p.n, p.r1, p.area), HBM), (struct(2, *plane), HBM), (struct(2, *plane), HBM)],
        [
            pltpu.VMEM(velocity.shape, F32),
            pltpu.VMEM((1, p.slots), jnp.int32),
            pltpu.VMEM(magnetic.shape, F32),
            pltpu.VMEM((p.n, p.r1, p.area), F32),
            pltpu.VMEM((-(-p.rb // 8) * 8, p.area), F32),
            pltpu.VMEM((-(-p.rb // 8) * 8, p.area), F32),
            dma((12,)),
        ],
        ALL_VMEM,
    )(velocity, table, magnetic)
    got = lax.all_to_all(sent, "xy", 0, 0, tiled=True)
    below, above = planes(up, down)
    held, held_table, _ = lax.optimization_barrier((magnetic, table, up))
    field, current, diffused, g3 = call(
        functools.partial(interior_kernel, p),
        [VMEM] * 2,
        [(struct(*magnetic.shape), VMEM)] * 3 + [(struct(p.zc * p.slots, p.rows, dtype=BF16), VMEM)],
    )(held, held_table)
    sent, emf, up, down = call(
        functools.partial(field_kernel, p),
        [VMEM] * 5,
        [
            (struct(p.n, p.ru, p.area), VMEM),
            (struct(*magnetic.shape), VMEM),
            (struct(3, *plane), VMEM),
            (struct(3, *plane), VMEM),
        ],
    )(got, field, current, below, above)
    got_force = lax.all_to_all(sent, "xy", 0, 0, tiled=True)
    emf_below, emf_above = planes(up, down)
    partial, widen = call(
        functools.partial(local_kernel, p), [VMEM] * 5, [(struct(*magnetic.shape), VMEM), (struct(p.area, p.edge * p.edge // 2, dtype=BF16), VMEM)]
    )(got, diffused, below, above, emf)
    return tuple(
        call(
            functools.partial(finish_kernel, p),
            [VMEM] * 7,
            [(struct(*velocity.shape), HBM), (struct(*magnetic.shape), HBM)],
            [pltpu.VMEM(velocity.shape, F32), pltpu.VMEM(magnetic.shape, F32), dma((1 + 3 * p.zc,))],
        )(got_force, g3, widen, velocity, partial, emf_below, emf_above)
    )


def solution(mesh):
    return jax.shard_map(
        body,
        mesh=mesh,
        in_specs=(P(None, "gz", "xy", None), P(None, "gz", "xy", None), P("xy")),
        out_specs=(P(None, "gz", "xy", None), P(None, "gz", "xy", None)),
        check_vma=False,
    )
```
